32 devices in a mesh: level: 2 (over core), dom: 8 (over z, x), samp: 2 (over y).
Axes of the slice: x: 2, y: 2, z: 4, core: 2. Of those that a mesh axis runs over, the one named last changes fastest.
Arguments:
- panels: float32 [2, 4096, 16, 256], P('level', 'dom', None, 'samp'), may hold values from 0 to 2
- courant: float32 [4096, 4, 256], P('dom', None, 'samp'), may hold values from 0.3 to 0.95
- direction: int32 [4096, 4, 2], P('dom', None, 'samp'), may hold values 0 or 1
- decay: float32 [4096], P('dom'), may hold values from 0.02 to 0.8
- booster: float32 [4096], P('dom'), may hold values from 0 to 1
- feeder: int32 [4096, 2], P('dom'), may hold values from 0 to 767, as said below
- face_index: int32 [1024], P('dom'), may hold values from 0 to 511
Outputs:
- advanced: float32 [2, 4096, 16, 256], P('level', 'dom', None, 'samp')
- level_gap: float32 [4096, 4, 256], P('dom', 'level', 'samp')
The draws below stay inside these ranges and needn't reach their ends.
Inputs may be any that keep to these rules, and one draw needn't show every extreme that they name: `feeder`: entries below 512 name the partition's own pipes, the next 128 name the face pipes of the partition before it, the last 128 those of the partition after it. Most entries are below 512. `face_index`: local pipe numbers within the partition; repeats may occur.
All inputs are finite; a program needn't handle non-finite values. No bound on the sum of `direction` on one device may be relied on, other than what follows from the above.
Results may differ from the reference program's by a relative error of at most 0.00016.
Values sent between devices are 32-bit elements; how exact they have to be, the bound alone decides.
No kernel may reach another device: no remote copies, remote signals or barrier semaphores. Data moves between devices by JAX's collectives and lax.ppermute only.
A program may use at most 128 MiB of HBM per device.

```python
import math
import jax
import jax.numpy as jnp

P_DEV = 512
FACES = 128
BLOCK = 128
SEGF = 16
SEGC = 4
GROUPS = 4
PIPES = 4096
SAMPLES = 256
N_DOM = 8


def draw_feeder(key, part):
    key_sel = jax.random.fold_in(key, 11)
    key_local = jax.random.fold_in(key, 12)
    key_left = jax.random.fold_in(key, 13)
    key_right = jax.random.fold_in(key, 14)
    selector = jax.random.randint(key_sel, (PIPES, 2), 0, 20)
    local_pick = jax.random.randint(key_local, (PIPES, 2), 0, P_DEV)
    left_pick = jax.random.randint(key_left, (PIPES, 2), P_DEV, P_DEV + FACES)
    right_pick = jax.random.randint(key_right, (PIPES, 2), P_DEV + FACES, P_DEV + 2 * FACES)
    chosen = jnp.where(selector == 0, left_pick, jnp.where(selector == 1, right_pick, local_pick))
    local_number = (jnp.arange(PIPES, dtype=jnp.int32) % P_DEV)[:, None]
    chosen = jnp.where(local_number == 0, left_pick, chosen)
    chosen = jnp.where(local_number == 1, right_pick, chosen)
    chosen = chosen.at[2 % PIPES, 0].set(0)
    chosen = chosen.at[1, 1].set(P_DEV + 2 * FACES - 1)
    return chosen.astype(jnp.int32)


def touch_ends(values, own_key, smallest, high):
    index_at = [jax.random.randint(jax.random.fold_in(own_key, axis), (), 0, length) for axis, length in enumerate(values.shape)]
    longest = values.shape.index(max(values.shape))
    next_to = index_at[:longest] + [(index_at[longest] + 1) % values.shape[longest]] + index_at[longest + 1:]
    return values.at[tuple(index_at)].set(smallest).at[tuple(next_to)].set(high)


def block_scale(stream_key, shape, pieces, smallest, high):
    gain, own = 1.0, jax.random.fold_in(stream_key, 6)
    for position, blocks in pieces:
        draws = jnp.exp(jax.random.uniform(jax.random.fold_in(own, position), (blocks,), jnp.float32, smallest / len(pieces), high / len(pieces)))
        gain = gain * jnp.repeat(draws, shape[position] // blocks).reshape([-1 if axis == position else 1 for axis in range(len(shape))])
    return gain


def setup_inputs(seed: int = 0) -> dict:
    key_list = jax.random.split(jax.random.key(seed), 8)
    panels = jnp.clip(2.0 * jax.random.uniform(key_list[0], (2, PIPES, SEGF, SAMPLES), jnp.float32) ** block_scale(key_list[0], (2, PIPES, SEGF, SAMPLES), ((0, 2), (1, 8), (3, 2)), -0.2, 0.2), 0.0, 2.0)
    courant = jnp.clip(0.3 + 0.65 * jax.random.uniform(key_list[1], (PIPES, GROUPS, SAMPLES), jnp.float32) ** block_scale(key_list[1], (PIPES, GROUPS, SAMPLES), ((0, 8), (2, 2)), -0.2, 0.2), 0.3, 0.95)
    direction = touch_ends((jax.random.randint(key_list[2], (PIPES, GROUPS, SAMPLES // BLOCK), 0, 4) < 1).astype(jnp.int32), jax.random.fold_in(key_list[2], 1), 0, 1)
    decay = jnp.clip(jnp.exp(math.log(0.8) - 3.6888795 * jax.random.uniform(key_list[3], (PIPES,), jnp.float32) ** block_scale(key_list[3], (PIPES,), ((0, 8),), -0.2, 0.2)), 0.02, 0.8)
    booster = jnp.clip(1.0 * jax.random.uniform(key_list[4], (PIPES,), jnp.float32) ** block_scale(key_list[4], (PIPES,), ((0, 8),), -0.2, 0.2), 0.0, 1.0)
    feeder = draw_feeder(jax.random.fold_in(key_list[7], 71), 0)
    face_index = touch_ends(jax.random.randint(key_list[6], (N_DOM * FACES,), 0, P_DEV), jax.random.fold_in(key_list[6], 1), 0, P_DEV - 1).astype(jnp.int32)
    return {"panels": panels, "courant": courant, "direction": direction, "decay": decay, "booster": booster, "feeder": feeder, "face_index": face_index}


def advance_all(panel, courant_now, reverse, decay_factor, source_ids, present, booster, steps):
    segments = panel.shape[2]
    flipped = reverse[:, :, None, :]
    oriented = jnp.where(flipped, panel[:, :, ::-1, :], panel)
    chosen = jnp.where(reverse, source_ids[:, 1][:, None, None], source_ids[:, 0][:, None, None])
    usable = jnp.where(reverse, present[:, 1][:, None, None], present[:, 0][:, None, None])
    for substep in range(steps):
        outflow = oriented[:, :, segments - 1, :]
        taken = jnp.take_along_axis(outflow, chosen, axis=0)
        inflow = jnp.where(usable, taken, jnp.float32(0.0)) + booster[:, None, None]
        upstream = jnp.concatenate([inflow[:, :, None, :], oriented[:, :, :-1, :]], axis=2)
        oriented = decay_factor[:, None, None, None] * (oriented - courant_now[:, :, None, :] * (oriented - upstream))
    return jnp.where(flipped, oriented[:, :, ::-1, :], oriented)


def reference(panels, courant, direction, decay, booster, feeder, face_index):
    partition = (jnp.arange(PIPES, dtype=jnp.int32) // P_DEV)[:, None]
    column = feeder
    local_id = partition * P_DEV + jnp.clip(column, 0, P_DEV - 1)
    left_part = partition - 1
    right_part = partition + 1
    left_safe = jnp.clip(left_part, 0, N_DOM - 1)
    right_safe = jnp.clip(right_part, 0, N_DOM - 1)
    left_entry = jnp.clip(column - P_DEV, 0, FACES - 1)
    right_entry = jnp.clip(column - P_DEV - FACES, 0, FACES - 1)
    left_id = left_safe * P_DEV + face_index[left_safe * FACES + left_entry]
    right_id = right_safe * P_DEV + face_index[right_safe * FACES + right_entry]
    is_local = column < P_DEV
    is_left = (column >= P_DEV) & (column < P_DEV + FACES)
    source_ids = jnp.where(is_local, local_id, jnp.where(is_left, left_id, right_id)).astype(jnp.int32)
    present = is_local | (is_left & (left_part >= 0)) | ((~is_local) & (~is_left) & (right_part < N_DOM))
    reverse = jnp.repeat(direction, BLOCK, axis=2) == 1
    fine_new = advance_all(panels[0][:, None], courant[:, 0:1], reverse[:, 0:1], jnp.exp(-decay * 0.25),
                           source_ids, present, booster, SEGF // SEGC)[:, 0]
    coarse_state = panels[1].reshape(PIPES, SEGF // SEGC, SEGC, SAMPLES)
    coarse_new = advance_all(coarse_state, courant, reverse, jnp.exp(-decay),
                             source_ids, present, booster, 1).reshape(PIPES, SEGF, SAMPLES)
    restricted = jnp.sum(fine_new.reshape(PIPES, SEGC, SEGF // SEGC, SAMPLES), axis=2) * 0.25
    level_gap = restricted - coarse_new[:, 0:SEGC, :]
    return jnp.stack([fine_new, coarse_new]), level_gap
```

```python
import jax
import jax.numpy as jnp
from jax import lax
from jax.experimental import pallas as pl
from jax.experimental.pallas import tpu as pltpu
from jax.sharding import PartitionSpec as P

SEGF = 16
SEGC = 4
GROUPS = SEGF // SEGC
LANES = 128
CHUNKS = 8

HBM = pl.BlockSpec(memory_space=pltpu.HBM)
VMEM = pl.BlockSpec(memory_space=pltpu.VMEM)
SMEM = pl.BlockSpec(memory_space=pltpu.SMEM)


def params():
    return pltpu.CompilerParams(vmem_limit_bytes=8 << 20)


def cost(nbytes):
    return pl.CostEstimate(flops=0, bytes_accessed=nbytes, transcendentals=0)


def pinned(space, *arrays):
    return [pltpu.with_memory_space_constraint(x, space) for x in arrays]


def down_rows(row):
    return jnp.broadcast_to(row, (LANES, LANES)).T


def spread(ref, row):
    return ref[pl.ds(row, 8, stride=0), :]


def load_kernel(
    panel, rate, dirs, feed, decay, boost, faces,
    cells, rates, outflow, factor, boosts, table, face_rows,
    flow_back, dir_v, feed_v, decay_v, boost_v, face_s, panel_sem, rate_sem, small_sem,
):
    rows = panel.shape[0] // CHUNKS
    blocks = decay.shape[0]
    pipes = blocks * LANES
    level = lax.axis_index("level")

    def chunk(n):
        part = pl.ds(pl.multiple_of(n * rows, rows), rows)
        return pltpu.make_async_copy(panel.at[part], cells.at[part], panel_sem.at[n])

    small = [
        pltpu.make_async_copy(src, dst, small_sem.at[n])
        for n, (src, dst) in enumerate(
            ((dirs, dir_v), (decay, decay_v), (feed, feed_v), (boost, boost_v), (faces, face_s))
        )
    ]
    rate_copy = pltpu.make_async_copy(rate, rates, rate_sem)
    for copy in small:
        copy.start()
    rate_copy.start()
    for n in range(CHUNKS):
        chunk(n).start()
    for copy in small:
        copy.wait()

    scale = jnp.where(level == 0, jnp.float32(-0.25), jnp.float32(-1.0))
    fac = jnp.exp(decay_v[...] * scale)
    for b in range(blocks):
        own = slice(b * LANES, (b + 1) * LANES)
        factor[own, :] = down_rows(fac[b : b + 1])
        boosts[own, :] = down_rows(boost_v[b : b + 1])
    outflow[GROUPS * pipes :, :] = jnp.zeros_like(outflow[GROUPS * pipes :, :])
    back = (dir_v[...] == 1).astype(jnp.int32)
    for b in range(blocks):
        ahead = feed_v[2 * b : 2 * b + 1, :]
        behind = feed_v[2 * b + 1 : 2 * b + 2, :]
        revs, ghost = [], []
        for g in range(GROUPS):
            at = g * blocks + b
            rev = back[at : at + 1, :]
            src = jnp.where(rev == 1, behind, ahead)
            table[at : at + 1, :] = src * GROUPS + g
            revs.append(rev)
            ghost.append((src >= pipes).astype(jnp.int32))
        for t in range(2):
            at = (GROUPS + t) * blocks + b
            table[at : at + 1, :] = 8 * (revs[2 * t] + 2 * revs[2 * t + 1])
        at = (GROUPS + 2) * blocks + b
        every = jnp.maximum(jnp.maximum(ghost[0], ghost[1]), jnp.maximum(ghost[2], ghost[3]))
        table[at : at + 1, :] = jnp.where(level == 0, ghost[0], every)

    backf = back.astype(jnp.float32)

    def back_rows(g):
        for b in range(blocks):
            at = g * blocks + b
            flow_back[at * LANES : (at + 1) * LANES, :] = down_rows(backf[at : at + 1])

    back_rows(0)

    @pl.when(level == 1)
    def _():
        for g in range(1, GROUPS):
            back_rows(g)

    rate_copy.wait()
    per_chunk = pipes // 8 // CHUNKS

    @pl.when(level == 0)
    def _():
        @pl.loop(0, CHUNKS)
        def _(n):
            chunk(n).wait()
            for i in range(per_chunk):
                q = n * per_chunk + i
                base = pl.multiple_of(q * 128, 128)
                own = pl.ds(pl.multiple_of(q * 8, 8), 8)
                rev = flow_back[own, :] != 0.0
                b = factor[own, :] * rates[pl.ds(pl.multiple_of(q * 32, 32), 8, stride=4), :]
                a = factor[own, :] - b
                y = [
                    jnp.where(
                        rev,
                        cells[pl.ds(base + j, 8, stride=16), :],
                        cells[pl.ds(base + 15 - j, 8, stride=16), :],
                    )
                    for j in range(GROUPS)
                ]
                for s in range(GROUPS):
                    outflow[pl.ds(pl.multiple_of(q * 32, 32) + s, 8, stride=4), :] = y[0]
                    y = [a * y[j] + b * y[j + 1] for j in range(len(y) - 1)]

    @pl.when(level == 1)
    def _():
        @pl.loop(0, CHUNKS)
        def _(n):
            chunk(n).wait()
            for i in range(per_chunk):
                q = n * per_chunk + i
                base = pl.multiple_of(q * 128, 128)
                for g in range(GROUPS):
                    rev = flow_back[pl.ds(pl.multiple_of(g * pipes + q * 8, 8), 8), :] != 0.0
                    outflow[pl.ds(pl.multiple_of(q * 32, 32) + g, 8, stride=4), :] = jnp.where(
                        rev,
                        cells[pl.ds(base + 4 * g, 8, stride=16), :],
                        cells[pl.ds(base + 4 * g + 3, 8, stride=16), :],
                    )

    @pl.loop(0, faces.shape[0] // 8)
    def _(m):
        for u in range(8):
            pipe = face_s[m * 8 + u]
            face_rows[pl.ds(pl.multiple_of(m * 32, 32) + 4 * u, 4), :] = outflow[
                pl.ds(pl.multiple_of(pipe * 4, 4), 4), :
            ]


def fine_pipe(p, rev, src, cells, rates, outflow, factor, boosts, new):
    near = pl.ds(pl.multiple_of(p * 16 + 8 * rev, 8), 8)
    far = pl.ds(pl.multiple_of(p * 16 + 8 - 8 * rev, 8), 8)
    f = spread(factor, p)
    b = f * spread(rates, p * 4)
    a = f - b
    bo = spread(boosts, p)
    y0, y1 = cells[near, :], cells[far, :]
    shift = 1 + 6 * rev
    edge = lax.broadcasted_iota(jnp.int32, (8, LANES), 0) == 7 * rev
    for s in range(GROUPS):
        inflow = spread(outflow, src + s) + bo
        q0 = pltpu.roll(y0, shift, 0)
        q1 = pltpu.roll(y1, shift, 0)
        y1 = a * y1 + b * jnp.where(edge, q0, q1)
        y0 = a * y0 + b * jnp.where(edge, inflow, q0)
    new[near, :] = y0
    new[far, :] = y1


def coarse_pipe(p, srcs, codes, masks, cells, rates, outflow, factor, boosts, new):
    low = lax.broadcasted_iota(jnp.int32, (8, LANES), 0) < 4
    f = spread(factor, p)
    bo = spread(boosts, p)
    for t in range(2):
        own = pl.ds(pl.multiple_of(p * 16 + 8 * t, 8), 8)
        x = cells[own, :]
        r = jnp.where(low, spread(rates, p * 4 + 2 * t), spread(rates, p * 4 + 2 * t + 1))
        inflow = jnp.where(low, spread(outflow, srcs[2 * t]), spread(outflow, srcs[2 * t + 1])) + bo
        code = pl.multiple_of(codes[t], 8)
        turned = masks[pl.ds(code, 8), :] != 0.0
        edge = masks[pl.ds(32 + code, 8), :] != 0.0
        up = jnp.where(edge, inflow, jnp.where(turned, pltpu.roll(x, 7, 0), pltpu.roll(x, 1, 0)))
        b = f * r
        new[own, :] = (f - b) * x + b * up


def fill_masks(masks):
    row = lax.broadcasted_iota(jnp.int32, (8, LANES), 0)
    for code in range(4):
        rev = jnp.where(row < 4, code & 1, code >> 1)
        masks[8 * code : 8 * code + 8, :] = rev.astype(jnp.float32)
        edge = (row & 3) == 3 * rev
        masks[32 + 8 * code : 40 + 8 * code, :] = edge.astype(jnp.float32)


def one_pipe(fine, p, b, j, table, dirs, masks, *state):
    blocks = dirs.shape[0] // GROUPS
    if fine:
        fine_pipe(p, dirs[b, j], table[b, j], *state)
    else:
        srcs = [table[g * blocks + b, j] for g in range(GROUPS)]
        codes = [table[(GROUPS + t) * blocks + b, j] for t in range(2)]
        coarse_pipe(p, srcs, codes, masks, *state)


def step_kernel(
    table, dirs, cells, rates, outflow, factor, boosts,
    new, out, keep, send, ghosts,
    masks, sems,
):
    blocks = dirs.shape[0] // GROUPS
    level = lax.axis_index("level")
    fill_masks(masks)

    def written(b):
        part = pl.ds(pl.multiple_of(b * 16 * LANES, 128), 16 * LANES)
        return pltpu.make_async_copy(new.at[part], out.at[part], sems.at[b])

    def run(fine):
        def block(b, count):
            def some(m, count):
                for u in range(8):
                    j = m * 8 + u
                    p = b * LANES + j
                    one_pipe(
                        fine, p, b, j, table, dirs, masks,
                        cells, rates, outflow, factor, boosts, new,
                    )
                    ghosts[count] = p
                    count = count + table[(GROUPS + 2) * blocks + b, j]
                return count

            count = lax.fori_loop(0, LANES // 8, some, count)
            written(b).start()

            @pl.loop(0, LANES // 8)
            def _(m):
                q = b * (LANES // 8) + m
                base = pl.multiple_of(q * 128, 128)
                for k in range(SEGC):
                    if fine:
                        part = [new[pl.ds(base + 4 * k + i, 8, stride=16), :] for i in range(4)]
                        share = ((part[0] + part[1]) + (part[2] + part[3])) * 0.25
                    else:
                        share = new[pl.ds(base + k, 8, stride=16), :]
                    dest = keep if (k < 2) == fine else send
                    dest[pl.ds(pl.multiple_of(q * 16, 16) + k % 2, 8, stride=2), :] = share

            return count

        count = lax.fori_loop(0, blocks, block, jnp.int32(0))
        last = ghosts[jnp.maximum(count - 1, 0)]
        for u in range(8):
            ghosts[count + u] = last
        ghosts[blocks * LANES + 8] = count

    @pl.when(level == 0)
    def _():
        run(True)

    @pl.when(level == 1)
    def _():
        run(False)

    for b in range(blocks):
        written(b).wait()


def arrive_kernel(first, rows, near, arrived, outflow_in, outflow):
    odd = lax.axis_index("dom") % 2
    half = arrived.shape[0]
    slot = 1 - odd if near else odd
    start = pl.multiple_of(first + slot * half, 8)
    outflow[pl.ds(start, half), :] = arrived[...]


def fix_kernel(
    first, table, dirs, ghosts, arrived, cells, rates, factor, boosts,
    outflow_in, new_in, keep_in, send_in,
    outflow, new, keep, send,
    masks,
):
    blocks = dirs.shape[0] // GROUPS
    level = lax.axis_index("level")
    arrive_kernel(first, 0, False, arrived, outflow_in, outflow)
    fill_masks(masks)
    count = ghosts[blocks * LANES + 8]

    def run(fine):
        @pl.loop(0, (count + 3) // 4)
        def _(m):
            pipes = [ghosts[m * 4 + u] for u in range(4)]
            for p in pipes:
                one_pipe(
                    fine, p, p // LANES, p % LANES, table, dirs, masks,
                    cells, rates, outflow, factor, boosts, new,
                )
            for p in pipes:
                if fine:
                    part = [new[pl.ds(p * 16 + i, 4, stride=4), :] for i in range(4)]
                    share = ((part[0] + part[1]) + (part[2] + part[3])) * 0.25
                else:
                    share = new[pl.ds(pl.multiple_of(p * 16, 16), 4), :]
                own = pl.ds(p * 2, 2)
                keep[own, :] = share[0:2] if fine else share[2:4]
                send[own, :] = share[2:4] if fine else share[0:2]

    @pl.when(level == 0)
    def _():
        run(True)

    @pl.when(level == 1)
    def _():
        run(False)


def gap_kernel(keep, partner, gap):
    sign = jnp.where(lax.axis_index("level") == 0, jnp.float32(1.0), jnp.float32(-1.0))
    gap[...] = (keep[...] - partner[...]) * sign


def write_kernel(ghosts, new, out_in, out, sems):
    pipes = new.shape[0] // SEGF
    count = ghosts[pipes + 8]

    def moved(i):
        part = pl.ds(pl.multiple_of(ghosts[i] * 16, 16), 16)
        return pltpu.make_async_copy(new.at[part], out.at[part], sems.at[i])

    @pl.loop(0, count)
    def _(i):
        moved(i).start()

    @pl.loop(0, count)
    def _(i):
        moved(i).wait()


def per_device(panels, courant, direction, decay, booster, feeder, face_index):
    pipes = panels.shape[1]
    columns = panels.shape[3]
    faces = face_index.shape[0]
    blocks = pipes // LANES
    domains = lax.axis_size("dom")
    f32, i32 = jnp.float32, jnp.int32
    cells_in = panels.reshape(pipes * SEGF, columns)
    rates_in = courant.reshape(pipes * GROUPS, columns)
    dirs = direction.transpose(1, 2, 0).reshape(GROUPS * blocks, LANES)
    feed = feeder.reshape(blocks, LANES, 2).transpose(0, 2, 1).reshape(2 * blocks, LANES)
    ghost_rows = GROUPS * (pipes + 2 * faces)

    cells, rates, outflow, factor, boosts, table, face_rows = pl.pallas_call(
        load_kernel,
        name="load_step",
        in_specs=[HBM] * 7,
        out_specs=[VMEM] * 7,
        out_shape=[
            pltpu.VMEM((pipes * SEGF, columns), f32),
            pltpu.VMEM((pipes * GROUPS, columns), f32),
            pltpu.VMEM((ghost_rows, columns), f32),
            pltpu.VMEM((pipes, columns), f32),
            pltpu.VMEM((pipes, columns), f32),
            jax.ShapeDtypeStruct(((GROUPS + 4) * blocks, LANES), i32),
            pltpu.VMEM((faces * GROUPS, columns), f32),
        ],
        scratch_shapes=[
            pltpu.VMEM((GROUPS * pipes, columns), f32),
            pltpu.VMEM(dirs.shape, i32),
            pltpu.VMEM(feed.shape, i32),
            pltpu.VMEM((blocks, LANES), f32),
            pltpu.VMEM((blocks, LANES), f32),
            pltpu.SMEM((faces,), i32),
            pltpu.SemaphoreType.DMA((CHUNKS,)),
            pltpu.SemaphoreType.DMA(()),
            pltpu.SemaphoreType.DMA((5,)),
        ],
        compiler_params=params(),
        cost_estimate=cost(5 << 20),
    )(
        *pinned(
            pltpu.HBM, cells_in, rates_in, dirs, feed,
            decay.reshape(blocks, LANES), booster.reshape(blocks, LANES), face_index,
        )
    )

    near_pairs = [(i, i ^ 1) for i in range(domains) if i ^ 1 < domains]
    far_pairs = [(i, i + 1) for i in range(1, domains - 1, 2)]
    far_pairs = far_pairs + [(j, i) for i, j in far_pairs]
    near_rows = lax.ppermute(face_rows, "dom", near_pairs)
    far_rows = lax.ppermute(face_rows, "dom", far_pairs)

    new, out, keep, send, ghosts = pl.pallas_call(
        step_kernel,
        name="advance_step",
        in_specs=[SMEM] * 2 + [VMEM] * 5,
        out_specs=[VMEM, HBM, VMEM, VMEM, SMEM],
        out_shape=[
            pltpu.VMEM((pipes * SEGF, columns), f32),
            jax.ShapeDtypeStruct((pipes * SEGF, columns), f32),
            pltpu.VMEM((pipes * 2, columns), f32),
            pltpu.VMEM((pipes * 2, columns), f32),
            jax.ShapeDtypeStruct((pipes + 16,), i32),
        ],
        scratch_shapes=[pltpu.VMEM((64, columns), f32), pltpu.SemaphoreType.DMA((blocks,))],
        compiler_params=params(),
        cost_estimate=cost(20 << 20),
    )(table, dirs, cells, rates, outflow, factor, boosts)

    first = GROUPS * pipes
    outflow = pl.pallas_call(
        lambda *refs: arrive_kernel(first, 0, True, *refs),
        name="near_arrive",
        in_specs=[VMEM] * 2,
        out_specs=VMEM,
        out_shape=pltpu.VMEM((ghost_rows, columns), f32),
        input_output_aliases={1: 0},
        compiler_params=params(),
        cost_estimate=cost(1 << 19),
    )(near_rows, outflow)

    outflow, new, keep, send = pl.pallas_call(
        lambda *refs: fix_kernel(first, *refs),
        name="ghost_fix",
        in_specs=[SMEM] * 3 + [VMEM] * 9,
        out_specs=[VMEM] * 4,
        out_shape=[
            pltpu.VMEM((ghost_rows, columns), f32),
            pltpu.VMEM((pipes * SEGF, columns), f32),
            pltpu.VMEM((pipes * 2, columns), f32),
            pltpu.VMEM((pipes * 2, columns), f32),
        ],
        scratch_shapes=[pltpu.VMEM((64, columns), f32)],
        input_output_aliases={8: 0, 9: 1, 10: 2, 11: 3},
        compiler_params=params(),
        cost_estimate=cost(3 << 20),
    )(table, dirs, ghosts, far_rows, cells, rates, factor, boosts, outflow, new, keep, send)

    partner = lax.ppermute(send, "level", [(0, 1), (1, 0)])

    out = pl.pallas_call(
        write_kernel,
        name="ghost_write",
        in_specs=[SMEM, VMEM, HBM],
        out_specs=HBM,
        out_shape=jax.ShapeDtypeStruct((pipes * SEGF, columns), f32),
        scratch_shapes=[pltpu.SemaphoreType.DMA((pipes,))],
        input_output_aliases={2: 0},
        compiler_params=params(),
        cost_estimate=cost(4 << 20),
    )(ghosts, new, *pinned(pltpu.HBM, out))

    gap = pl.pallas_call(
        gap_kernel,
        name="level_gap",
        in_specs=[VMEM] * 2,
        out_specs=VMEM,
        out_shape=jax.ShapeDtypeStruct((pipes * 2, columns), f32),
        compiler_params=params(),
        cost_estimate=cost(1 << 20),
    )(keep, partner)
    return (out.reshape(1, pipes, SEGF, columns), gap.reshape(pipes, 2, columns))


def solution(mesh):
    in_specs = (
        P("level", "dom", None, "samp"),
        P("dom", None, "samp"),
        P("dom", None, "samp"),
        P("dom"),
        P("dom"),
        P("dom", None),
        P("dom"),
    )
    out_specs = (P("level", "dom", None, "samp"), P("dom", "level", "samp"))
    return jax.shard_map(
        per_device, mesh=mesh, in_specs=in_specs, out_specs=out_specs, check_vma=False
    )
```

```python
import jax
import jax.numpy as jnp
from jax import lax
from jax.experimental import pallas as pl
from jax.experimental.pallas import tpu as pltpu
from jax.sharding import PartitionSpec as P

SEGF = 16
SEGC = 4
GROUPS = SEGF // SEGC
LANES = 128
CHUNKS = 8

HBM = pl.BlockSpec(memory_space=pltpu.HBM)
VMEM = pl.BlockSpec(memory_space=pltpu.VMEM)
SMEM = pl.BlockSpec(memory_space=pltpu.SMEM)


def params():
    return pltpu.CompilerParams(vmem_limit_bytes=8 << 20)


def cost(nbytes):
    return pl.CostEstimate(flops=0, bytes_accessed=nbytes, transcendentals=0)


def pinned(space, *arrays):
    return [pltpu.with_memory_space_constraint(x, space) for x in arrays]


def down_rows(row):
    return jnp.broadcast_to(row, (LANES, LANES)).T


def spread(ref, row):
    return ref[pl.ds(row, 8, stride=0), :]


def load_kernel(
    panel, rate, dirs, feed, decay, boost, faces,
    cells, rates, outflow, factor, boosts, table, face_rows,
    flow_back, dir_v, feed_v, decay_v, boost_v, face_s, panel_sem, rate_sem, small_sem,
):
    rows = panel.shape[0] // CHUNKS
    blocks = decay.shape[0]
    pipes = blocks * LANES
    level = lax.axis_index("level")

    def chunk(n):
        part = pl.ds(pl.multiple_of(n * rows, rows), rows)
        return pltpu.make_async_copy(panel.at[part], cells.at[part], panel_sem.at[n])

    small = [
        pltpu.make_async_copy(src, dst, small_sem.at[n])
        for n, (src, dst) in enumerate(
            ((dirs, dir_v), (decay, decay_v), (feed, feed_v), (boost, boost_v), (faces, face_s))
        )
    ]
    rate_copy = pltpu.make_async_copy(rate, rates, rate_sem)
    for copy in small:
        copy.start()
    rate_copy.start()
    for n in range(CHUNKS):
        chunk(n).start()
    for copy in small:
        copy.wait()

    scale = jnp.where(level == 0, jnp.float32(-0.25), jnp.float32(-1.0))
    fac = jnp.exp(decay_v[...] * scale)
    for b in range(blocks):
        own = slice(b * LANES, (b + 1) * LANES)
        factor[own, :] = down_rows(fac[b : b + 1])
        boosts[own, :] = down_rows(boost_v[b : b + 1])
    outflow[GROUPS * pipes :, :] = jnp.zeros_like(outflow[GROUPS * pipes :, :])
    back = (dir_v[...] == 1).astype(jnp.int32)
    for b in range(blocks):
        ahead = feed_v[2 * b : 2 * b + 1, :]
        behind = feed_v[2 * b + 1 : 2 * b + 2, :]
        revs, ghost = [], []
        for g in range(GROUPS):
            at = g * blocks + b
            rev = back[at : at + 1, :]
            src = jnp.where(rev == 1, behind, ahead)
            table[at : at + 1, :] = src * GROUPS + g
            revs.append(rev)
            ghost.append((src >= pipes).astype(jnp.int32))
        for t in range(2):
            at = (GROUPS + t) * blocks + b
            table[at : at + 1, :] = 8 * (revs[2 * t] + 2 * revs[2 * t + 1])
        at = (GROUPS + 2) * blocks + b
        every = jnp.maximum(jnp.maximum(ghost[0], ghost[1]), jnp.maximum(ghost[2], ghost[3]))
        table[at : at + 1, :] = jnp.where(level == 0, ghost[0], every)

    backf = back.astype(jnp.float32)

    def back_rows(g):
        for b in range(blocks):
            at = g * blocks + b
            flow_back[at * LANES : (at + 1) * LANES, :] = down_rows(backf[at : at + 1])

    back_rows(0)

    @pl.when(level == 1)
    def _():
        for g in range(1, GROUPS):
            back_rows(g)

    rate_copy.wait()
    per_chunk = pipes // 8 // CHUNKS

    @pl.when(level == 0)
    def _():
        @pl.loop(0, CHUNKS)
        def _(n):
            chunk(n).wait()
            for i in range(per_chunk):
                q = n * per_chunk + i
                base = pl.multiple_of(q * 128, 128)
                own = pl.ds(pl.multiple_of(q * 8, 8), 8)
                rev = flow_back[own, :] != 0.0
                b = factor[own, :] * rates[pl.ds(pl.multiple_of(q * 32, 32), 8, stride=4), :]
                a = factor[own, :] - b
                y = [
                    jnp.where(
                        rev,
                        cells[pl.ds(base + j, 8, stride=16), :],
                        cells[pl.ds(base + 15 - j, 8, stride=16), :],
                    )
                    for j in range(GROUPS)
                ]
                for s in range(GROUPS):
                    outflow[pl.ds(pl.multiple_of(q * 32, 32) + s, 8, stride=4), :] = y[0]
                    y = [a * y[j] + b * y[j + 1] for j in range(len(y) - 1)]

    @pl.when(level == 1)
    def _():
        @pl.loop(0, CHUNKS)
        def _(n):
            chunk(n).wait()
            for i in range(per_chunk):
                q = n * per_chunk + i
                base = pl.multiple_of(q * 128, 128)
                for g in range(GROUPS):
                    rev = flow_back[pl.ds(pl.multiple_of(g * pipes + q * 8, 8), 8), :] != 0.0
                    outflow[pl.ds(pl.multiple_of(q * 32, 32) + g, 8, stride=4), :] = jnp.where(
                        rev,
                        cells[pl.ds(base + 4 * g, 8, stride=16), :],
                        cells[pl.ds(base + 4 * g + 3, 8, stride=16), :],
                    )

    @pl.loop(0, faces.shape[0] // 8)
    def _(m):
        for u in range(8):
            pipe = face_s[m * 8 + u]
            face_rows[pl.ds(pl.multiple_of(m * 32, 32) + 4 * u, 4), :] = outflow[
                pl.ds(pl.multiple_of(pipe * 4, 4), 4), :
            ]


def fine_load(p, rev, src, cells, rates, outflow, factor, boosts):
    f = spread(factor, p)
    r = spread(rates, p * 4)
    bo = spread(boosts, p)
    near = cells[pl.ds(pl.multiple_of(p * 16 + 8 * rev, 8), 8), :]
    far = cells[pl.ds(pl.multiple_of(p * 16 + 8 - 8 * rev, 8), 8), :]
    return f, r, bo, near, far, [spread(outflow, src + s) for s in range(GROUPS)]


def fine_step(rev, loaded):
    f, r, bo, near, far, inflow = loaded
    b = f * r
    a = f - b
    edge = lax.broadcasted_iota(jnp.int32, (8, LANES), 0) == 7 * rev
    shift = 1 + 6 * rev
    for s in range(GROUPS):
        q0 = pltpu.roll(near, shift, 0)
        q1 = pltpu.roll(far, shift, 0)
        far = a * far + b * jnp.where(edge, q0, q1)
        near = a * near + b * jnp.where(edge, inflow[s] + bo, q0)
    return near, far


def low_rows():
    return lax.broadcasted_iota(jnp.int32, (8, LANES), 0) < 4


def coarse_load(p, srcs, codes, masks, cells, rates, outflow, factor, boosts):
    loaded = []
    for t in range(2):
        x = cells[pl.ds(pl.multiple_of(p * 16 + 8 * t, 8), 8), :]
        r = [spread(rates, p * 4 + 2 * t + h) for h in range(2)]
        inflow = [spread(outflow, srcs[2 * t + h]) for h in range(2)]
        code = pl.multiple_of(codes[t], 8)
        loaded.append((x, r, inflow, masks[pl.ds(code, 8), :], masks[pl.ds(32 + code, 8), :]))
    return spread(factor, p), spread(boosts, p), loaded


def coarse_step(loaded):
    f, bo, tiles = loaded
    low = low_rows()
    done = []
    for x, r, inflow, turned, edge in tiles:
        up = jnp.where(turned != 0.0, pltpu.roll(x, 7, 0), pltpu.roll(x, 1, 0))
        up = jnp.where(edge != 0.0, jnp.where(low, inflow[0], inflow[1]) + bo, up)
        b = f * jnp.where(low, r[0], r[1])
        done.append((f - b) * x + b * up)
    return done


def fill_masks(masks):
    row = lax.broadcasted_iota(jnp.int32, (8, LANES), 0)
    for code in range(4):
        rev = jnp.where(row < 4, code & 1, code >> 1)
        masks[8 * code : 8 * code + 8, :] = rev.astype(jnp.float32)
        edge = (row & 3) == 3 * rev
        masks[32 + 8 * code : 40 + 8 * code, :] = edge.astype(jnp.float32)


def shares(fine, k, q, new):
    base = pl.multiple_of(q * 128, 128)
    if not fine:
        return new[pl.ds(base + k, 8, stride=16), :]
    part = [new[pl.ds(base + 4 * k + i, 8, stride=16), :] for i in range(4)]
    return ((part[0] + part[1]) + (part[2] + part[3])) * 0.25


def step_kernel(
    table, dirs, cells, rates, outflow, factor, boosts, new, send, ghosts, masks
):
    blocks = dirs.shape[0] // GROUPS
    level = lax.axis_index("level")
    fill_masks(masks)
    state = (cells, rates, outflow, factor, boosts)

    def run(fine):
        def block(b, count):
            def some(m, count):
                lanes = [m * 4 + u for u in range(4)]
                pipes = [b * LANES + j for j in lanes]
                for p, j in zip(pipes, lanes):
                    ghosts[count] = p
                    count = count + table[(GROUPS + 2) * blocks + b, j]
                if fine:
                    revs = [dirs[b, j] for j in lanes]
                    loaded = [
                        fine_load(p, rev, table[b, j], *state)
                        for p, j, rev in zip(pipes, lanes, revs)
                    ]
                    done = [fine_step(rev, one) for rev, one in zip(revs, loaded)]
                    for p, rev, (near, far) in zip(pipes, revs, done):
                        new[pl.ds(pl.multiple_of(p * 16 + 8 * rev, 8), 8), :] = near
                        new[pl.ds(pl.multiple_of(p * 16 + 8 - 8 * rev, 8), 8), :] = far
                else:
                    loaded = [
                        coarse_load(
                            p,
                            [table[g * blocks + b, j] for g in range(GROUPS)],
                            [table[(GROUPS + t) * blocks + b, j] for t in range(2)],
                            masks,
                            *state,
                        )
                        for p, j in zip(pipes, lanes)
                    ]
                    for p, one in zip(pipes, [coarse_step(one) for one in loaded]):
                        for t in range(2):
                            new[pl.ds(pl.multiple_of(p * 16 + 8 * t, 8), 8), :] = one[t]
                return count

            count = lax.fori_loop(0, LANES // 4, some, count)

            @pl.loop(0, LANES // 8)
            def _(m):
                q = b * (LANES // 8) + m
                for k in range(2):
                    send[pl.ds(pl.multiple_of(q * 16, 16) + k, 8, stride=2), :] = shares(
                        fine, k + 2 * fine, q, new
                    )

            return count

        count = lax.fori_loop(0, blocks, block, jnp.int32(0))
        ghosts[blocks * LANES] = count

    @pl.when(level == 0)
    def _():
        run(True)

    @pl.when(level == 1)
    def _():
        run(False)


def arrive_kernel(first, near, arrived, outflow_in, outflow):
    odd = lax.axis_index("dom") % 2
    half = arrived.shape[0]
    slot = 1 - odd if near else odd
    start = pl.multiple_of(first + slot * half, 8)
    outflow[pl.ds(start, half), :] = arrived[...]


def fix_kernel(
    first, table, dirs, ghosts, arrived, rates, factor,
    outflow_in, new_in, send_in, outflow, new, send, masks,
):
    blocks = dirs.shape[0] // GROUPS
    level = lax.axis_index("level")
    arrive_kernel(first, False, arrived, outflow_in, outflow)
    fill_masks(masks)
    count = ghosts[blocks * LANES]
    row = lax.broadcasted_iota(jnp.int32, (8, LANES), 0)

    @pl.when(level == 0)
    def _():
        @pl.loop(0, count)
        def _(i):
            p = ghosts[i]
            b, j = p // LANES, p % LANES
            rev, src = dirs[b, j], table[b, j]
            f = spread(factor, p)
            beta = f * spread(rates, p * 4)
            alpha = f - beta
            edge = row == 7 * rev
            shift = 1 + 6 * rev
            delta = beta * jnp.where(edge, spread(outflow, src), 0.0)
            for s in range(1, GROUPS):
                up = jnp.where(edge, spread(outflow, src + s), pltpu.roll(delta, shift, 0))
                delta = alpha * delta + beta * up
            near = pl.ds(pl.multiple_of(p * 16 + 8 * rev, 8), 8)
            new[near, :] = new[near, :] + delta

            @pl.when(rev == 1)
            def _():
                own = pl.ds(p * 2 + 1, 1)
                send[own, :] = send[own, :] + jnp.sum(delta, axis=0, keepdims=True) * 0.25

    @pl.when(level == 1)
    def _():
        @pl.loop(0, count)
        def _(i):
            p = ghosts[i]
            b, j = p // LANES, p % LANES
            f = spread(factor, p)
            low = row < 4
            for t in range(2):
                code = pl.multiple_of(table[(GROUPS + t) * blocks + b, j], 8)
                edge = masks[pl.ds(32 + code, 8), :] != 0.0
                terms = []
                for g in (2 * t, 2 * t + 1):
                    src = table[g * blocks + b, j]
                    fed = jnp.where(src >= first, jnp.float32(1.0), jnp.float32(0.0))
                    terms.append(spread(rates, p * 4 + g) * spread(outflow, src) * fed)
                own = pl.ds(pl.multiple_of(p * 16 + 8 * t, 8), 8)
                both = jnp.where(low, terms[0], terms[1])
                tile = new[own, :] + jnp.where(edge, f * both, 0.0)
                new[own, :] = tile
                if t == 0:
                    send[pl.ds(p * 2, 2), :] = tile[0:2]


def keep_kernel(new, keep, out, sems):
    level = lax.axis_index("level")
    rows = new.shape[0] // sems.shape[0]
    copies = []
    for n in range(sems.shape[0]):
        part = pl.ds(n * rows, rows)
        copies.append(pltpu.make_async_copy(new.at[part], out.at[part], sems.at[n]))
    for copy in copies:
        copy.start()

    def run(fine):
        @pl.loop(0, new.shape[0] // 256)
        def _(m):
            for u in range(2):
                q = m * 2 + u
                for k in range(2):
                    keep[pl.ds(pl.multiple_of(q * 16, 16) + k, 8, stride=2), :] = shares(
                        fine, k + 2 * (not fine), q, new
                    )

    @pl.when(level == 0)
    def _():
        run(True)

    @pl.when(level == 1)
    def _():
        run(False)

    for copy in copies:
        copy.wait()


def gap_kernel(keep, partner, gap):
    sign = jnp.where(lax.axis_index("level") == 0, jnp.float32(1.0), jnp.float32(-1.0))
    gap[...] = (keep[...] - partner[...]) * sign


def per_device(panels, courant, direction, decay, booster, feeder, face_index):
    pipes = panels.shape[1]
    columns = panels.shape[3]
    faces = face_index.shape[0]
    blocks = pipes // LANES
    domains = lax.axis_size("dom")
    f32, i32 = jnp.float32, jnp.int32
    cells_in = panels.reshape(pipes * SEGF, columns)
    rates_in = courant.reshape(pipes * GROUPS, columns)
    dirs = direction.transpose(1, 2, 0).reshape(GROUPS * blocks, LANES)
    feed = feeder.reshape(blocks, LANES, 2).transpose(0, 2, 1).reshape(2 * blocks, LANES)
    ghost_rows = GROUPS * (pipes + 2 * faces)

    cells, rates, outflow, factor, boosts, table, face_rows = pl.pallas_call(
        load_kernel,
        name="load_step",
        in_specs=[HBM] * 7,
        out_specs=[VMEM] * 7,
        out_shape=[
            pltpu.VMEM((pipes * SEGF, columns), f32),
            pltpu.VMEM((pipes * GROUPS, columns), f32),
            pltpu.VMEM((ghost_rows, columns), f32),
            pltpu.VMEM((pipes, columns), f32),
            pltpu.VMEM((pipes, columns), f32),
            jax.ShapeDtypeStruct(((GROUPS + 4) * blocks, LANES), i32),
            pltpu.VMEM((faces * GROUPS, columns), f32),
        ],
        scratch_shapes=[
            pltpu.VMEM((GROUPS * pipes, columns), f32),
            pltpu.VMEM(dirs.shape, i32),
            pltpu.VMEM(feed.shape, i32),
            pltpu.VMEM((blocks, LANES), f32),
            pltpu.VMEM((blocks, LANES), f32),
            pltpu.SMEM((faces,), i32),
            pltpu.SemaphoreType.DMA((CHUNKS,)),
            pltpu.SemaphoreType.DMA(()),
            pltpu.SemaphoreType.DMA((5,)),
        ],
        compiler_params=params(),
        cost_estimate=cost(5 << 20),
    )(
        *pinned(
            pltpu.HBM, cells_in, rates_in, dirs, feed,
            decay.reshape(blocks, LANES), booster.reshape(blocks, LANES), face_index,
        )
    )

    near_pairs = [(i, i ^ 1) for i in range(domains) if i ^ 1 < domains]
    far_pairs = [(i, i + 1) for i in range(1, domains - 1, 2)]
    far_pairs = far_pairs + [(j, i) for i, j in far_pairs]
    near_rows = lax.ppermute(face_rows, "dom", near_pairs)
    far_rows = lax.ppermute(face_rows, "dom", far_pairs)

    new, send, ghosts = pl.pallas_call(
        step_kernel,
        name="advance_step",
        in_specs=[SMEM] * 2 + [VMEM] * 5,
        out_specs=[VMEM, VMEM, SMEM],
        out_shape=[
            pltpu.VMEM((pipes * SEGF, columns), f32),
            pltpu.VMEM((pipes * 2, columns), f32),
            jax.ShapeDtypeStruct((pipes + 16,), i32),
        ],
        scratch_shapes=[pltpu.VMEM((64, columns), f32)],
        compiler_params=params(),
        cost_estimate=cost(20 << 20),
    )(table, dirs, cells, rates, outflow, factor, boosts)

    first = GROUPS * pipes
    outflow = pl.pallas_call(
        lambda *refs: arrive_kernel(first, True, *refs),
        name="near_arrive",
        in_specs=[VMEM] * 2,
        out_specs=VMEM,
        out_shape=pltpu.VMEM((ghost_rows, columns), f32),
        input_output_aliases={1: 0},
        compiler_params=params(),
        cost_estimate=cost(1 << 19),
    )(near_rows, outflow)

    outflow, new, send = pl.pallas_call(
        lambda *refs: fix_kernel(first, *refs),
        name="ghost_fix",
        in_specs=[SMEM] * 3 + [VMEM] * 6,
        out_specs=[VMEM] * 3,
        out_shape=[
            pltpu.VMEM((ghost_rows, columns), f32),
            pltpu.VMEM((pipes * SEGF, columns), f32),
            pltpu.VMEM((pipes * 2, columns), f32),
        ],
        scratch_shapes=[pltpu.VMEM((64, columns), f32)],
        input_output_aliases={6: 0, 7: 1, 8: 2},
        compiler_params=params(),
        cost_estimate=cost(3 << 20),
    )(table, dirs, ghosts, far_rows, rates, factor, outflow, new, send)

    partner = lax.ppermute(send, "level", [(0, 1), (1, 0)])

    keep, out = pl.pallas_call(
        keep_kernel,
        name="keep_share",
        in_specs=[VMEM],
        out_specs=[VMEM, HBM],
        out_shape=[
            pltpu.VMEM((pipes * 2, columns), f32),
            jax.ShapeDtypeStruct((pipes * SEGF, columns), f32),
        ],
        scratch_shapes=[pltpu.SemaphoreType.DMA((4,))],
        compiler_params=params(),
        cost_estimate=cost(4 << 20),
    )(new)

    gap = pl.pallas_call(
        gap_kernel,
        name="level_gap",
        in_specs=[VMEM] * 2,
        out_specs=VMEM,
        out_shape=jax.ShapeDtypeStruct((pipes * 2, columns), f32),
        compiler_params=params(),
        cost_estimate=cost(1 << 20),
    )(keep, partner)
    return (out.reshape(1, pipes, SEGF, columns), gap.reshape(pipes, 2, columns))


def solution(mesh):
    in_specs = (
        P("level", "dom", None, "samp"),
        P("dom", None, "samp"),
        P("dom", None, "samp"),
        P("dom"),
        P("dom"),
        P("dom", None),
        P("dom"),
    )
    out_specs = (P("level", "dom", None, "samp"), P("dom", "level", "samp"))
    return jax.shard_map(
        per_device, mesh=mesh, in_specs=in_specs, out_specs=out_specs, check_vma=False
    )
```

```python
import jax
import jax.numpy as jnp
from jax import lax
from jax.experimental import pallas as pl
from jax.experimental.pallas import tpu as pltpu
from jax.sharding import PartitionSpec as P

SEGF = 16
SEGC = 4
GROUPS = SEGF // SEGC
LANES = 128
CHUNKS = 4
MARK = -(1 << 31)

HBM = pl.BlockSpec(memory_space=pltpu.HBM)
VMEM = pl.BlockSpec(memory_space=pltpu.VMEM)
SMEM = pl.BlockSpec(memory_space=pltpu.SMEM)


def params():
    return pltpu.CompilerParams(vmem_limit_bytes=8 << 20)


def cost(nbytes):
    return pl.CostEstimate(flops=0, bytes_accessed=nbytes, transcendentals=0)


def pinned(space, *arrays):
    return [pltpu.with_memory_space_constraint(x, space) for x in arrays]


def down_rows(row):
    return jnp.broadcast_to(row, (LANES, LANES)).T


def spread(ref, row):
    return ref[pl.ds(row, 8, stride=0), :]


def load_kernel(
    panel, rate, dirs, feed, decay, boost, faces,
    cells, rates, outflow, factor, boosts, flow_back, words, face_rows,
    dir_v, feed_v, decay_v, boost_v, face_s, panel_sem, rate_sem, small_sem,
):
    rows = panel.shape[0] // CHUNKS
    blocks = decay.shape[0]
    pipes = blocks * LANES
    level = lax.axis_index("level")

    def chunk(n):
        part = pl.ds(pl.multiple_of(n * rows, rows), rows)
        return pltpu.make_async_copy(panel.at[part], cells.at[part], panel_sem.at[n])

    small = [
        pltpu.make_async_copy(src, dst, small_sem.at[n])
        for n, (src, dst) in enumerate(
            ((dirs, dir_v), (feed, feed_v), (decay, decay_v), (boost, boost_v), (faces, face_s))
        )
    ]
    rate_copy = pltpu.make_async_copy(rate, rates, rate_sem)
    for copy in small:
        copy.start()
    rate_copy.start()
    for n in range(CHUNKS):
        chunk(n).start()
    for copy in small:
        copy.wait()

    scale = jnp.where(level == 0, jnp.float32(-0.25), jnp.float32(-1.0))
    fac = jnp.exp(decay_v[...] * scale)
    for b in range(blocks):
        own = slice(b * LANES, (b + 1) * LANES)
        factor[own, :] = down_rows(fac[b : b + 1])
        boosts[own, :] = down_rows(boost_v[b : b + 1])
    outflow[GROUPS * pipes :, :] = jnp.zeros_like(outflow[GROUPS * pipes :, :])
    back = (dir_v[...] == 1).astype(jnp.int32)
    lane = lax.broadcasted_iota(jnp.int32, (1, LANES), 1)
    for b in range(blocks):
        ahead = feed_v[2 * b : 2 * b + 1, :]
        behind = feed_v[2 * b + 1 : 2 * b + 2, :]
        rev = back[b : b + 1, :]
        src = jnp.where(rev == 1, behind, ahead)
        p = lane + b * LANES
        fine = src + (p << 10) + (rev << 20) + jnp.where(src >= pipes, MARK, 0)
        fed = jnp.maximum(ahead, behind) >= pipes
        coarse = ahead + (behind << 10) + (p << 20) + jnp.where(fed, MARK, 0)
        words[b : b + 1, :] = jnp.where(level == 0, fine, coarse)
    backf = back.astype(jnp.float32)

    def back_rows(g):
        for b in range(blocks):
            at = g * blocks + b
            flow_back[at * LANES : (at + 1) * LANES, :] = down_rows(backf[at : at + 1])

    back_rows(0)

    @pl.when(level == 1)
    def _():
        for g in range(1, GROUPS):
            back_rows(g)

    rate_copy.wait()
    per_chunk = pipes // 8 // CHUNKS

    @pl.when(level == 0)
    def _():
        @pl.loop(0, CHUNKS)
        def _(n):
            chunk(n).wait()
            for i in range(per_chunk):
                q = n * per_chunk + i
                base = pl.multiple_of(q * 128, 128)
                own = pl.ds(pl.multiple_of(q * 8, 8), 8)
                rev = flow_back[own, :] != 0.0
                b = factor[own, :] * rates[pl.ds(pl.multiple_of(q * 32, 32), 8, stride=4), :]
                a = factor[own, :] - b
                y = [
                    jnp.where(
                        rev,
                        cells[pl.ds(base + j, 8, stride=16), :],
                        cells[pl.ds(base + 15 - j, 8, stride=16), :],
                    )
                    for j in range(GROUPS)
                ]
                for s in range(GROUPS):
                    outflow[pl.ds(pl.multiple_of(q * 32, 32) + s, 8, stride=4), :] = y[0]
                    y = [a * y[j] + b * y[j + 1] for j in range(len(y) - 1)]

    @pl.when(level == 1)
    def _():
        @pl.loop(0, CHUNKS)
        def _(n):
            chunk(n).wait()
            for i in range(per_chunk):
                q = n * per_chunk + i
                base = pl.multiple_of(q * 128, 128)
                for g in range(GROUPS):
                    rev = flow_back[pl.ds(pl.multiple_of(g * pipes + q * 8, 8), 8), :] != 0.0
                    outflow[pl.ds(pl.multiple_of(q * 32, 32) + g, 8, stride=4), :] = jnp.where(
                        rev,
                        cells[pl.ds(base + 4 * g, 8, stride=16), :],
                        cells[pl.ds(base + 4 * g + 3, 8, stride=16), :],
                    )

    @pl.loop(0, faces.shape[0] // 8)
    def _(m):
        for u in range(8):
            pipe = face_s[m * 8 + u]
            face_rows[pl.ds(pl.multiple_of(m * 32, 32) + 4 * u, 4), :] = outflow[
                pl.ds(pl.multiple_of(pipe * 4, 4), 4), :
            ]


def eight_words(q, words):
    per = LANES // 8
    return [words[q // per, (q % per) * 8 + u] for u in range(8)]


def gather_eight(fine, q, words, outflow, ahead_in, behind_in):
    start = pl.multiple_of(q * 32, 32)
    entries = eight_words(q, words)
    moved = [[outflow[pl.ds(pl.multiple_of((w & 1023) * 4, 4), 4), :] for w in entries]]
    if not fine:
        moved.append(
            [outflow[pl.ds(pl.multiple_of((w >> 10 & 1023) * 4, 4), 4), :] for w in entries]
        )
    for dest, tiles in zip((ahead_in, behind_in), moved):
        for u in range(8):
            dest[pl.ds(start + 4 * u, 4), :] = tiles[u]


def list_eight(q, words, ghosts, count):
    for w in eight_words(q, words):
        ghosts[count] = w
        count = count + lax.shift_right_logical(w, 31)
    return count


def fine_block(q, cells, rates, factor, boosts, flow_back, ahead_in, new, keep, send):
    own = pl.ds(pl.multiple_of(q * 8, 8), 8)
    base = pl.multiple_of(q * 128, 128)
    quad = pl.multiple_of(q * 32, 32)
    pair = pl.multiple_of(q * 16, 16)
    rev = flow_back[own, :] != 0.0
    f = factor[own, :]
    b = f * rates[pl.ds(quad, 8, stride=4), :]
    a = f - b
    bo = boosts[own, :]
    x = [cells[pl.ds(base + k, 8, stride=16), :] for k in range(SEGF)]
    o = [jnp.where(rev, x[SEGF - 1 - k], x[k]) for k in range(SEGF)]
    for s in range(GROUPS):
        inflow = ahead_in[pl.ds(quad + s, 8, stride=4), :] + bo
        o = [a * o[k] + b * (o[k - 1] if k else inflow) for k in range(SEGF)]
    y = [jnp.where(rev, o[SEGF - 1 - k], o[k]) for k in range(SEGF)]
    for k in range(SEGF):
        new[pl.ds(base + k, 8, stride=16), :] = y[k]
    for k in range(SEGC):
        share = ((y[4 * k] + y[4 * k + 1]) + (y[4 * k + 2] + y[4 * k + 3])) * 0.25
        (keep if k < 2 else send)[pl.ds(pair + k % 2, 8, stride=2), :] = share


def coarse_block(
    q, cells, rates, factor, boosts, flow_back, ahead_in, behind_in, new, keep, send
):
    pipes = factor.shape[0]
    own = pl.ds(pl.multiple_of(q * 8, 8), 8)
    base = pl.multiple_of(q * 128, 128)
    quad = pl.multiple_of(q * 32, 32)
    pair = pl.multiple_of(q * 16, 16)
    f = factor[own, :]
    bo = boosts[own, :]
    for g in range(GROUPS):
        rev = flow_back[pl.ds(pl.multiple_of(g * pipes + q * 8, 8), 8), :] != 0.0
        four = pl.ds(quad + g, 8, stride=4)
        b = f * rates[four, :]
        a = f - b
        inflow = jnp.where(rev, behind_in[four, :], ahead_in[four, :]) + bo
        x = [cells[pl.ds(base + 4 * g + k, 8, stride=16), :] for k in range(SEGC)]
        up = [
            jnp.where(
                rev, x[k + 1] if k + 1 < SEGC else inflow, x[k - 1] if k else inflow
            )
            for k in range(SEGC)
        ]
        y = [a * x[k] + b * up[k] for k in range(SEGC)]
        for k in range(SEGC):
            new[pl.ds(base + 4 * g + k, 8, stride=16), :] = y[k]
            if g == 0:
                (send if k < 2 else keep)[pl.ds(pair + k % 2, 8, stride=2), :] = y[k]


def step_kernel(
    words, cells, rates, outflow, factor, boosts, flow_back,
    new, keep, send, ghosts, ahead_in, behind_in,
):
    level = lax.axis_index("level")
    eights = factor.shape[0] // 8

    def run(fine):
        gather_eight(fine, 0, words, outflow, ahead_in, behind_in)

        def some(q, count):
            if fine:
                fine_block(q, cells, rates, factor, boosts, flow_back, ahead_in, new, keep, send)
            else:
                coarse_block(
                    q, cells, rates, factor, boosts, flow_back, ahead_in, behind_in,
                    new, keep, send,
                )
            later = jnp.minimum(q + 1, eights - 1)
            gather_eight(fine, later, words, outflow, ahead_in, behind_in)
            return list_eight(q, words, ghosts, count)

        ghosts[8 * eights] = lax.fori_loop(0, eights, some, jnp.int32(0))

    @pl.when(level == 0)
    def _():
        run(True)

    @pl.when(level == 1)
    def _():
        run(False)


def arrive_kernel(first, near, arrived, outflow_in, outflow):
    odd = lax.axis_index("dom") % 2
    half = arrived.shape[0]
    slot = 1 - odd if near else odd
    start = pl.multiple_of(first + slot * half, 8)
    outflow[pl.ds(start, half), :] = arrived[...]


def fine_fix(first, words, rates, factor, outflow, new, keep, send):
    row = lax.broadcasted_iota(jnp.int32, (8, LANES), 0)
    loaded = []
    for w in words:
        src, p, rev = w & 1023, w >> 10 & 1023, w >> 20 & 1
        near = pl.ds(pl.multiple_of(p * 16 + 8 * rev, 8), 8)
        kept, sent = pl.ds(p * 2, 1), pl.ds(p * 2 + 1, 1)
        inflow = [spread(outflow, src * 4 + s) for s in range(GROUPS)]
        loaded.append((
            rev, near, kept, sent, spread(factor, p), spread(rates, p * 4), inflow,
            new[near, :], keep[kept, :], send[sent, :],
        ))
    done = []
    for rev, near, kept, sent, f, r, inflow, tile, keep_row, send_row in loaded:
        b = f * r
        a = f - b
        edge = row == 7 * rev
        shift = 1 + 6 * rev
        total = b * inflow[0]
        delta = jnp.where(edge, total, 0.0)
        for s in range(1, GROUPS):
            up = jnp.where(edge, inflow[s], pltpu.roll(delta, shift, 0))
            delta = a * delta + b * up
            total = f * total + b * inflow[s]
        part = total[0:1] * 0.25
        back = jnp.where(rev == 1, jnp.float32(1.0), jnp.float32(0.0))
        done.append((
            near, kept, sent, tile + delta,
            keep_row + part * (1.0 - back), send_row + part * back,
        ))
    for near, kept, sent, tile, keep_row, send_row in done:
        new[near, :] = tile
        keep[kept, :] = keep_row
        send[sent, :] = send_row


def coarse_fix(first, words, rates, factor, flow_back, outflow, new, keep, send):
    pipes = factor.shape[0]
    zeros = outflow.shape[0] - 8
    loaded = []
    for w in words:
        p = w >> 20 & 1023
        rows = []
        for src in (w & 1023, w >> 10 & 1023):
            at = jnp.where(src >= pipes, src * 4, zeros)
            rows.append(outflow[pl.ds(pl.multiple_of(at, 4), 4), :])
        low = pl.ds(p * 16, 4, stride=4)
        high = pl.ds(p * 16 + 3, 4, stride=4)
        loaded.append((
            p, low, high, rows, flow_back[pl.ds(p, 4, stride=pipes), :],
            rates[pl.ds(pl.multiple_of(p * 4, 4), 4), :], factor[pl.ds(p, 4, stride=0), :],
            new[low, :], new[high, :],
        ))
    done = []
    for p, low, high, rows, rev, r, f, first_rows, last_rows in loaded:
        turned = rev != 0.0
        delta = f * r * jnp.where(turned, rows[1], rows[0])
        done.append((
            p, low, high,
            first_rows + jnp.where(turned, 0.0, delta), last_rows + jnp.where(turned, delta, 0.0),
        ))
    for p, low, high, first_rows, last_rows in done:
        new[low, :] = first_rows
        new[high, :] = last_rows
        send[pl.ds(p * 2, 1), :] = first_rows[0:1]
        keep[pl.ds(p * 2 + 1, 1), :] = last_rows[0:1]


def fix_kernel(
    first, ghosts, arrived, rates, factor, flow_back,
    outflow_in, new_in, keep_in, send_in, outflow, new, keep, send,
):
    level = lax.axis_index("level")
    arrive_kernel(first, False, arrived, outflow_in, outflow)
    count = ghosts[factor.shape[0]]

    def run(fix, *state):
        def some(start, width):
            at = [start + u for u in range(width)]
            fix(first, [ghosts[i] for i in at], *state)

        whole = count // 4

        @pl.loop(0, whole)
        def _(m):
            some(m * 4, 4)

        @pl.loop(whole * 4, count)
        def _(i):
            some(i, 1)

    @pl.when(level == 0)
    def _():
        run(fine_fix, rates, factor, outflow, new, keep, send)

    @pl.when(level == 1)
    def _():
        run(coarse_fix, rates, factor, flow_back, outflow, new, keep, send)


def write_kernel(new, out, sems):
    rows = new.shape[0] // sems.shape[0]
    copies = []
    for n in range(sems.shape[0]):
        part = pl.ds(n * rows, rows)
        copies.append(pltpu.make_async_copy(new.at[part], out.at[part], sems.at[n]))
    for copy in copies:
        copy.start()
    for copy in copies:
        copy.wait()


def gap_kernel(keep, partner, gap):
    sign = jnp.where(lax.axis_index("level") == 0, jnp.float32(1.0), jnp.float32(-1.0))
    gap[...] = (keep[...] - partner[...]) * sign


def per_device(panels, courant, direction, decay, booster, feeder, face_index):
    pipes = panels.shape[1]
    columns = panels.shape[3]
    faces = face_index.shape[0]
    blocks = pipes // LANES
    domains = lax.axis_size("dom")
    f32, i32 = jnp.float32, jnp.int32
    cells_in = panels.reshape(pipes * SEGF, columns)
    rates_in = courant.reshape(pipes * GROUPS, columns)
    dirs = direction.transpose(1, 2, 0).reshape(GROUPS * blocks, LANES)
    feed = feeder.reshape(blocks, LANES, 2).transpose(0, 2, 1).reshape(2 * blocks, LANES)
    ghost_rows = GROUPS * (pipes + 2 * faces) + 8

    cells, rates, outflow, factor, boosts, flow_back, words, face_rows = pl.pallas_call(
        load_kernel,
        name="load_step",
        in_specs=[HBM] * 7,
        out_specs=[VMEM] * 8,
        out_shape=[
            pltpu.VMEM((pipes * SEGF, columns), f32),
            pltpu.VMEM((pipes * GROUPS, columns), f32),
            pltpu.VMEM((ghost_rows, columns), f32),
            pltpu.VMEM((pipes, columns), f32),
            pltpu.VMEM((pipes, columns), f32),
            pltpu.VMEM((GROUPS * pipes, columns), f32),
            jax.ShapeDtypeStruct((blocks, LANES), i32),
            pltpu.VMEM((faces * GROUPS, columns), f32),
        ],
        scratch_shapes=[
            pltpu.VMEM(dirs.shape, i32),
            pltpu.VMEM(feed.shape, i32),
            pltpu.VMEM((blocks, LANES), f32),
            pltpu.VMEM((blocks, LANES), f32),
            pltpu.SMEM((faces,), i32),
            pltpu.SemaphoreType.DMA((CHUNKS,)),
            pltpu.SemaphoreType.DMA(()),
            pltpu.SemaphoreType.DMA((5,)),
        ],
        compiler_params=params(),
        cost_estimate=cost(5 << 20),
    )(
        *pinned(
            pltpu.HBM, cells_in, rates_in, dirs, feed,
            decay.reshape(blocks, LANES), booster.reshape(blocks, LANES), face_index,
        )
    )

    near_pairs = [(i, i ^ 1) for i in range(domains) if i ^ 1 < domains]
    far_pairs = [(i, i + 1) for i in range(1, domains - 1, 2)]
    far_pairs = far_pairs + [(j, i) for i, j in far_pairs]
    near_rows = lax.ppermute(face_rows, "dom", near_pairs)
    far_rows = lax.ppermute(face_rows, "dom", far_pairs)

    new, keep, send, ghosts = pl.pallas_call(
        step_kernel,
        name="advance_step",
        in_specs=[SMEM] + [VMEM] * 6,
        out_specs=[VMEM, VMEM, VMEM, SMEM],
        out_shape=[
            pltpu.VMEM((pipes * SEGF, columns), f32),
            pltpu.VMEM((pipes * 2, columns), f32),
            pltpu.VMEM((pipes * 2, columns), f32),
            pltpu.SMEM((pipes + 8,), i32),
        ],
        scratch_shapes=[pltpu.VMEM((GROUPS * pipes, columns), f32)] * 2,
        compiler_params=params(),
        cost_estimate=cost(20 << 20),
    )(words, cells, rates, outflow, factor, boosts, flow_back)

    first = GROUPS * pipes
    outflow = pl.pallas_call(
        lambda *refs: arrive_kernel(first, True, *refs),
        name="near_arrive",
        in_specs=[VMEM] * 2,
        out_specs=VMEM,
        out_shape=pltpu.VMEM((ghost_rows, columns), f32),
        input_output_aliases={1: 0},
        compiler_params=params(),
        cost_estimate=cost(1 << 19),
    )(near_rows, outflow)

    outflow, new, keep, send = pl.pallas_call(
        lambda *refs: fix_kernel(first, *refs),
        name="ghost_fix",
        in_specs=[SMEM] + [VMEM] * 8,
        out_specs=[VMEM] * 4,
        out_shape=[
            pltpu.VMEM((ghost_rows, columns), f32),
            pltpu.VMEM((pipes * SEGF, columns), f32),
            pltpu.VMEM((pipes * 2, columns), f32),
            pltpu.VMEM((pipes * 2, columns), f32),
        ],
        input_output_aliases={5: 0, 6: 1, 7: 2, 8: 3},
        compiler_params=params(),
        cost_estimate=cost(3 << 20),
    )(ghosts, far_rows, rates, factor, flow_back, outflow, new, keep, send)

    partner = lax.ppermute(send, "level", [(0, 1), (1, 0)])

    out = pl.pallas_call(
        write_kernel,
        name="write_cells",
        in_specs=[VMEM],
        out_specs=HBM,
        out_shape=jax.ShapeDtypeStruct((pipes * SEGF, columns), f32),
        scratch_shapes=[pltpu.SemaphoreType.DMA((4,))],
        compiler_params=params(),
        cost_estimate=cost(4 << 20),
    )(new)

    gap = pl.pallas_call(
        gap_kernel,
        name="level_gap",
        in_specs=[VMEM] * 2,
        out_specs=VMEM,
        out_shape=jax.ShapeDtypeStruct((pipes * 2, columns), f32),
        compiler_params=params(),
        cost_estimate=cost(1 << 20),
    )(keep, partner)
    return (out.reshape(1, pipes, SEGF, columns), gap.reshape(pipes, 2, columns))


def solution(mesh):
    in_specs = (
        P("level", "dom", None, "samp"),
        P("dom", None, "samp"),
        P("dom", None, "samp"),
        P("dom"),
        P("dom"),
        P("dom", None),
        P("dom"),
    )
    out_specs = (P("level", "dom", None, "samp"), P("dom", "level", "samp"))
    return jax.shard_map(
        per_device, mesh=mesh, in_specs=in_specs, out_specs=out_specs, check_vma=False
    )
```

```python
import jax
import jax.numpy as jnp
from jax import lax
from jax.experimental import pallas as pl
from jax.experimental.pallas import tpu as pltpu
from jax.sharding import PartitionSpec as P

SEGF = 16
SEGC = 4
GROUPS = SEGF // SEGC
LANES = 128
CHUNKS = 4
MARK = -(1 << 31)

HBM = pl.BlockSpec(memory_space=pltpu.HBM)
VMEM = pl.BlockSpec(memory_space=pltpu.VMEM)
SMEM = pl.BlockSpec(memory_space=pltpu.SMEM)


def params():
    return pltpu.CompilerParams(vmem_limit_bytes=8 << 20)


def cost(nbytes):
    return pl.CostEstimate(flops=0, bytes_accessed=nbytes, transcendentals=0)


def pinned(space, *arrays):
    return [pltpu.with_memory_space_constraint(x, space) for x in arrays]


def down_rows(row):
    return jnp.broadcast_to(row, (LANES, LANES)).T


def spread(ref, row):
    return ref[pl.ds(row, 8, stride=0), :]


def load_kernel(
    panel, rate, dirs, feed, decay, boost, faces,
    cells, rates, outflow, factor, boosts, flow_back, words, face_rows,
    dir_v, feed_v, decay_v, boost_v, face_s, panel_sem, rate_sem, small_sem,
):
    rows = panel.shape[0] // CHUNKS
    blocks = decay.shape[0]
    pipes = blocks * LANES
    level = lax.axis_index("level")

    def chunk(n):
        part = pl.ds(pl.multiple_of(n * rows, rows), rows)
        return pltpu.make_async_copy(panel.at[part], cells.at[part], panel_sem.at[n])

    small = [
        pltpu.make_async_copy(src, dst, small_sem.at[n])
        for n, (src, dst) in enumerate(
            ((dirs, dir_v), (feed, feed_v), (decay, decay_v), (boost, boost_v), (faces, face_s))
        )
    ]
    rate_copy = pltpu.make_async_copy(rate, rates, rate_sem)
    for copy in small:
        copy.start()
    rate_copy.start()
    for n in range(CHUNKS):
        chunk(n).start()
    for copy in small:
        copy.wait()

    scale = jnp.where(level == 0, jnp.float32(-0.25), jnp.float32(-1.0))
    fac = jnp.exp(decay_v[...] * scale)
    for b in range(blocks):
        own = slice(b * LANES, (b + 1) * LANES)
        factor[own, :] = down_rows(fac[b : b + 1])
        boosts[own, :] = down_rows(boost_v[b : b + 1])
    outflow[GROUPS * pipes :, :] = jnp.zeros_like(outflow[GROUPS * pipes :, :])
    back = (dir_v[...] == 1).astype(jnp.int32)
    lane = lax.broadcasted_iota(jnp.int32, (1, LANES), 1)
    for b in range(blocks):
        ahead = feed_v[2 * b : 2 * b + 1, :]
        behind = feed_v[2 * b + 1 : 2 * b + 2, :]
        rev = back[b : b + 1, :]
        src = jnp.where(rev == 1, behind, ahead)
        p = lane + b * LANES
        fine = src + (p << 10) + (rev << 20) + jnp.where(src >= pipes, MARK, 0)
        revs = [back[g * blocks + b : g * blocks + b + 1, :] for g in range(GROUPS)]
        most = jnp.maximum(jnp.maximum(revs[0], revs[1]), jnp.maximum(revs[2], revs[3]))
        least = jnp.minimum(jnp.minimum(revs[0], revs[1]), jnp.minimum(revs[2], revs[3]))
        fed = jnp.maximum(ahead * (1 - least), behind * most) >= pipes
        coarse = ahead + (behind << 10) + (p << 20) + jnp.where(fed, MARK, 0)
        words[b : b + 1, :] = jnp.where(level == 0, fine, coarse)
    backf = back.astype(jnp.float32)

    def back_rows(g):
        for b in range(blocks):
            at = g * blocks + b
            flow_back[at * LANES : (at + 1) * LANES, :] = down_rows(backf[at : at + 1])

    back_rows(0)

    @pl.when(level == 1)
    def _():
        for g in range(1, GROUPS):
            back_rows(g)

    rate_copy.wait()
    per_chunk = pipes // 8 // CHUNKS

    @pl.when(level == 0)
    def _():
        @pl.loop(0, CHUNKS)
        def _(n):
            chunk(n).wait()
            for i in range(per_chunk):
                q = n * per_chunk + i
                base = pl.multiple_of(q * 128, 128)
                own = pl.ds(pl.multiple_of(q * 8, 8), 8)
                rev = flow_back[own, :] != 0.0
                b = factor[own, :] * rates[pl.ds(pl.multiple_of(q * 32, 32), 8, stride=4), :]
                a = factor[own, :] - b
                y = [
                    jnp.where(
                        rev,
                        cells[pl.ds(base + j, 8, stride=16), :],
                        cells[pl.ds(base + 15 - j, 8, stride=16), :],
                    )
                    for j in range(GROUPS)
                ]
                for s in range(GROUPS):
                    outflow[pl.ds(pl.multiple_of(q * 32, 32) + s, 8, stride=4), :] = y[0]
                    y = [a * y[j] + b * y[j + 1] for j in range(len(y) - 1)]

    @pl.when(level == 1)
    def _():
        @pl.loop(0, CHUNKS)
        def _(n):
            chunk(n).wait()
            for i in range(per_chunk):
                q = n * per_chunk + i
                base = pl.multiple_of(q * 128, 128)
                for g in range(GROUPS):
                    rev = flow_back[pl.ds(pl.multiple_of(g * pipes + q * 8, 8), 8), :] != 0.0
                    outflow[pl.ds(pl.multiple_of(q * 32, 32) + g, 8, stride=4), :] = jnp.where(
                        rev,
                        cells[pl.ds(base + 4 * g, 8, stride=16), :],
                        cells[pl.ds(base + 4 * g + 3, 8, stride=16), :],
                    )

    @pl.loop(0, faces.shape[0] // 8)
    def _(m):
        moved = [
            outflow[pl.ds(pl.multiple_of(face_s[m * 8 + u] * 4, 4), 4), :] for u in range(8)
        ]
        for u in range(8):
            face_rows[pl.ds(pl.multiple_of(m * 32, 32) + 4 * u, 4), :] = moved[u]


def eight_words(q, words):
    per = LANES // 8
    return [words[q // per, (q % per) * 8 + u] for u in range(8)]


def gather_eight(fine, q, words, outflow, ahead_in, behind_in):
    start = pl.multiple_of(q * 32, 32)
    entries = eight_words(q, words)
    moved = [[outflow[pl.ds(pl.multiple_of((w & 1023) * 4, 4), 4), :] for w in entries]]
    if not fine:
        moved.append(
            [outflow[pl.ds(pl.multiple_of((w >> 10 & 1023) * 4, 4), 4), :] for w in entries]
        )
    for dest, tiles in zip((ahead_in, behind_in), moved):
        for u in range(8):
            dest[pl.ds(start + 4 * u, 4), :] = tiles[u]


def list_eight(q, words, ghosts, count):
    for w in eight_words(q, words):
        ghosts[count] = w
        count = count + lax.shift_right_logical(w, 31)
    return count


def fine_block(q, cells, rates, factor, boosts, flow_back, ahead_in, new, shares):
    kept, kept_mid, sent_mid, sent = shares
    own = pl.ds(pl.multiple_of(q * 8, 8), 8)
    base = pl.multiple_of(q * 128, 128)
    quad = pl.multiple_of(q * 32, 32)
    rev = flow_back[own, :] != 0.0
    f = factor[own, :]
    b = f * rates[pl.ds(quad, 8, stride=4), :]
    a = f - b
    bo = boosts[own, :]
    x = [cells[pl.ds(base + k, 8, stride=16), :] for k in range(SEGF)]
    o = [jnp.where(rev, x[SEGF - 1 - k], x[k]) for k in range(SEGF)]
    for s in range(GROUPS):
        inflow = ahead_in[pl.ds(quad + s, 8, stride=4), :] + bo
        o = [a * o[k] + b * (o[k - 1] if k else inflow) for k in range(SEGF)]
    y = [jnp.where(rev, o[SEGF - 1 - k], o[k]) for k in range(SEGF)]
    for k in range(SEGF):
        new[pl.ds(base + k, 8, stride=16), :] = y[k]
    for k, dest in enumerate((kept, kept_mid, sent_mid, sent)):
        dest[own, :] = ((y[4 * k] + y[4 * k + 1]) + (y[4 * k + 2] + y[4 * k + 3])) * 0.25


def coarse_block(
    q, cells, rates, factor, boosts, flow_back, ahead_in, behind_in, new, shares
):
    kept, kept_mid, sent_mid, sent = shares
    pipes = factor.shape[0]
    own = pl.ds(pl.multiple_of(q * 8, 8), 8)
    base = pl.multiple_of(q * 128, 128)
    quad = pl.multiple_of(q * 32, 32)
    f = factor[own, :]
    bo = boosts[own, :]
    for g in range(GROUPS):
        rev = flow_back[pl.ds(pl.multiple_of(g * pipes + q * 8, 8), 8), :] != 0.0
        four = pl.ds(quad + g, 8, stride=4)
        b = f * rates[four, :]
        a = f - b
        inflow = jnp.where(rev, behind_in[four, :], ahead_in[four, :]) + bo
        x = [cells[pl.ds(base + 4 * g + k, 8, stride=16), :] for k in range(SEGC)]
        up = [
            jnp.where(
                rev, x[k + 1] if k + 1 < SEGC else inflow, x[k - 1] if k else inflow
            )
            for k in range(SEGC)
        ]
        y = [a * x[k] + b * up[k] for k in range(SEGC)]
        for k in range(SEGC):
            new[pl.ds(base + 4 * g + k, 8, stride=16), :] = y[k]
            if g == 0:
                (sent, sent_mid, kept_mid, kept)[k][own, :] = y[k]


def step_kernel(
    words, cells, rates, outflow, factor, boosts, flow_back,
    new, out, kept, kept_mid, sent_mid, sent, ghosts, ahead_in, behind_in, sems,
):
    shares = (kept, kept_mid, sent_mid, sent)
    level = lax.axis_index("level")
    eights = factor.shape[0] // 8
    parts = sems.shape[0]
    rows = new.shape[0] // parts

    def written(n):
        part = pl.ds(pl.multiple_of(n * rows, rows), rows)
        return pltpu.make_async_copy(new.at[part], out.at[part], sems.at[n])

    def run(fine):
        gather_eight(fine, 0, words, outflow, ahead_in, behind_in)

        def some(q, count):
            if fine:
                fine_block(q, cells, rates, factor, boosts, flow_back, ahead_in, new, shares)
            else:
                coarse_block(
                    q, cells, rates, factor, boosts, flow_back, ahead_in, behind_in,
                    new, shares,
                )
            later = jnp.minimum(q + 1, eights - 1)
            gather_eight(fine, later, words, outflow, ahead_in, behind_in)
            return list_eight(q, words, ghosts, count)

        per = eights // parts

        def part(n, count):
            count = lax.fori_loop(n * per, (n + 1) * per, some, count)
            written(n).start()
            return count

        ghosts[8 * eights] = lax.fori_loop(0, parts, part, jnp.int32(0))

    @pl.when(level == 0)
    def _():
        run(True)

    @pl.when(level == 1)
    def _():
        run(False)

    for n in range(parts):
        written(n).wait()


def arrive_kernel(first, near, arrived, outflow_in, outflow):
    odd = lax.axis_index("dom") % 2
    half = arrived.shape[0]
    slot = 1 - odd if near else odd
    start = pl.multiple_of(first + slot * half, 8)
    outflow[pl.ds(start, half), :] = arrived[...]


def over_list(count, ghosts, width, each):
    whole = count // width

    @pl.loop(0, whole)
    def _(m):
        each([ghosts[m * width + u] for u in range(width)])

    @pl.loop(whole * width, count)
    def _(i):
        each([ghosts[i]])


def send_kernel(
    first, ghosts, arrived, rates, factor, flow_back,
    outflow_in, sent_in, new_in, kept_in, outflow, sent, new, kept,
):
    pipes = factor.shape[0]
    level = lax.axis_index("level")
    arrive_kernel(first, False, arrived, outflow_in, outflow)

    def fine(entries):
        done = []
        for w in entries:
            src, p, rev = w & 1023, w >> 10 & 1023, w >> 20 & 1
            own = pl.ds(p, 1)
            rows = outflow[pl.ds(pl.multiple_of(src * 4, 4), 4), :]
            f, r = factor[own, :], rates[pl.ds(p * 4, 1), :]
            total = rows[0:1]
            for s in range(1, GROUPS):
                total = f * total + rows[s : s + 1]
            back = jnp.where(rev == 1, jnp.float32(0.25), jnp.float32(0.0))
            done.append((own, sent[own, :] + f * r * total * back))
        for own, row in done:
            sent[own, :] = row

    def coarse(entries):
        coarse_fix(entries, rates, factor, flow_back, outflow, new, kept, sent)

    @pl.when(level == 0)
    def _():
        over_list(ghosts[pipes], ghosts, 8, fine)

    @pl.when(level == 1)
    def _():
        over_list(ghosts[pipes], ghosts, 4, coarse)


def fine_fix(entries, rates, factor, outflow, new, kept):
    row = lax.broadcasted_iota(jnp.int32, (8, LANES), 0)
    loaded = []
    for w in entries:
        src, p, rev = w & 1023, w >> 10 & 1023, w >> 20 & 1
        near = pl.ds(pl.multiple_of(p * 16 + 8 * rev, 8), 8)
        own = pl.ds(p, 1)
        inflow = [spread(outflow, src * 4 + s) for s in range(GROUPS)]
        loaded.append((
            rev, near, own, spread(factor, p), spread(rates, p * 4), inflow,
            new[near, :], kept[own, :],
        ))
    done = []
    for rev, near, own, f, r, inflow, tile, kept_row in loaded:
        b = f * r
        a = f - b
        edge = row == 7 * rev
        shift = 1 + 6 * rev
        total = b * inflow[0]
        delta = jnp.where(edge, total, 0.0)
        for s in range(1, GROUPS):
            up = jnp.where(edge, inflow[s], pltpu.roll(delta, shift, 0))
            delta = a * delta + b * up
            total = f * total + b * inflow[s]
        ahead = jnp.where(rev == 1, jnp.float32(0.0), jnp.float32(0.25))
        done.append((near, own, tile + delta, kept_row + total[0:1] * ahead))
    for near, own, tile, kept_row in done:
        new[near, :] = tile
        kept[own, :] = kept_row


def coarse_fix(entries, rates, factor, flow_back, outflow, new, kept, sent):
    pipes = factor.shape[0]
    zeros = outflow.shape[0] - 8
    loaded = []
    for w in entries:
        p = w >> 20 & 1023
        rows = []
        for src in (w & 1023, w >> 10 & 1023):
            at = jnp.where(src >= pipes, src * 4, zeros)
            rows.append(outflow[pl.ds(pl.multiple_of(at, 4), 4), :])
        low = pl.ds(p * 16, 4, stride=4)
        high = pl.ds(p * 16 + 3, 4, stride=4)
        loaded.append((
            p, low, high, rows, flow_back[pl.ds(p, 4, stride=pipes), :],
            rates[pl.ds(pl.multiple_of(p * 4, 4), 4), :], factor[pl.ds(p, 4, stride=0), :],
            new[low, :], new[high, :],
        ))
    done = []
    for p, low, high, rows, rev, r, f, first_rows, last_rows in loaded:
        turned = rev != 0.0
        delta = f * r * jnp.where(turned, rows[1], rows[0])
        done.append((
            p, low, high,
            first_rows + jnp.where(turned, 0.0, delta), last_rows + jnp.where(turned, delta, 0.0),
        ))
    for p, low, high, first_rows, last_rows in done:
        new[low, :] = first_rows
        new[high, :] = last_rows
        kept[pl.ds(p, 1), :] = last_rows[0:1]
        sent[pl.ds(p, 1), :] = first_rows[0:1]


def fix_kernel(
    ghosts, rates, factor, outflow, new_in, kept_in, out_in, new, kept, out, sem
):
    pipes = factor.shape[0]
    level = lax.axis_index("level")
    shift = jnp.where(level == 0, 10, 20)
    count = ghosts[pipes]

    def write(entries):
        for w in entries:
            p = lax.shift_right_logical(w, shift) & 1023
            part = pl.ds(pl.multiple_of(p * SEGF, SEGF), SEGF)
            pltpu.make_async_copy(new.at[part], out.at[part], sem).start()

    def fine(entries):
        fine_fix(entries, rates, factor, outflow, new, kept)
        write(entries)

    @pl.when(level == 0)
    def _():
        over_list(count, ghosts, 4, fine)

    @pl.when(level == 1)
    def _():
        over_list(count, ghosts, 8, write)

    def wait(some):
        part = pl.ds(0, SEGF * some)
        pltpu.make_async_copy(new.at[part], out.at[part], sem).wait()

    whole = count // 8

    @pl.loop(0, whole)
    def _(m):
        wait(8)

    @pl.loop(whole * 8, count)
    def _(i):
        wait(1)


def gap_kernel(kept, kept_mid, partner_mid, partner, gap):
    level = lax.axis_index("level")
    sign = jnp.where(level == 0, jnp.float32(1.0), jnp.float32(-1.0))

    @pl.loop(0, kept.shape[0] // 32)
    def _(m):
        for u in range(4):
            own = pl.ds(pl.multiple_of(m * 32 + 8 * u, 8), 8)
            pair = pl.multiple_of(m * 64 + 16 * u, 16)
            gap[pl.ds(pair + level, 8, stride=2), :] = (kept[own, :] - partner[own, :]) * sign
            gap[pl.ds(pair + 1 - level, 8, stride=2), :] = (
                kept_mid[own, :] - partner_mid[own, :]
            ) * sign


def per_device(panels, courant, direction, decay, booster, feeder, face_index):
    pipes = panels.shape[1]
    columns = panels.shape[3]
    faces = face_index.shape[0]
    blocks = pipes // LANES
    domains = lax.axis_size("dom")
    f32, i32 = jnp.float32, jnp.int32
    cells_in = panels.reshape(pipes * SEGF, columns)
    rates_in = courant.reshape(pipes * GROUPS, columns)
    dirs = direction.transpose(1, 2, 0).reshape(GROUPS * blocks, LANES)
    feed = feeder.reshape(blocks, LANES, 2).transpose(0, 2, 1).reshape(2 * blocks, LANES)
    ghost_rows = GROUPS * (pipes + 2 * faces) + 8

    cells, rates, outflow, factor, boosts, flow_back, words, face_rows = pl.pallas_call(
        load_kernel,
        name="load_step",
        in_specs=[HBM] * 7,
        out_specs=[VMEM] * 8,
        out_shape=[
            pltpu.VMEM((pipes * SEGF, columns), f32),
            pltpu.VMEM((pipes * GROUPS, columns), f32),
            pltpu.VMEM((ghost_rows, columns), f32),
            pltpu.VMEM((pipes, columns), f32),
            pltpu.VMEM((pipes, columns), f32),
            pltpu.VMEM((GROUPS * pipes, columns), f32),
            jax.ShapeDtypeStruct((blocks, LANES), i32),
            pltpu.VMEM((faces * GROUPS, columns), f32),
        ],
        scratch_shapes=[
            pltpu.VMEM(dirs.shape, i32),
            pltpu.VMEM(feed.shape, i32),
            pltpu.VMEM((blocks, LANES), f32),
            pltpu.VMEM((blocks, LANES), f32),
            pltpu.SMEM((faces,), i32),
            pltpu.SemaphoreType.DMA((CHUNKS,)),
            pltpu.SemaphoreType.DMA(()),
            pltpu.SemaphoreType.DMA((5,)),
        ],
        compiler_params=params(),
        cost_estimate=cost(5 << 20),
    )(
        *pinned(
            pltpu.HBM, cells_in, rates_in, dirs, feed,
            decay.reshape(blocks, LANES), booster.reshape(blocks, LANES), face_index,
        )
    )

    near_pairs = [(i, i ^ 1) for i in range(domains) if i ^ 1 < domains]
    far_pairs = [(i, i + 1) for i in range(1, domains - 1, 2)]
    far_pairs = far_pairs + [(j, i) for i, j in far_pairs]
    near_rows = lax.ppermute(face_rows, "dom", near_pairs)
    far_rows = lax.ppermute(face_rows, "dom", far_pairs)

    new, out, kept, kept_mid, sent_mid, sent, ghosts = pl.pallas_call(
        step_kernel,
        name="advance_step",
        in_specs=[SMEM] + [VMEM] * 6,
        out_specs=[VMEM, HBM] + [VMEM] * 4 + [SMEM],
        out_shape=[
            pltpu.VMEM((pipes * SEGF, columns), f32),
            jax.ShapeDtypeStruct((pipes * SEGF, columns), f32),
            *[pltpu.VMEM((pipes, columns), f32)] * 4,
            pltpu.SMEM((pipes + 8,), i32),
        ],
        scratch_shapes=[pltpu.VMEM((GROUPS * pipes, columns), f32)] * 2
        + [pltpu.SemaphoreType.DMA((8,))],
        compiler_params=params(),
        cost_estimate=cost(20 << 20),
    )(words, cells, rates, outflow, factor, boosts, flow_back)

    swap = [(0, 1), (1, 0)]
    partner_mid = lax.ppermute(sent_mid, "level", swap)
    first = GROUPS * pipes
    outflow = pl.pallas_call(
        lambda *refs: arrive_kernel(first, True, *refs),
        name="near_arrive",
        in_specs=[VMEM] * 2,
        out_specs=VMEM,
        out_shape=pltpu.VMEM((ghost_rows, columns), f32),
        input_output_aliases={1: 0},
        compiler_params=params(),
        cost_estimate=cost(1 << 19),
    )(near_rows, outflow)

    outflow, sent, new, kept = pl.pallas_call(
        lambda *refs: send_kernel(first, *refs),
        name="ghost_send",
        in_specs=[SMEM] + [VMEM] * 8,
        out_specs=[VMEM] * 4,
        out_shape=[
            pltpu.VMEM((ghost_rows, columns), f32),
            pltpu.VMEM((pipes, columns), f32),
            pltpu.VMEM((pipes * SEGF, columns), f32),
            pltpu.VMEM((pipes, columns), f32),
        ],
        input_output_aliases={5: 0, 6: 1, 7: 2, 8: 3},
        compiler_params=params(),
        cost_estimate=cost(1 << 20),
    )(ghosts, far_rows, rates, factor, flow_back, outflow, sent, new, kept)

    partner = lax.ppermute(sent, "level", swap)

    new, kept, out = pl.pallas_call(
        fix_kernel,
        name="ghost_fix",
        in_specs=[SMEM] + [VMEM] * 5 + [HBM],
        out_specs=[VMEM, VMEM, HBM],
        out_shape=[
            pltpu.VMEM((pipes * SEGF, columns), f32),
            pltpu.VMEM((pipes, columns), f32),
            jax.ShapeDtypeStruct((pipes * SEGF, columns), f32),
        ],
        scratch_shapes=[pltpu.SemaphoreType.DMA(())],
        input_output_aliases={4: 0, 5: 1, 6: 2},
        compiler_params=params(),
        cost_estimate=cost(4 << 20),
    )(ghosts, rates, factor, outflow, new, kept, *pinned(pltpu.HBM, out))

    gap = pl.pallas_call(
        gap_kernel,
        name="level_gap",
        in_specs=[VMEM] * 4,
        out_specs=VMEM,
        out_shape=jax.ShapeDtypeStruct((pipes * 2, columns), f32),
        compiler_params=params(),
        cost_estimate=cost(1 << 20),
    )(kept, kept_mid, partner_mid, partner)
    return (out.reshape(1, pipes, SEGF, columns), gap.reshape(pipes, 2, columns))


def solution(mesh):
    in_specs = (
        P("level", "dom", None, "samp"),
        P("dom", None, "samp"),
        P("dom", None, "samp"),
        P("dom"),
        P("dom"),
        P("dom", None),
        P("dom"),
    )
    out_specs = (P("level", "dom", None, "samp"), P("dom", "level", "samp"))
    return jax.shard_map(
        per_device, mesh=mesh, in_specs=in_specs, out_specs=out_specs, check_vma=False
    )
```

```python
import jax
import jax.numpy as jnp
from jax import lax
from jax.experimental import pallas as pl
from jax.experimental.pallas import tpu as pltpu
from jax.sharding import PartitionSpec as P

SEGF = 16
SEGC = 4
GROUPS = SEGF // SEGC
LANES = 128
CHUNKS = 4
MARK = -(1 << 31)

HBM = pl.BlockSpec(memory_space=pltpu.HBM)
VMEM = pl.BlockSpec(memory_space=pltpu.VMEM)
SMEM = pl.BlockSpec(memory_space=pltpu.SMEM)


def params():
    return pltpu.CompilerParams(vmem_limit_bytes=8 << 20)


def cost(nbytes):
    return pl.CostEstimate(flops=0, bytes_accessed=nbytes, transcendentals=0)


def pinned(space, *arrays):
    return [pltpu.with_memory_space_constraint(x, space) for x in arrays]


def down_rows(row):
    return jnp.broadcast_to(row, (LANES, LANES)).T


def spread(ref, row):
    return ref[pl.ds(row, 8, stride=0), :]


def load_kernel(
    panel, rate, dirs, feed, decay, boost, faces,
    cells, rates, outflow, factor, boosts, flow_back, words, face_rows,
    dir_v, feed_v, decay_v, boost_v, face_s, panel_sem, rate_sem, small_sem,
):
    rows = panel.shape[0] // CHUNKS
    blocks = decay.shape[0]
    pipes = blocks * LANES
    level = lax.axis_index("level")

    def chunk(n):
        part = pl.ds(pl.multiple_of(n * rows, rows), rows)
        return pltpu.make_async_copy(panel.at[part], cells.at[part], panel_sem.at[n])

    small = [
        pltpu.make_async_copy(src, dst, small_sem.at[n])
        for n, (src, dst) in enumerate(
            ((dirs, dir_v), (feed, feed_v), (decay, decay_v), (boost, boost_v), (faces, face_s))
        )
    ]
    rate_copy = pltpu.make_async_copy(rate, rates, rate_sem)
    for copy in small:
        copy.start()
    rate_copy.start()
    for n in range(CHUNKS):
        chunk(n).start(priority=1)
    for copy in small:
        copy.wait()

    scale = jnp.where(level == 0, jnp.float32(-0.25), jnp.float32(-1.0))
    fac = jnp.exp(decay_v[...] * scale)
    for b in range(blocks):
        own = slice(b * LANES, (b + 1) * LANES)
        factor[own, :] = down_rows(fac[b : b + 1])
        boosts[own, :] = down_rows(boost_v[b : b + 1])
    outflow[GROUPS * pipes :, :] = jnp.zeros_like(outflow[GROUPS * pipes :, :])
    back = (dir_v[...] == 1).astype(jnp.int32)
    lane = lax.broadcasted_iota(jnp.int32, (1, LANES), 1)
    for b in range(blocks):
        ahead = feed_v[2 * b : 2 * b + 1, :]
        behind = feed_v[2 * b + 1 : 2 * b + 2, :]
        rev = back[b : b + 1, :]
        src = jnp.where(rev == 1, behind, ahead)
        p = lane + b * LANES
        fine = src + (p << 10) + (rev << 20) + jnp.where(src >= pipes, MARK, 0)
        revs = [back[g * blocks + b : g * blocks + b + 1, :] for g in range(GROUPS)]
        most = jnp.maximum(jnp.maximum(revs[0], revs[1]), jnp.maximum(revs[2], revs[3]))
        least = jnp.minimum(jnp.minimum(revs[0], revs[1]), jnp.minimum(revs[2], revs[3]))
        fed = jnp.maximum(ahead * (1 - least), behind * most) >= pipes
        coarse = ahead + (behind << 10) + (p << 20) + jnp.where(fed, MARK, 0)
        words[b : b + 1, :] = jnp.where(level == 0, fine, coarse)
    backf = back.astype(jnp.float32)

    def back_rows(g):
        for b in range(blocks):
            at = g * blocks + b
            flow_back[at * LANES : (at + 1) * LANES, :] = down_rows(backf[at : at + 1])

    back_rows(0)

    @pl.when(level == 1)
    def _():
        for g in range(1, GROUPS):
            back_rows(g)

    rate_copy.wait()
    per_chunk = pipes // 8 // CHUNKS

    @pl.when(level == 0)
    def _():
        @pl.loop(0, CHUNKS)
        def _(n):
            chunk(n).wait()
            for i in range(per_chunk):
                q = n * per_chunk + i
                base = pl.multiple_of(q * 128, 128)
                own = pl.ds(pl.multiple_of(q * 8, 8), 8)
                rev = flow_back[own, :] != 0.0
                b = factor[own, :] * rates[pl.ds(pl.multiple_of(q * 32, 32), 8, stride=4), :]
                a = factor[own, :] - b
                y = [
                    jnp.where(
                        rev,
                        cells[pl.ds(base + j, 8, stride=16), :],
                        cells[pl.ds(base + 15 - j, 8, stride=16), :],
                    )
                    for j in range(GROUPS)
                ]
                for s in range(GROUPS):
                    outflow[pl.ds(pl.multiple_of(q * 32, 32) + s, 8, stride=4), :] = y[0]
                    y = [a * y[j] + b * y[j + 1] for j in range(len(y) - 1)]

    @pl.when(level == 1)
    def _():
        @pl.loop(0, CHUNKS)
        def _(n):
            chunk(n).wait()
            for i in range(per_chunk):
                q = n * per_chunk + i
                base = pl.multiple_of(q * 128, 128)
                for g in range(GROUPS):
                    rev = flow_back[pl.ds(pl.multiple_of(g * pipes + q * 8, 8), 8), :] != 0.0
                    outflow[pl.ds(pl.multiple_of(q * 32, 32) + g, 8, stride=4), :] = jnp.where(
                        rev,
                        cells[pl.ds(base + 4 * g, 8, stride=16), :],
                        cells[pl.ds(base + 4 * g + 3, 8, stride=16), :],
                    )

    @pl.loop(0, faces.shape[0] // 16)
    def _(m):
        moved = [
            outflow[pl.ds(pl.multiple_of(face_s[m * 16 + u] * 4, 4), 4), :] for u in range(16)
        ]
        for u in range(16):
            face_rows[pl.ds(pl.multiple_of(m * 64, 64) + 4 * u, 4), :] = moved[u]


def eight_words(q, words):
    per = LANES // 8
    return [words[q // per, (q % per) * 8 + u] for u in range(8)]


def gather_eight(fine, q, words, outflow, ahead_in, behind_in):
    start = pl.multiple_of(q * 32, 32)
    entries = eight_words(q, words)
    moved = [[outflow[pl.ds(pl.multiple_of((w & 1023) * 4, 4), 4), :] for w in entries]]
    if not fine:
        moved.append(
            [outflow[pl.ds(pl.multiple_of((w >> 10 & 1023) * 4, 4), 4), :] for w in entries]
        )
    for dest, tiles in zip((ahead_in, behind_in), moved):
        for u in range(8):
            dest[pl.ds(start + 4 * u, 4), :] = tiles[u]


def list_eight(q, words, ghosts, count):
    for w in eight_words(q, words):
        ghosts[count] = w
        count = count + lax.shift_right_logical(w, 31)
    return count


def fine_block(q, cells, rates, factor, boosts, flow_back, ahead_in, new, shares):
    kept, kept_mid, sent_mid, sent = shares
    own = pl.ds(pl.multiple_of(q * 8, 8), 8)
    base = pl.multiple_of(q * 128, 128)
    quad = pl.multiple_of(q * 32, 32)
    rev = flow_back[own, :] != 0.0
    f = factor[own, :]
    b = f * rates[pl.ds(quad, 8, stride=4), :]
    a = f - b
    bo = boosts[own, :]
    x = [cells[pl.ds(base + k, 8, stride=16), :] for k in range(SEGF)]
    o = [jnp.where(rev, x[SEGF - 1 - k], x[k]) for k in range(SEGF)]
    for s in range(GROUPS):
        inflow = ahead_in[pl.ds(quad + s, 8, stride=4), :] + bo
        o = [a * o[k] + b * (o[k - 1] if k else inflow) for k in range(SEGF)]
    y = [jnp.where(rev, o[SEGF - 1 - k], o[k]) for k in range(SEGF)]
    for k in range(SEGF):
        new[pl.ds(base + k, 8, stride=16), :] = y[k]
    for k, dest in enumerate((kept, kept_mid, sent_mid, sent)):
        dest[own, :] = ((y[4 * k] + y[4 * k + 1]) + (y[4 * k + 2] + y[4 * k + 3])) * 0.25


def coarse_block(
    q, cells, rates, factor, boosts, flow_back, ahead_in, behind_in, new, shares
):
    kept, kept_mid, sent_mid, sent = shares
    pipes = factor.shape[0]
    own = pl.ds(pl.multiple_of(q * 8, 8), 8)
    base = pl.multiple_of(q * 128, 128)
    quad = pl.multiple_of(q * 32, 32)
    f = factor[own, :]
    bo = boosts[own, :]
    for g in range(GROUPS):
        rev = flow_back[pl.ds(pl.multiple_of(g * pipes + q * 8, 8), 8), :] != 0.0
        four = pl.ds(quad + g, 8, stride=4)
        b = f * rates[four, :]
        a = f - b
        inflow = jnp.where(rev, behind_in[four, :], ahead_in[four, :]) + bo
        x = [cells[pl.ds(base + 4 * g + k, 8, stride=16), :] for k in range(SEGC)]
        up = [
            jnp.where(
                rev, x[k + 1] if k + 1 < SEGC else inflow, x[k - 1] if k else inflow
            )
            for k in range(SEGC)
        ]
        y = [a * x[k] + b * up[k] for k in range(SEGC)]
        for k in range(SEGC):
            new[pl.ds(base + 4 * g + k, 8, stride=16), :] = y[k]
            if g == 0:
                (sent, sent_mid, kept_mid, kept)[k][own, :] = y[k]


def step_kernel(
    words, cells, rates, outflow, factor, boosts, flow_back,
    new, out, kept, kept_mid, sent_mid, sent, ghosts, ahead_in, behind_in, sems,
):
    shares = (kept, kept_mid, sent_mid, sent)
    level = lax.axis_index("level")
    eights = factor.shape[0] // 8
    parts = sems.shape[0]
    rows = new.shape[0] // parts

    def written(n):
        part = pl.ds(pl.multiple_of(n * rows, rows), rows)
        return pltpu.make_async_copy(new.at[part], out.at[part], sems.at[n])

    def run(fine):
        gather_eight(fine, 0, words, outflow, ahead_in, behind_in)

        def some(q, count):
            if fine:
                fine_block(q, cells, rates, factor, boosts, flow_back, ahead_in, new, shares)
            else:
                coarse_block(
                    q, cells, rates, factor, boosts, flow_back, ahead_in, behind_in,
                    new, shares,
                )
            later = jnp.minimum(q + 1, eights - 1)
            gather_eight(fine, later, words, outflow, ahead_in, behind_in)
            return list_eight(q, words, ghosts, count)

        per = eights // parts

        def part(n, count):
            count = lax.fori_loop(n * per, (n + 1) * per, some, count)
            written(n).start()
            return count

        ghosts[8 * eights] = lax.fori_loop(0, parts, part, jnp.int32(0))

    @pl.when(level == 0)
    def _():
        run(True)

    @pl.when(level == 1)
    def _():
        run(False)

    for n in range(parts):
        written(n).wait()


def arrive_kernel(first, near, arrived, outflow_in, outflow):
    odd = lax.axis_index("dom") % 2
    half = arrived.shape[0]
    slot = 1 - odd if near else odd
    start = pl.multiple_of(first + slot * half, 8)
    outflow[pl.ds(start, half), :] = arrived[...]


def over_list(count, ghosts, width, each):
    whole = count // width

    @pl.loop(0, whole)
    def _(m):
        each([ghosts[m * width + u] for u in range(width)])

    @pl.loop(whole * width, count)
    def _(i):
        each([ghosts[i]])


def send_kernel(
    first, ghosts, arrived, rates, factor, flow_back,
    outflow_in, sent_in, new_in, kept_in, outflow, sent, new, kept,
):
    pipes = factor.shape[0]
    level = lax.axis_index("level")
    arrive_kernel(first, False, arrived, outflow_in, outflow)

    def fine(entries):
        done = []
        for w in entries:
            src, p, rev = w & 1023, w >> 10 & 1023, w >> 20 & 1
            own = pl.ds(p, 1)
            rows = outflow[pl.ds(pl.multiple_of(src * 4, 4), 4), :]
            f, r = factor[own, :], rates[pl.ds(p * 4, 1), :]
            total = rows[0:1]
            for s in range(1, GROUPS):
                total = f * total + rows[s : s + 1]
            back = jnp.where(rev == 1, jnp.float32(0.25), jnp.float32(0.0))
            done.append((own, sent[own, :] + f * r * total * back))
        for own, row in done:
            sent[own, :] = row

    def coarse(entries):
        coarse_fix(entries, rates, factor, flow_back, outflow, new, kept, sent)

    @pl.when(level == 0)
    def _():
        over_list(ghosts[pipes], ghosts, 8, fine)

    @pl.when(level == 1)
    def _():
        over_list(ghosts[pipes], ghosts, 4, coarse)


def fine_fix(entries, rates, factor, outflow, new, kept):
    row = lax.broadcasted_iota(jnp.int32, (8, LANES), 0)
    loaded = []
    for w in entries:
        src, p, rev = w & 1023, w >> 10 & 1023, w >> 20 & 1
        near = pl.ds(pl.multiple_of(p * 16 + 8 * rev, 8), 8)
        own = pl.ds(p, 1)
        inflow = [spread(outflow, src * 4 + s) for s in range(GROUPS)]
        loaded.append((
            rev, near, own, spread(factor, p), spread(rates, p * 4), inflow,
            new[near, :], kept[own, :],
        ))
    done = []
    for rev, near, own, f, r, inflow, tile, kept_row in loaded:
        b = f * r
        a = f - b
        edge = row == 7 * rev
        shift = 1 + 6 * rev
        total = b * inflow[0]
        delta = jnp.where(edge, total, 0.0)
        for s in range(1, GROUPS):
            up = jnp.where(edge, inflow[s], pltpu.roll(delta, shift, 0))
            delta = a * delta + b * up
            total = f * total + b * inflow[s]
        ahead = jnp.where(rev == 1, jnp.float32(0.0), jnp.float32(0.25))
        done.append((near, own, tile + delta, kept_row + total[0:1] * ahead))
    for near, own, tile, kept_row in done:
        new[near, :] = tile
        kept[own, :] = kept_row


def coarse_fix(entries, rates, factor, flow_back, outflow, new, kept, sent):
    pipes = factor.shape[0]
    zeros = outflow.shape[0] - 8
    loaded = []
    for w in entries:
        p = w >> 20 & 1023
        rows = []
        for src in (w & 1023, w >> 10 & 1023):
            at = jnp.where(src >= pipes, src * 4, zeros)
            rows.append(outflow[pl.ds(pl.multiple_of(at, 4), 4), :])
        low = pl.ds(p * 16, 4, stride=4)
        high = pl.ds(p * 16 + 3, 4, stride=4)
        loaded.append((
            p, low, high, rows, flow_back[pl.ds(p, 4, stride=pipes), :],
            rates[pl.ds(pl.multiple_of(p * 4, 4), 4), :], factor[pl.ds(p, 4, stride=0), :],
            new[low, :], new[high, :],
        ))
    done = []
    for p, low, high, rows, rev, r, f, first_rows, last_rows in loaded:
        turned = rev != 0.0
        delta = f * r * jnp.where(turned, rows[1], rows[0])
        done.append((
            p, low, high,
            first_rows + jnp.where(turned, 0.0, delta), last_rows + jnp.where(turned, delta, 0.0),
        ))
    for p, low, high, first_rows, last_rows in done:
        new[low, :] = first_rows
        new[high, :] = last_rows
        kept[pl.ds(p, 1), :] = last_rows[0:1]
        sent[pl.ds(p, 1), :] = first_rows[0:1]


def fix_kernel(
    ghosts, rates, factor, outflow, kept_mid, partner_mid, new_in, kept_in, out_in,
    new, kept, out, gap_rows, sem,
):
    pipes = factor.shape[0]
    level = lax.axis_index("level")
    shift = jnp.where(level == 0, 10, 20)
    count = ghosts[pipes]

    def write(entries):
        for w in entries:
            p = lax.shift_right_logical(w, shift) & 1023
            part = pl.ds(pl.multiple_of(p * SEGF, SEGF), SEGF)
            pltpu.make_async_copy(new.at[part], out.at[part], sem).start()

    def fine(entries):
        fine_fix(entries, rates, factor, outflow, new, kept)
        write(entries)

    @pl.when(level == 0)
    def _():
        over_list(count, ghosts, 4, fine)

    @pl.when(level == 1)
    def _():
        over_list(count, ghosts, 8, write)

    sign = jnp.where(level == 0, jnp.float32(1.0), jnp.float32(-1.0))

    @pl.loop(0, pipes // 64)
    def _(m):
        for u in range(8):
            own = pl.ds(pl.multiple_of(m * 64 + 8 * u, 8), 8)
            spots = pl.ds(pl.multiple_of(m * 128, 128) + 16 * u + 1 - level, 8, stride=2)
            gap_rows[spots, :] = (kept_mid[own, :] - partner_mid[own, :]) * sign

    def wait(some):
        part = pl.ds(0, SEGF * some)
        pltpu.make_async_copy(new.at[part], out.at[part], sem).wait()

    whole = count // 8

    @pl.loop(0, whole)
    def _(m):
        wait(8)

    @pl.loop(whole * 8, count)
    def _(i):
        wait(1)


def gap_kernel(kept, partner, rows_in, rows, gap, sems):
    level = lax.axis_index("level")
    sign = jnp.where(level == 0, jnp.float32(1.0), jnp.float32(-1.0))
    parts = sems.shape[0]
    copies = []
    per = kept.shape[0] // 8 // parts
    for n in range(parts):
        for q in range(n * per, (n + 1) * per):
            own = pl.ds(8 * q, 8)
            rows[pl.ds(16 * q + level, 8, stride=2), :] = (kept[own, :] - partner[own, :]) * sign
        part = pl.ds(n * per * 16, per * 16)
        copies.append(pltpu.make_async_copy(rows.at[part], gap.at[part], sems.at[n]))
        copies[-1].start()
    for copy in copies:
        copy.wait()


def per_device(panels, courant, direction, decay, booster, feeder, face_index):
    pipes = panels.shape[1]
    columns = panels.shape[3]
    faces = face_index.shape[0]
    blocks = pipes // LANES
    domains = lax.axis_size("dom")
    f32, i32 = jnp.float32, jnp.int32
    cells_in = panels.reshape(pipes * SEGF, columns)
    rates_in = courant.reshape(pipes * GROUPS, columns)
    dirs = direction.transpose(1, 2, 0).reshape(GROUPS * blocks, LANES)
    feed = feeder.reshape(blocks, LANES, 2).transpose(0, 2, 1).reshape(2 * blocks, LANES)
    ghost_rows = GROUPS * (pipes + 2 * faces) + 8

    cells, rates, outflow, factor, boosts, flow_back, words, face_rows = pl.pallas_call(
        load_kernel,
        name="load_step",
        in_specs=[HBM] * 7,
        out_specs=[VMEM] * 8,
        out_shape=[
            pltpu.VMEM((pipes * SEGF, columns), f32),
            pltpu.VMEM((pipes * GROUPS, columns), f32),
            pltpu.VMEM((ghost_rows, columns), f32),
            pltpu.VMEM((pipes, columns), f32),
            pltpu.VMEM((pipes, columns), f32),
            pltpu.VMEM((GROUPS * pipes, columns), f32),
            jax.ShapeDtypeStruct((blocks, LANES), i32),
            pltpu.VMEM((faces * GROUPS, columns), f32),
        ],
        scratch_shapes=[
            pltpu.VMEM(dirs.shape, i32),
            pltpu.VMEM(feed.shape, i32),
            pltpu.VMEM((blocks, LANES), f32),
            pltpu.VMEM((blocks, LANES), f32),
            pltpu.SMEM((faces,), i32),
            pltpu.SemaphoreType.DMA((CHUNKS,)),
            pltpu.SemaphoreType.DMA(()),
            pltpu.SemaphoreType.DMA((5,)),
        ],
        compiler_params=params(),
        cost_estimate=cost(5 << 20),
    )(
        *pinned(
            pltpu.HBM, cells_in, rates_in, dirs, feed,
            decay.reshape(blocks, LANES), booster.reshape(blocks, LANES), face_index,
        )
    )

    near_pairs = [(i, i ^ 1) for i in range(domains) if i ^ 1 < domains]
    far_pairs = [(i, i + 1) for i in range(1, domains - 1, 2)]
    far_pairs = far_pairs + [(j, i) for i, j in far_pairs]
    near_rows = lax.ppermute(face_rows, "dom", near_pairs)
    far_rows = lax.ppermute(face_rows, "dom", far_pairs)

    new, out, kept, kept_mid, sent_mid, sent, ghosts = pl.pallas_call(
        step_kernel,
        name="advance_step",
        in_specs=[SMEM] + [VMEM] * 6,
        out_specs=[VMEM, HBM] + [VMEM] * 4 + [SMEM],
        out_shape=[
            pltpu.VMEM((pipes * SEGF, columns), f32),
            jax.ShapeDtypeStruct((pipes * SEGF, columns), f32),
            *[pltpu.VMEM((pipes, columns), f32)] * 4,
            pltpu.SMEM((pipes + 8,), i32),
        ],
        scratch_shapes=[pltpu.VMEM((GROUPS * pipes, columns), f32)] * 2
        + [pltpu.SemaphoreType.DMA((8,))],
        compiler_params=params(),
        cost_estimate=cost(20 << 20),
    )(words, cells, rates, outflow, factor, boosts, flow_back)

    swap = [(0, 1), (1, 0)]
    partner_mid = lax.ppermute(sent_mid, "level", swap)
    first = GROUPS * pipes
    outflow = pl.pallas_call(
        lambda *refs: arrive_kernel(first, True, *refs),
        name="near_arrive",
        in_specs=[VMEM] * 2,
        out_specs=VMEM,
        out_shape=pltpu.VMEM((ghost_rows, columns), f32),
        input_output_aliases={1: 0},
        compiler_params=params(),
        cost_estimate=cost(1 << 19),
    )(near_rows, outflow)

    outflow, sent, new, kept = pl.pallas_call(
        lambda *refs: send_kernel(first, *refs),
        name="ghost_send",
        in_specs=[SMEM] + [VMEM] * 8,
        out_specs=[VMEM] * 4,
        out_shape=[
            pltpu.VMEM((ghost_rows, columns), f32),
            pltpu.VMEM((pipes, columns), f32),
            pltpu.VMEM((pipes * SEGF, columns), f32),
            pltpu.VMEM((pipes, columns), f32),
        ],
        input_output_aliases={5: 0, 6: 1, 7: 2, 8: 3},
        compiler_params=params(),
        cost_estimate=cost(1 << 20),
    )(ghosts, far_rows, rates, factor, flow_back, outflow, sent, new, kept)

    partner = lax.ppermute(sent, "level", swap)

    new, kept, out, gap_rows = pl.pallas_call(
        fix_kernel,
        name="ghost_fix",
        in_specs=[SMEM] + [VMEM] * 7 + [HBM],
        out_specs=[VMEM, VMEM, HBM, VMEM],
        out_shape=[
            pltpu.VMEM((pipes * SEGF, columns), f32),
            pltpu.VMEM((pipes, columns), f32),
            jax.ShapeDtypeStruct((pipes * SEGF, columns), f32),
            pltpu.VMEM((pipes * 2, columns), f32),
        ],
        scratch_shapes=[pltpu.SemaphoreType.DMA(())],
        input_output_aliases={6: 0, 7: 1, 8: 2},
        compiler_params=params(),
        cost_estimate=cost(4 << 20),
    )(
        ghosts, rates, factor, outflow, kept_mid, partner_mid, new, kept,
        *pinned(pltpu.HBM, out),
    )

    _, gap = pl.pallas_call(
        gap_kernel,
        name="level_gap",
        in_specs=[VMEM] * 3,
        out_specs=[VMEM, HBM],
        out_shape=[
            pltpu.VMEM((pipes * 2, columns), f32),
            jax.ShapeDtypeStruct((pipes * 2, columns), f32),
        ],
        scratch_shapes=[pltpu.SemaphoreType.DMA((2,))],
        input_output_aliases={2: 0},
        compiler_params=params(),
        cost_estimate=cost(1 << 20),
    )(kept, partner, gap_rows)
    return (out.reshape(1, pipes, SEGF, columns), gap.reshape(pipes, 2, columns))


def solution(mesh):
    in_specs = (
        P("level", "dom", None, "samp"),
        P("dom", None, "samp"),
        P("dom", None, "samp"),
        P("dom"),
        P("dom"),
        P("dom", None),
        P("dom"),
    )
    out_specs = (P("level", "dom", None, "samp"), P("dom", "level", "samp"))
    return jax.shard_map(
        per_device, mesh=mesh, in_specs=in_specs, out_specs=out_specs, check_vma=False
    )
```

```python
import jax
import jax.numpy as jnp
from jax import lax
from jax.experimental import pallas as pl
from jax.experimental.pallas import tpu as pltpu
from jax.sharding import PartitionSpec as P

SEGF = 16
SEGC = 4
GROUPS = SEGF // SEGC
LANES = 128
CHUNKS = 4
MARK = -(1 << 31)

HBM = pl.BlockSpec(memory_space=pltpu.HBM)
VMEM = pl.BlockSpec(memory_space=pltpu.VMEM)
SMEM = pl.BlockSpec(memory_space=pltpu.SMEM)


def params():
    return pltpu.CompilerParams(vmem_limit_bytes=8 << 20)


def cost(nbytes):
    return pl.CostEstimate(flops=0, bytes_accessed=nbytes, transcendentals=0)


def pinned(space, *arrays):
    return [pltpu.with_memory_space_constraint(x, space) for x in arrays]


def down_rows(row):
    return jnp.broadcast_to(row, (LANES, LANES)).T


def spread(ref, row):
    return ref[pl.ds(row, 8, stride=0), :]


def load_kernel(
    panel, rate, dirs, feed, decay, boost, faces,
    cells, rates, outflow, factor, boosts, flow_back, words, face_rows,
    dir_v, feed_v, decay_v, boost_v, face_s, panel_sem, rate_sem, small_sem,
):
    rows = panel.shape[0] // CHUNKS
    blocks = decay.shape[0]
    pipes = blocks * LANES
    level = lax.axis_index("level")

    def chunk(n):
        part = pl.ds(pl.multiple_of(n * rows, rows), rows)
        return pltpu.make_async_copy(panel.at[part], cells.at[part], panel_sem.at[n])

    small = [
        pltpu.make_async_copy(src, dst, small_sem.at[n])
        for n, (src, dst) in enumerate(
            ((dirs, dir_v), (feed, feed_v), (decay, decay_v), (boost, boost_v), (faces, face_s))
        )
    ]
    rate_copy = pltpu.make_async_copy(rate, rates, rate_sem)
    for copy in small:
        copy.start()

    @pl.when(level == 0)
    def _():
        rate_copy.start()

    for n in range(CHUNKS):
        chunk(n).start(priority=1)
    for copy in small:
        copy.wait()

    scale = jnp.where(level == 0, jnp.float32(-0.25), jnp.float32(-1.0))
    fac = jnp.exp(decay_v[...] * scale)
    for b in range(blocks):
        own = slice(b * LANES, (b + 1) * LANES)
        factor[own, :] = down_rows(fac[b : b + 1])
        boosts[own, :] = down_rows(boost_v[b : b + 1])
    outflow[GROUPS * pipes :, :] = jnp.zeros_like(outflow[GROUPS * pipes :, :])
    back = (dir_v[...] == 1).astype(jnp.int32)
    lane = lax.broadcasted_iota(jnp.int32, (1, LANES), 1)
    for b in range(blocks):
        ahead = feed_v[2 * b : 2 * b + 1, :]
        behind = feed_v[2 * b + 1 : 2 * b + 2, :]
        rev = back[b : b + 1, :]
        src = jnp.where(rev == 1, behind, ahead)
        p = lane + b * LANES
        fine = src + (p << 10) + (rev << 20) + jnp.where(src >= pipes, MARK, 0)
        revs = [back[g * blocks + b : g * blocks + b + 1, :] for g in range(GROUPS)]
        most = jnp.maximum(jnp.maximum(revs[0], revs[1]), jnp.maximum(revs[2], revs[3]))
        least = jnp.minimum(jnp.minimum(revs[0], revs[1]), jnp.minimum(revs[2], revs[3]))
        fed = jnp.maximum(ahead * (1 - least), behind * most) >= pipes
        coarse = ahead + (behind << 10) + (p << 20) + jnp.where(fed, MARK, 0)
        words[b : b + 1, :] = jnp.where(level == 0, fine, coarse)
    backf = back.astype(jnp.float32)

    def back_rows(g):
        for b in range(blocks):
            at = g * blocks + b
            flow_back[at * LANES : (at + 1) * LANES, :] = down_rows(backf[at : at + 1])

    back_rows(0)

    @pl.when(level == 1)
    def _():
        for g in range(1, GROUPS):
            back_rows(g)

    per_chunk = pipes // 8 // CHUNKS

    @pl.when(level == 0)
    def _():
        rate_copy.wait()

        @pl.loop(0, CHUNKS)
        def _(n):
            chunk(n).wait()
            for i in range(per_chunk):
                q = n * per_chunk + i
                base = pl.multiple_of(q * 128, 128)
                own = pl.ds(pl.multiple_of(q * 8, 8), 8)
                rev = flow_back[own, :] != 0.0
                b = factor[own, :] * rates[pl.ds(pl.multiple_of(q * 32, 32), 8, stride=4), :]
                a = factor[own, :] - b
                y = [
                    jnp.where(
                        rev,
                        cells[pl.ds(base + j, 8, stride=16), :],
                        cells[pl.ds(base + 15 - j, 8, stride=16), :],
                    )
                    for j in range(GROUPS)
                ]
                for s in range(GROUPS):
                    outflow[pl.ds(pl.multiple_of(q * 32, 32) + s, 8, stride=4), :] = y[0]
                    y = [a * y[j] + b * y[j + 1] for j in range(len(y) - 1)]

    @pl.when(level == 1)
    def _():
        @pl.loop(0, CHUNKS)
        def _(n):
            chunk(n).wait()
            for i in range(per_chunk):
                q = n * per_chunk + i
                base = pl.multiple_of(q * 128, 128)
                for g in range(GROUPS):
                    rev = flow_back[pl.ds(pl.multiple_of(g * pipes + q * 8, 8), 8), :] != 0.0
                    outflow[pl.ds(pl.multiple_of(q * 32, 32) + g, 8, stride=4), :] = jnp.where(
                        rev,
                        cells[pl.ds(base + 4 * g, 8, stride=16), :],
                        cells[pl.ds(base + 4 * g + 3, 8, stride=16), :],
                    )

    @pl.loop(0, faces.shape[0] // 16)
    def _(m):
        moved = [
            outflow[pl.ds(pl.multiple_of(face_s[m * 16 + u] * 4, 4), 4), :] for u in range(16)
        ]
        for u in range(16):
            face_rows[pl.ds(pl.multiple_of(m * 64, 64) + 4 * u, 4), :] = moved[u]


def eight_words(q, words):
    per = LANES // 8
    return [words[q // per, (q % per) * 8 + u] for u in range(8)]


def gather_eight(fine, q, words, outflow, ahead_in, behind_in):
    start = pl.multiple_of(q * 32, 32)
    entries = eight_words(q, words)
    moved = [[outflow[pl.ds(pl.multiple_of((w & 1023) * 4, 4), 4), :] for w in entries]]
    if not fine:
        moved.append(
            [outflow[pl.ds(pl.multiple_of((w >> 10 & 1023) * 4, 4), 4), :] for w in entries]
        )
    for dest, tiles in zip((ahead_in, behind_in), moved):
        for u in range(8):
            dest[pl.ds(start + 4 * u, 4), :] = tiles[u]


def list_eight(q, words, ghosts, count):
    for w in eight_words(q, words):
        ghosts[count] = w
        count = count + lax.shift_right_logical(w, 31)
    return count


def fine_block(q, cells, rates, factor, boosts, flow_back, ahead_in, new, shares):
    kept, kept_mid, sent_mid, sent = shares
    own = pl.ds(pl.multiple_of(q * 8, 8), 8)
    base = pl.multiple_of(q * 128, 128)
    quad = pl.multiple_of(q * 32, 32)
    rev = flow_back[own, :] != 0.0
    f = factor[own, :]
    b = f * rates[pl.ds(quad, 8, stride=4), :]
    a = f - b
    bo = boosts[own, :]
    x = [cells[pl.ds(base + k, 8, stride=16), :] for k in range(SEGF)]
    o = [jnp.where(rev, x[SEGF - 1 - k], x[k]) for k in range(SEGF)]
    for s in range(GROUPS):
        inflow = ahead_in[pl.ds(quad + s, 8, stride=4), :] + bo
        o = [a * o[k] + b * (o[k - 1] if k else inflow) for k in range(SEGF)]
    y = [jnp.where(rev, o[SEGF - 1 - k], o[k]) for k in range(SEGF)]
    for k in range(SEGF):
        new[pl.ds(base + k, 8, stride=16), :] = y[k]
    for k, dest in enumerate((kept, kept_mid, sent_mid, sent)):
        dest[own, :] = ((y[4 * k] + y[4 * k + 1]) + (y[4 * k + 2] + y[4 * k + 3])) * 0.25


def coarse_block(
    q, cells, rates, factor, boosts, flow_back, ahead_in, behind_in, new, shares
):
    kept, kept_mid, sent_mid, sent = shares
    pipes = factor.shape[0]
    own = pl.ds(pl.multiple_of(q * 8, 8), 8)
    base = pl.multiple_of(q * 128, 128)
    quad = pl.multiple_of(q * 32, 32)
    f = factor[own, :]
    bo = boosts[own, :]
    for g in range(GROUPS):
        rev = flow_back[pl.ds(pl.multiple_of(g * pipes + q * 8, 8), 8), :] != 0.0
        four = pl.ds(quad + g, 8, stride=4)
        b = f * rates[four, :]
        a = f - b
        inflow = jnp.where(rev, behind_in[four, :], ahead_in[four, :]) + bo
        x = [cells[pl.ds(base + 4 * g + k, 8, stride=16), :] for k in range(SEGC)]
        up = [
            jnp.where(
                rev, x[k + 1] if k + 1 < SEGC else inflow, x[k - 1] if k else inflow
            )
            for k in range(SEGC)
        ]
        y = [a * x[k] + b * up[k] for k in range(SEGC)]
        for k in range(SEGC):
            new[pl.ds(base + 4 * g + k, 8, stride=16), :] = y[k]
            if g == 0:
                (sent, sent_mid, kept_mid, kept)[k][own, :] = y[k]


def step_kernel(
    words, rate, cells, rates_in, outflow, factor, boosts, flow_back,
    new, out, kept, kept_mid, sent_mid, sent, ghosts, rates,
    ahead_in, behind_in, sems, rate_sems,
):
    shares = (kept, kept_mid, sent_mid, sent)
    level = lax.axis_index("level")
    eights = factor.shape[0] // 8
    parts = sems.shape[0]
    rows = new.shape[0] // parts

    def written(n):
        part = pl.ds(pl.multiple_of(n * rows, rows), rows)
        return pltpu.make_async_copy(new.at[part], out.at[part], sems.at[n])

    rate_rows = rates.shape[0] // parts

    def fetched(n):
        part = pl.ds(pl.multiple_of(n * rate_rows, rate_rows), rate_rows)
        return pltpu.make_async_copy(rate.at[part], rates.at[part], rate_sems.at[n])

    def run(fine):
        if not fine:
            for n in range(parts):
                fetched(n).start()
        gather_eight(fine, 0, words, outflow, ahead_in, behind_in)

        def some(q, count):
            if fine:
                fine_block(q, cells, rates, factor, boosts, flow_back, ahead_in, new, shares)
            else:
                coarse_block(
                    q, cells, rates, factor, boosts, flow_back, ahead_in, behind_in,
                    new, shares,
                )
            later = jnp.minimum(q + 1, eights - 1)
            gather_eight(fine, later, words, outflow, ahead_in, behind_in)
            return list_eight(q, words, ghosts, count)

        per = eights // parts

        def part(n, count):
            if not fine:
                fetched(n).wait()
            count = lax.fori_loop(n * per, (n + 1) * per, some, count)
            written(n).start()
            return count

        ghosts[8 * eights] = lax.fori_loop(0, parts, part, jnp.int32(0))

    @pl.when(level == 0)
    def _():
        run(True)

    @pl.when(level == 1)
    def _():
        run(False)

    for n in range(parts):
        written(n).wait()


def arrive_kernel(first, near, arrived, outflow_in, outflow):
    odd = lax.axis_index("dom") % 2
    half = arrived.shape[0]
    slot = 1 - odd if near else odd
    start = pl.multiple_of(first + slot * half, 8)
    outflow[pl.ds(start, half), :] = arrived[...]


def over_list(count, ghosts, width, each):
    whole = count // width

    @pl.loop(0, whole)
    def _(m):
        each([ghosts[m * width + u] for u in range(width)])

    @pl.loop(whole * width, count)
    def _(i):
        each([ghosts[i]])


def send_kernel(
    first, ghosts, arrived, rates, factor, flow_back,
    outflow_in, sent_in, new_in, kept_in, outflow, sent, new, kept,
):
    pipes = factor.shape[0]
    level = lax.axis_index("level")
    arrive_kernel(first, False, arrived, outflow_in, outflow)

    def fine(entries):
        done = []
        for w in entries:
            src, p, rev = w & 1023, w >> 10 & 1023, w >> 20 & 1
            own = pl.ds(p, 1)
            rows = outflow[pl.ds(pl.multiple_of(src * 4, 4), 4), :]
            f, r = factor[own, :], rates[pl.ds(p * 4, 1), :]
            total = rows[0:1]
            for s in range(1, GROUPS):
                total = f * total + rows[s : s + 1]
            back = jnp.where(rev == 1, jnp.float32(0.25), jnp.float32(0.0))
            done.append((own, sent[own, :] + f * r * total * back))
        for own, row in done:
            sent[own, :] = row

    def coarse(entries):
        coarse_fix(entries, rates, factor, flow_back, outflow, new, kept, sent)

    @pl.when(level == 0)
    def _():
        over_list(ghosts[pipes], ghosts, 8, fine)

    @pl.when(level == 1)
    def _():
        over_list(ghosts[pipes], ghosts, 4, coarse)


def fine_fix(entries, rates, factor, outflow, new, kept):
    row = lax.broadcasted_iota(jnp.int32, (8, LANES), 0)
    loaded = []
    for w in entries:
        src, p, rev = w & 1023, w >> 10 & 1023, w >> 20 & 1
        near = pl.ds(pl.multiple_of(p * 16 + 8 * rev, 8), 8)
        own = pl.ds(p, 1)
        inflow = [spread(outflow, src * 4 + s) for s in range(GROUPS)]
        loaded.append((
            rev, near, own, spread(factor, p), spread(rates, p * 4), inflow,
            new[near, :], kept[own, :],
        ))
    done = []
    for rev, near, own, f, r, inflow, tile, kept_row in loaded:
        b = f * r
        a = f - b
        edge = row == 7 * rev
        shift = 1 + 6 * rev
        total = b * inflow[0]
        delta = jnp.where(edge, total, 0.0)
        for s in range(1, GROUPS):
            up = jnp.where(edge, inflow[s], pltpu.roll(delta, shift, 0))
            delta = a * delta + b * up
            total = f * total + b * inflow[s]
        ahead = jnp.where(rev == 1, jnp.float32(0.0), jnp.float32(0.25))
        done.append((near, own, tile + delta, kept_row + total[0:1] * ahead))
    for near, own, tile, kept_row in done:
        new[near, :] = tile
        kept[own, :] = kept_row


def coarse_fix(entries, rates, factor, flow_back, outflow, new, kept, sent):
    pipes = factor.shape[0]
    zeros = outflow.shape[0] - 8
    loaded = []
    for w in entries:
        p = w >> 20 & 1023
        rows = []
        for src in (w & 1023, w >> 10 & 1023):
            at = jnp.where(src >= pipes, src * 4, zeros)
            rows.append(outflow[pl.ds(pl.multiple_of(at, 4), 4), :])
        low = pl.ds(p * 16, 4, stride=4)
        high = pl.ds(p * 16 + 3, 4, stride=4)
        loaded.append((
            p, low, high, rows, flow_back[pl.ds(p, 4, stride=pipes), :],
            rates[pl.ds(pl.multiple_of(p * 4, 4), 4), :], factor[pl.ds(p, 4, stride=0), :],
            new[low, :], new[high, :],
        ))
    done = []
    for p, low, high, rows, rev, r, f, first_rows, last_rows in loaded:
        turned = rev != 0.0
        delta = f * r * jnp.where(turned, rows[1], rows[0])
        done.append((
            p, low, high,
            first_rows + jnp.where(turned, 0.0, delta), last_rows + jnp.where(turned, delta, 0.0),
        ))
    for p, low, high, first_rows, last_rows in done:
        new[low, :] = first_rows
        new[high, :] = last_rows
        kept[pl.ds(p, 1), :] = last_rows[0:1]
        sent[pl.ds(p, 1), :] = first_rows[0:1]


def fix_kernel(
    ghosts, rates, factor, outflow, kept_mid, partner_mid, new_in, kept_in, out_in,
    new, kept, out, gap_rows, sem,
):
    pipes = factor.shape[0]
    level = lax.axis_index("level")
    shift = jnp.where(level == 0, 10, 20)
    count = ghosts[pipes]

    def write(entries):
        for w in entries:
            p = lax.shift_right_logical(w, shift) & 1023
            part = pl.ds(pl.multiple_of(p * SEGF, SEGF), SEGF)
            pltpu.make_async_copy(new.at[part], out.at[part], sem).start()

    def fine(entries):
        fine_fix(entries, rates, factor, outflow, new, kept)
        write(entries)

    @pl.when(level == 0)
    def _():
        over_list(count, ghosts, 4, fine)

    @pl.when(level == 1)
    def _():
        over_list(count, ghosts, 8, write)

    sign = jnp.where(level == 0, jnp.float32(1.0), jnp.float32(-1.0))

    @pl.loop(0, pipes // 64)
    def _(m):
        for u in range(8):
            own = pl.ds(pl.multiple_of(m * 64 + 8 * u, 8), 8)
            spots = pl.ds(pl.multiple_of(m * 128, 128) + 16 * u + 1 - level, 8, stride=2)
            gap_rows[spots, :] = (kept_mid[own, :] - partner_mid[own, :]) * sign

    def wait(some):
        part = pl.ds(0, SEGF * some)
        pltpu.make_async_copy(new.at[part], out.at[part], sem).wait()

    whole = count // 8

    @pl.loop(0, whole)
    def _(m):
        wait(8)

    @pl.loop(whole * 8, count)
    def _(i):
        wait(1)


def gap_kernel(kept, partner, rows_in, rows, gap, sems):
    level = lax.axis_index("level")
    sign = jnp.where(level == 0, jnp.float32(1.0), jnp.float32(-1.0))
    parts = sems.shape[0]
    copies = []
    per = kept.shape[0] // 8 // parts
    for n in range(parts):
        for q in range(n * per, (n + 1) * per):
            own = pl.ds(8 * q, 8)
            rows[pl.ds(16 * q + level, 8, stride=2), :] = (kept[own, :] - partner[own, :]) * sign
        part = pl.ds(n * per * 16, per * 16)
        copies.append(pltpu.make_async_copy(rows.at[part], gap.at[part], sems.at[n]))
        copies[-1].start()
    for copy in copies:
        copy.wait()


def per_device(panels, courant, direction, decay, booster, feeder, face_index):
    pipes = panels.shape[1]
    columns = panels.shape[3]
    faces = face_index.shape[0]
    blocks = pipes // LANES
    domains = lax.axis_size("dom")
    f32, i32 = jnp.float32, jnp.int32
    cells_in = panels.reshape(pipes * SEGF, columns)
    rates_in = courant.reshape(pipes * GROUPS, columns)
    dirs = direction.transpose(1, 2, 0).reshape(GROUPS * blocks, LANES)
    feed = feeder.reshape(blocks, LANES, 2).transpose(0, 2, 1).reshape(2 * blocks, LANES)
    ghost_rows = GROUPS * (pipes + 2 * faces) + 8

    cells_in, rates_in, dirs, feed, decay, booster, face_index = pinned(
        pltpu.HBM, cells_in, rates_in, dirs, feed,
        decay.reshape(blocks, LANES), booster.reshape(blocks, LANES), face_index,
    )
    cells, rates, outflow, factor, boosts, flow_back, words, face_rows = pl.pallas_call(
        load_kernel,
        name="load_step",
        in_specs=[HBM] * 7,
        out_specs=[VMEM] * 8,
        out_shape=[
            pltpu.VMEM((pipes * SEGF, columns), f32),
            pltpu.VMEM((pipes * GROUPS, columns), f32),
            pltpu.VMEM((ghost_rows, columns), f32),
            pltpu.VMEM((pipes, columns), f32),
            pltpu.VMEM((pipes, columns), f32),
            pltpu.VMEM((GROUPS * pipes, columns), f32),
            jax.ShapeDtypeStruct((blocks, LANES), i32),
            pltpu.VMEM((faces * GROUPS, columns), f32),
        ],
        scratch_shapes=[
            pltpu.VMEM(dirs.shape, i32),
            pltpu.VMEM(feed.shape, i32),
            pltpu.VMEM((blocks, LANES), f32),
            pltpu.VMEM((blocks, LANES), f32),
            pltpu.SMEM((faces,), i32),
            pltpu.SemaphoreType.DMA((CHUNKS,)),
            pltpu.SemaphoreType.DMA(()),
            pltpu.SemaphoreType.DMA((5,)),
        ],
        compiler_params=params(),
        cost_estimate=cost(5 << 20),
    )(cells_in, rates_in, dirs, feed, decay, booster, face_index)

    near_pairs = [(i, i ^ 1) for i in range(domains) if i ^ 1 < domains]
    far_pairs = [(i, i + 1) for i in range(1, domains - 1, 2)]
    far_pairs = far_pairs + [(j, i) for i, j in far_pairs]
    near_rows = lax.ppermute(face_rows, "dom", near_pairs)
    far_rows = lax.ppermute(face_rows, "dom", far_pairs)

    new, out, kept, kept_mid, sent_mid, sent, ghosts, rates = pl.pallas_call(
        step_kernel,
        name="advance_step",
        in_specs=[SMEM, HBM] + [VMEM] * 6,
        out_specs=[VMEM, HBM] + [VMEM] * 4 + [SMEM, VMEM],
        out_shape=[
            pltpu.VMEM((pipes * SEGF, columns), f32),
            jax.ShapeDtypeStruct((pipes * SEGF, columns), f32),
            *[pltpu.VMEM((pipes, columns), f32)] * 4,
            pltpu.SMEM((pipes + 8,), i32),
            pltpu.VMEM((pipes * GROUPS, columns), f32),
        ],
        scratch_shapes=[pltpu.VMEM((GROUPS * pipes, columns), f32)] * 2
        + [pltpu.SemaphoreType.DMA((8,))] * 2,
        input_output_aliases={3: 7},
        compiler_params=params(),
        cost_estimate=cost(20 << 20),
    )(words, rates_in, cells, rates, outflow, factor, boosts, flow_back)

    swap = [(0, 1), (1, 0)]
    partner_mid = lax.ppermute(sent_mid, "level", swap)
    first = GROUPS * pipes
    outflow = pl.pallas_call(
        lambda *refs: arrive_kernel(first, True, *refs),
        name="near_arrive",
        in_specs=[VMEM] * 2,
        out_specs=VMEM,
        out_shape=pltpu.VMEM((ghost_rows, columns), f32),
        input_output_aliases={1: 0},
        compiler_params=params(),
        cost_estimate=cost(1 << 19),
    )(near_rows, outflow)

    outflow, sent, new, kept = pl.pallas_call(
        lambda *refs: send_kernel(first, *refs),
        name="ghost_send",
        in_specs=[SMEM] + [VMEM] * 8,
        out_specs=[VMEM] * 4,
        out_shape=[
            pltpu.VMEM((ghost_rows, columns), f32),
            pltpu.VMEM((pipes, columns), f32),
            pltpu.VMEM((pipes * SEGF, columns), f32),
            pltpu.VMEM((pipes, columns), f32),
        ],
        input_output_aliases={5: 0, 6: 1, 7: 2, 8: 3},
        compiler_params=params(),
        cost_estimate=cost(1 << 20),
    )(ghosts, far_rows, rates, factor, flow_back, outflow, sent, new, kept)

    partner = lax.ppermute(sent, "level", swap)

    new, kept, out, gap_rows = pl.pallas_call(
        fix_kernel,
        name="ghost_fix",
        in_specs=[SMEM] + [VMEM] * 7 + [HBM],
        out_specs=[VMEM, VMEM, HBM, VMEM],
        out_shape=[
            pltpu.VMEM((pipes * SEGF, columns), f32),
            pltpu.VMEM((pipes, columns), f32),
            jax.ShapeDtypeStruct((pipes * SEGF, columns), f32),
            pltpu.VMEM((pipes * 2, columns), f32),
        ],
        scratch_shapes=[pltpu.SemaphoreType.DMA(())],
        input_output_aliases={6: 0, 7: 1, 8: 2},
        compiler_params=params(),
        cost_estimate=cost(4 << 20),
    )(
        ghosts, rates, factor, outflow, kept_mid, partner_mid, new, kept,
        *pinned(pltpu.HBM, out),
    )

    _, gap = pl.pallas_call(
        gap_kernel,
        name="level_gap",
        in_specs=[VMEM] * 3,
        out_specs=[VMEM, HBM],
        out_shape=[
            pltpu.VMEM((pipes * 2, columns), f32),
            jax.ShapeDtypeStruct((pipes * 2, columns), f32),
        ],
        scratch_shapes=[pltpu.SemaphoreType.DMA((2,))],
        input_output_aliases={2: 0},
        compiler_params=params(),
        cost_estimate=cost(1 << 20),
    )(kept, partner, gap_rows)
    return (out.reshape(1, pipes, SEGF, columns), gap.reshape(pipes, 2, columns))


def solution(mesh):
    in_specs = (
        P("level", "dom", None, "samp"),
        P("dom", None, "samp"),
        P("dom", None, "samp"),
        P("dom"),
        P("dom"),
        P("dom", None),
        P("dom"),
    )
    out_specs = (P("level", "dom", None, "samp"), P("dom", "level", "samp"))
    return jax.shard_map(
        per_device, mesh=mesh, in_specs=in_specs, out_specs=out_specs, check_vma=False
    )
```

```python
import jax
import jax.numpy as jnp
from jax import lax
from jax.experimental import pallas as pl
from jax.experimental.pallas import tpu as pltpu
from jax.sharding import PartitionSpec as P

SEGF = 16
SEGC = 4
GROUPS = SEGF // SEGC
LANES = 128
CHUNKS = 8
MARK = -(1 << 31)

HBM = pl.BlockSpec(memory_space=pltpu.HBM)
VMEM = pl.BlockSpec(memory_space=pltpu.VMEM)
SMEM = pl.BlockSpec(memory_space=pltpu.SMEM)


def params():
    return pltpu.CompilerParams(vmem_limit_bytes=8 << 20)


def cost(nbytes):
    return pl.CostEstimate(flops=0, bytes_accessed=nbytes, transcendentals=0)


def pinned(space, *arrays):
    return [pltpu.with_memory_space_constraint(x, space) for x in arrays]


def down_rows(row):
    return jnp.broadcast_to(row, (LANES, LANES)).T


def spread(ref, row):
    return jnp.broadcast_to(ref[pl.ds(row, 1), :], (8, LANES))


def load_kernel(
    panel, rate, dirs, feed, decay, boost, faces,
    cells, rates, outflow, factor, boosts, flow_back, words, face_rows,
    dir_v, feed_v, decay_v, boost_v, face_s, panel_sem, rate_sem, small_sem,
):
    rows = panel.shape[0] // CHUNKS
    blocks = decay.shape[0]
    pipes = blocks * LANES
    level = lax.axis_index("level")

    def chunk(n):
        part = pl.ds(pl.multiple_of(n * rows, rows), rows)
        return pltpu.make_async_copy(panel.at[part], cells.at[part], panel_sem.at[n])

    small = [
        pltpu.make_async_copy(src, dst, small_sem.at[n])
        for n, (src, dst) in enumerate(
            ((dirs, dir_v), (feed, feed_v), (decay, decay_v), (boost, boost_v), (faces, face_s))
        )
    ]
    rate_copy = pltpu.make_async_copy(rate, rates, rate_sem)
    for copy in small:
        copy.start()

    @pl.when(level == 0)
    def _():
        rate_copy.start()

    for n in range(CHUNKS):
        chunk(n).start(priority=1)
    for copy in small:
        copy.wait()

    scale = jnp.where(level == 0, jnp.float32(-0.25), jnp.float32(-1.0))
    fac = jnp.exp(decay_v[...] * scale)
    for b in range(blocks):
        own = slice(b * LANES, (b + 1) * LANES)
        factor[own, :] = down_rows(fac[b : b + 1])
        boosts[own, :] = down_rows(boost_v[b : b + 1])
    outflow[GROUPS * pipes :, :] = jnp.zeros_like(outflow[GROUPS * pipes :, :])
    back = (dir_v[...] == 1).astype(jnp.int32)
    lane = lax.broadcasted_iota(jnp.int32, (1, LANES), 1)
    for b in range(blocks):
        ahead = feed_v[2 * b : 2 * b + 1, :]
        behind = feed_v[2 * b + 1 : 2 * b + 2, :]
        rev = back[b : b + 1, :]
        src = jnp.where(rev == 1, behind, ahead)
        p = lane + b * LANES
        fine = src + (p << 10) + (rev << 20) + jnp.where(src >= pipes, MARK, 0)
        revs = [back[g * blocks + b : g * blocks + b + 1, :] for g in range(GROUPS)]
        most = jnp.maximum(jnp.maximum(revs[0], revs[1]), jnp.maximum(revs[2], revs[3]))
        least = jnp.minimum(jnp.minimum(revs[0], revs[1]), jnp.minimum(revs[2], revs[3]))
        fed = jnp.maximum(ahead * (1 - least), behind * most) >= pipes
        coarse = ahead + (behind << 10) + (p << 20) + jnp.where(fed, MARK, 0)
        words[b : b + 1, :] = jnp.where(level == 0, fine, coarse)
    backf = back.astype(jnp.float32)

    def back_rows(g):
        for b in range(blocks):
            at = g * blocks + b
            flow_back[at * LANES : (at + 1) * LANES, :] = down_rows(backf[at : at + 1])

    back_rows(0)

    @pl.when(level == 1)
    def _():
        for g in range(1, GROUPS):
            back_rows(g)

    per_chunk = pipes // 8 // CHUNKS

    @pl.when(level == 0)
    def _():
        rate_copy.wait()

        @pl.loop(0, CHUNKS)
        def _(n):
            chunk(n).wait()
            for i in range(per_chunk):
                q = n * per_chunk + i
                base = pl.multiple_of(q * 128, 128)
                own = pl.ds(pl.multiple_of(q * 8, 8), 8)
                rev = flow_back[own, :] != 0.0
                b = factor[own, :] * rates[pl.ds(pl.multiple_of(q * 32, 32), 8, stride=4), :]
                a = factor[own, :] - b
                y = [
                    jnp.where(
                        rev,
                        cells[pl.ds(base + j, 8, stride=16), :],
                        cells[pl.ds(base + 15 - j, 8, stride=16), :],
                    )
                    for j in range(GROUPS)
                ]
                for s in range(GROUPS):
                    outflow[pl.ds(pl.multiple_of(q * 32, 32) + s, 8, stride=4), :] = y[0]
                    y = [a * y[j] + b * y[j + 1] for j in range(len(y) - 1)]

    @pl.when(level == 1)
    def _():
        @pl.loop(0, CHUNKS)
        def _(n):
            chunk(n).wait()
            for i in range(per_chunk):
                q = n * per_chunk + i
                base = pl.multiple_of(q * 128, 128)
                for g in range(GROUPS):
                    rev = flow_back[pl.ds(pl.multiple_of(g * pipes + q * 8, 8), 8), :] != 0.0
                    outflow[pl.ds(pl.multiple_of(q * 32, 32) + g, 8, stride=4), :] = jnp.where(
                        rev,
                        cells[pl.ds(base + 4 * g, 8, stride=16), :],
                        cells[pl.ds(base + 4 * g + 3, 8, stride=16), :],
                    )

    @pl.loop(0, faces.shape[0] // 16)
    def _(m):
        moved = [
            outflow[pl.ds(pl.multiple_of(face_s[m * 16 + u] * 4, 4), 4), :] for u in range(16)
        ]
        for u in range(16):
            face_rows[pl.ds(pl.multiple_of(m * 64, 64) + 4 * u, 4), :] = moved[u]


def eight_words(q, words):
    per = LANES // 8
    return [words[q // per, (q % per) * 8 + u] for u in range(8)]


def gather_eight(fine, q, words, outflow, ahead_in, behind_in):
    start = pl.multiple_of(q * 32, 32)
    entries = eight_words(q, words)
    moved = [[outflow[pl.ds(pl.multiple_of((w & 1023) * 4, 4), 4), :] for w in entries]]
    if not fine:
        moved.append(
            [outflow[pl.ds(pl.multiple_of((w >> 10 & 1023) * 4, 4), 4), :] for w in entries]
        )
    for dest, tiles in zip((ahead_in, behind_in), moved):
        for u in range(8):
            dest[pl.ds(start + 4 * u, 4), :] = tiles[u]


def list_eight(q, words, ghosts, count):
    for w in eight_words(q, words):
        ghosts[count] = w
        count = count + lax.shift_right_logical(w, 31)
    return count


def fine_block(q, cells, rates, factor, boosts, flow_back, ahead_in, new, shares):
    kept, kept_mid, sent_mid, sent = shares
    own = pl.ds(pl.multiple_of(q * 8, 8), 8)
    base = pl.multiple_of(q * 128, 128)
    quad = pl.multiple_of(q * 32, 32)
    rev = flow_back[own, :] != 0.0
    f = factor[own, :]
    b = f * rates[pl.ds(quad, 8, stride=4), :]
    a = f - b
    bo = boosts[own, :]
    x = [cells[pl.ds(base + k, 8, stride=16), :] for k in range(SEGF)]
    o = [jnp.where(rev, x[SEGF - 1 - k], x[k]) for k in range(SEGF)]
    for s in range(GROUPS):
        inflow = ahead_in[pl.ds(quad + s, 8, stride=4), :] + bo
        o = [a * o[k] + b * (o[k - 1] if k else inflow) for k in range(SEGF)]
    y = [jnp.where(rev, o[SEGF - 1 - k], o[k]) for k in range(SEGF)]
    for k in range(SEGF):
        new[pl.ds(base + k, 8, stride=16), :] = y[k]
    for k, dest in enumerate((kept, kept_mid, sent_mid, sent)):
        dest[own, :] = ((y[4 * k] + y[4 * k + 1]) + (y[4 * k + 2] + y[4 * k + 3])) * 0.25


def coarse_block(
    q, cells, rates, factor, boosts, flow_back, ahead_in, behind_in, new, shares
):
    kept, kept_mid, sent_mid, sent = shares
    pipes = factor.shape[0]
    own = pl.ds(pl.multiple_of(q * 8, 8), 8)
    base = pl.multiple_of(q * 128, 128)
    quad = pl.multiple_of(q * 32, 32)
    f = factor[own, :]
    bo = boosts[own, :]
    for g in range(GROUPS):
        rev = flow_back[pl.ds(pl.multiple_of(g * pipes + q * 8, 8), 8), :] != 0.0
        four = pl.ds(quad + g, 8, stride=4)
        b = f * rates[four, :]
        a = f - b
        inflow = jnp.where(rev, behind_in[four, :], ahead_in[four, :]) + bo
        x = [cells[pl.ds(base + 4 * g + k, 8, stride=16), :] for k in range(SEGC)]
        up = [
            jnp.where(
                rev, x[k + 1] if k + 1 < SEGC else inflow, x[k - 1] if k else inflow
            )
            for k in range(SEGC)
        ]
        y = [a * x[k] + b * up[k] for k in range(SEGC)]
        for k in range(SEGC):
            new[pl.ds(base + 4 * g + k, 8, stride=16), :] = y[k]
            if g == 0:
                (sent, sent_mid, kept_mid, kept)[k][own, :] = y[k]


def step_kernel(
    words, rate, cells, rates_in, outflow, factor, boosts, flow_back,
    new, out, kept, kept_mid, sent_mid, sent, ghosts, rates,
    ahead_in, behind_in, sems, rate_sems,
):
    shares = (kept, kept_mid, sent_mid, sent)
    level = lax.axis_index("level")
    eights = factor.shape[0] // 8
    parts = sems.shape[0]
    rows = new.shape[0] // parts

    def written(n):
        part = pl.ds(pl.multiple_of(n * rows, rows), rows)
        return pltpu.make_async_copy(new.at[part], out.at[part], sems.at[n])

    rate_rows = rates.shape[0] // parts

    def fetched(n):
        part = pl.ds(pl.multiple_of(n * rate_rows, rate_rows), rate_rows)
        return pltpu.make_async_copy(rate.at[part], rates.at[part], rate_sems.at[n])

    def run(fine):
        if not fine:
            for n in range(parts):
                fetched(n).start()
        gather_eight(fine, 0, words, outflow, ahead_in, behind_in)

        def some(q, count):
            if fine:
                fine_block(q, cells, rates, factor, boosts, flow_back, ahead_in, new, shares)
            else:
                coarse_block(
                    q, cells, rates, factor, boosts, flow_back, ahead_in, behind_in,
                    new, shares,
                )
            later = jnp.minimum(q + 1, eights - 1)
            gather_eight(fine, later, words, outflow, ahead_in, behind_in)
            return list_eight(q, words, ghosts, count)

        per = eights // parts

        def part(n, count):
            if not fine:
                fetched(n).wait()
            count = lax.fori_loop(n * per, (n + 1) * per, some, count)
            @pl.when(n < parts - 1)
            def _():
                written(n).start()

            return count

        ghosts[8 * eights] = lax.fori_loop(0, parts, part, jnp.int32(0))

    @pl.when(level == 0)
    def _():
        run(True)

    @pl.when(level == 1)
    def _():
        run(False)

    for n in range(parts - 1):
        written(n).wait()


def arrive_kernel(first, near, arrived, outflow_in, outflow):
    odd = lax.axis_index("dom") % 2
    half = arrived.shape[0]
    slot = 1 - odd if near else odd
    start = pl.multiple_of(first + slot * half, 8)
    outflow[pl.ds(start, half), :] = arrived[...]


def over_list(count, ghosts, width, each):
    whole = count // width

    @pl.loop(0, whole)
    def _(m):
        each([ghosts[m * width + u] for u in range(width)])

    @pl.loop(whole * width, count)
    def _(i):
        each([ghosts[i]])


def send_kernel(
    first, ghosts, arrived, rates, factor, flow_back,
    outflow_in, sent_in, new_in, kept_in, outflow, sent, new, kept,
):
    pipes = factor.shape[0]
    level = lax.axis_index("level")
    arrive_kernel(first, False, arrived, outflow_in, outflow)

    def fine(entries):
        done = []
        for w in entries:
            src, p, rev = w & 1023, w >> 10 & 1023, w >> 20 & 1
            own = pl.ds(p, 1)
            rows = outflow[pl.ds(pl.multiple_of(src * 4, 4), 4), :]
            f, r = factor[own, :], rates[pl.ds(p * 4, 1), :]
            total = rows[0:1]
            for s in range(1, GROUPS):
                total = f * total + rows[s : s + 1]
            back = jnp.where(rev == 1, jnp.float32(0.25), jnp.float32(0.0))
            done.append((own, sent[own, :] + f * r * total * back))
        for own, row in done:
            sent[own, :] = row

    def coarse(entries):
        coarse_fix(entries, rates, factor, flow_back, outflow, new, kept, sent)

    @pl.when(level == 0)
    def _():
        over_list(ghosts[pipes], ghosts, 8, fine)

    @pl.when(level == 1)
    def _():
        over_list(ghosts[pipes], ghosts, 4, coarse)


def fine_fix(entries, rates, factor, outflow, new, kept):
    row = lax.broadcasted_iota(jnp.int32, (8, LANES), 0)
    loaded = []
    for w in entries:
        src, p, rev = w & 1023, w >> 10 & 1023, w >> 20 & 1
        near = pl.ds(pl.multiple_of(p * 16 + 8 * rev, 8), 8)
        own = pl.ds(p, 1)
        inflow = [spread(outflow, src * 4 + s) for s in range(GROUPS)]
        loaded.append((
            rev, near, own, spread(factor, p), spread(rates, p * 4), inflow,
            new[near, :], kept[own, :],
        ))
    done = []
    for rev, near, own, f, r, inflow, tile, kept_row in loaded:
        b = f * r
        a = f - b
        edge = row == 7 * rev
        shift = 1 + 6 * rev
        total = b * inflow[0]
        delta = jnp.where(edge, total, 0.0)
        for s in range(1, GROUPS):
            up = jnp.where(edge, inflow[s], pltpu.roll(delta, shift, 0))
            delta = a * delta + b * up
            total = f * total + b * inflow[s]
        ahead = jnp.where(rev == 1, jnp.float32(0.0), jnp.float32(0.25))
        done.append((near, own, tile + delta, kept_row + total[0:1] * ahead))
    for near, own, tile, kept_row in done:
        new[near, :] = tile
        kept[own, :] = kept_row


def coarse_fix(entries, rates, factor, flow_back, outflow, new, kept, sent):
    pipes = factor.shape[0]
    zeros = outflow.shape[0] - 8
    loaded = []
    for w in entries:
        p = w >> 20 & 1023
        rows = []
        for src in (w & 1023, w >> 10 & 1023):
            at = jnp.where(src >= pipes, src * 4, zeros)
            rows.append(outflow[pl.ds(pl.multiple_of(at, 4), 4), :])
        low = pl.ds(p * 16, 4, stride=4)
        high = pl.ds(p * 16 + 3, 4, stride=4)
        loaded.append((
            p, low, high, rows, flow_back[pl.ds(p, 4, stride=pipes), :],
            rates[pl.ds(pl.multiple_of(p * 4, 4), 4), :], jnp.broadcast_to(factor[pl.ds(p, 1), :], (4, LANES)),
            new[low, :], new[high, :],
        ))
    done = []
    for p, low, high, rows, rev, r, f, first_rows, last_rows in loaded:
        turned = rev != 0.0
        delta = f * r * jnp.where(turned, rows[1], rows[0])
        done.append((
            p, low, high,
            first_rows + jnp.where(turned, 0.0, delta), last_rows + jnp.where(turned, delta, 0.0),
        ))
    for p, low, high, first_rows, last_rows in done:
        new[low, :] = first_rows
        new[high, :] = last_rows
        kept[pl.ds(p, 1), :] = last_rows[0:1]
        sent[pl.ds(p, 1), :] = first_rows[0:1]


def fix_kernel(
    ghosts, rates, factor, outflow, kept_mid, partner_mid, new_in, kept_in, out_in,
    new, kept, out, gap_rows, sem, tail_sem,
):
    pipes = factor.shape[0]
    level = lax.axis_index("level")
    shift = jnp.where(level == 0, 10, 20)
    count = ghosts[pipes]

    def write(entries):
        for w in entries:
            p = lax.shift_right_logical(w, shift) & 1023
            part = pl.ds(pl.multiple_of(p * SEGF, SEGF), SEGF)
            pltpu.make_async_copy(new.at[part], out.at[part], sem).start()

    def fine(entries):
        fine_fix(entries, rates, factor, outflow, new, kept)
        write(entries)

    @pl.when(level == 0)
    def _():
        over_list(count, ghosts, 4, fine)

    @pl.when(level == 1)
    def _():
        over_list(count, ghosts, 8, write)

    tail = pl.ds(pipes * SEGF // 8 * 7, pipes * SEGF // 8)
    last = pltpu.make_async_copy(new.at[tail], out.at[tail], tail_sem)
    last.start()
    sign = jnp.where(level == 0, jnp.float32(1.0), jnp.float32(-1.0))

    @pl.loop(0, pipes // 64)
    def _(m):
        for u in range(8):
            own = pl.ds(pl.multiple_of(m * 64 + 8 * u, 8), 8)
            spots = pl.ds(pl.multiple_of(m * 128, 128) + 16 * u + 1 - level, 8, stride=2)
            gap_rows[spots, :] = (kept_mid[own, :] - partner_mid[own, :]) * sign

    def wait(some):
        part = pl.ds(0, SEGF * some)
        pltpu.make_async_copy(new.at[part], out.at[part], sem).wait()

    whole = count // 8

    @pl.loop(0, whole)
    def _(m):
        wait(8)

    @pl.loop(whole * 8, count)
    def _(i):
        wait(1)

    last.wait()


def gap_kernel(kept, partner, rows_in, rows, gap, sems):
    level = lax.axis_index("level")
    sign = jnp.where(level == 0, jnp.float32(1.0), jnp.float32(-1.0))
    parts = sems.shape[0]
    copies = []
    per = kept.shape[0] // 8 // parts
    for n in range(parts):
        for q in range(n * per, (n + 1) * per):
            own = pl.ds(8 * q, 8)
            rows[pl.ds(16 * q + level, 8, stride=2), :] = (kept[own, :] - partner[own, :]) * sign
        part = pl.ds(n * per * 16, per * 16)
        copies.append(pltpu.make_async_copy(rows.at[part], gap.at[part], sems.at[n]))
        copies[-1].start()
    for copy in copies:
        copy.wait()


def per_device(panels, courant, direction, decay, booster, feeder, face_index):
    pipes = panels.shape[1]
    columns = panels.shape[3]
    faces = face_index.shape[0]
    blocks = pipes // LANES
    domains = lax.axis_size("dom")
    f32, i32 = jnp.float32, jnp.int32
    cells_in = panels.reshape(pipes * SEGF, columns)
    rates_in = courant.reshape(pipes * GROUPS, columns)
    dirs = direction.transpose(1, 2, 0).reshape(GROUPS * blocks, LANES)
    feed = feeder.reshape(blocks, LANES, 2).transpose(0, 2, 1).reshape(2 * blocks, LANES)
    ghost_rows = GROUPS * (pipes + 2 * faces) + 8

    cells_in, rates_in, dirs, feed, decay, booster, face_index = pinned(
        pltpu.HBM, cells_in, rates_in, dirs, feed,
        decay.reshape(blocks, LANES), booster.reshape(blocks, LANES), face_index,
    )
    cells, rates, outflow, factor, boosts, flow_back, words, face_rows = pl.pallas_call(
        load_kernel,
        name="load_step",
        in_specs=[HBM] * 7,
        out_specs=[VMEM] * 8,
        out_shape=[
            pltpu.VMEM((pipes * SEGF, columns), f32),
            pltpu.VMEM((pipes * GROUPS, columns), f32),
            pltpu.VMEM((ghost_rows, columns), f32),
            pltpu.VMEM((pipes, columns), f32),
            pltpu.VMEM((pipes, columns), f32),
            pltpu.VMEM((GROUPS * pipes, columns), f32),
            jax.ShapeDtypeStruct((blocks, LANES), i32),
            pltpu.VMEM((faces * GROUPS, columns), f32),
        ],
        scratch_shapes=[
            pltpu.VMEM(dirs.shape, i32),
            pltpu.VMEM(feed.shape, i32),
            pltpu.VMEM((blocks, LANES), f32),
            pltpu.VMEM((blocks, LANES), f32),
            pltpu.SMEM((faces,), i32),
            pltpu.SemaphoreType.DMA((CHUNKS,)),
            pltpu.SemaphoreType.DMA(()),
            pltpu.SemaphoreType.DMA((5,)),
        ],
        compiler_params=params(),
        cost_estimate=cost(5 << 20),
    )(cells_in, rates_in, dirs, feed, decay, booster, face_index)

    near_pairs = [(i, i ^ 1) for i in range(domains) if i ^ 1 < domains]
    far_pairs = [(i, i + 1) for i in range(1, domains - 1, 2)]
    far_pairs = far_pairs + [(j, i) for i, j in far_pairs]
    near_rows = lax.ppermute(face_rows, "dom", near_pairs)
    far_rows = lax.ppermute(face_rows, "dom", far_pairs)

    new, out, kept, kept_mid, sent_mid, sent, ghosts, rates = pl.pallas_call(
        step_kernel,
        name="advance_step",
        in_specs=[SMEM, HBM] + [VMEM] * 6,
        out_specs=[VMEM, HBM] + [VMEM] * 4 + [SMEM, VMEM],
        out_shape=[
            pltpu.VMEM((pipes * SEGF, columns), f32),
            jax.ShapeDtypeStruct((pipes * SEGF, columns), f32),
            *[pltpu.VMEM((pipes, columns), f32)] * 4,
            pltpu.SMEM((pipes + 8,), i32),
            pltpu.VMEM((pipes * GROUPS, columns), f32),
        ],
        scratch_shapes=[pltpu.VMEM((GROUPS * pipes, columns), f32)] * 2
        + [pltpu.SemaphoreType.DMA((8,))] * 2,
        input_output_aliases={3: 7},
        compiler_params=params(),
        cost_estimate=cost(20 << 20),
    )(words, rates_in, cells, rates, outflow, factor, boosts, flow_back)

    swap = [(0, 1), (1, 0)]
    partner_mid = lax.ppermute(sent_mid, "level", swap)
    first = GROUPS * pipes
    outflow = pl.pallas_call(
        lambda *refs: arrive_kernel(first, True, *refs),
        name="near_arrive",
        in_specs=[VMEM] * 2,
        out_specs=VMEM,
        out_shape=pltpu.VMEM((ghost_rows, columns), f32),
        input_output_aliases={1: 0},
        compiler_params=params(),
        cost_estimate=cost(1 << 19),
    )(near_rows, outflow)

    outflow, sent, new, kept = pl.pallas_call(
        lambda *refs: send_kernel(first, *refs),
        name="ghost_send",
        in_specs=[SMEM] + [VMEM] * 8,
        out_specs=[VMEM] * 4,
        out_shape=[
            pltpu.VMEM((ghost_rows, columns), f32),
            pltpu.VMEM((pipes, columns), f32),
            pltpu.VMEM((pipes * SEGF, columns), f32),
            pltpu.VMEM((pipes, columns), f32),
        ],
        input_output_aliases={5: 0, 6: 1, 7: 2, 8: 3},
        compiler_params=params(),
        cost_estimate=cost(1 << 20),
    )(ghosts, far_rows, rates, factor, flow_back, outflow, sent, new, kept)

    partner = lax.ppermute(sent, "level", swap)

    new, kept, out, gap_rows = pl.pallas_call(
        fix_kernel,
        name="ghost_fix",
        in_specs=[SMEM] + [VMEM] * 7 + [HBM],
        out_specs=[VMEM, VMEM, HBM, VMEM],
        out_shape=[
            pltpu.VMEM((pipes * SEGF, columns), f32),
            pltpu.VMEM((pipes, columns), f32),
            jax.ShapeDtypeStruct((pipes * SEGF, columns), f32),
            pltpu.VMEM((pipes * 2, columns), f32),
        ],
        scratch_shapes=[pltpu.SemaphoreType.DMA(())] * 2,
        input_output_aliases={6: 0, 7: 1, 8: 2},
        compiler_params=params(),
        cost_estimate=cost(4 << 20),
    )(
        ghosts, rates, factor, outflow, kept_mid, partner_mid, new, kept,
        *pinned(pltpu.HBM, out),
    )

    _, gap = pl.pallas_call(
        gap_kernel,
        name="level_gap",
        in_specs=[VMEM] * 3,
        out_specs=[VMEM, HBM],
        out_shape=[
            pltpu.VMEM((pipes * 2, columns), f32),
            jax.ShapeDtypeStruct((pipes * 2, columns), f32),
        ],
        scratch_shapes=[pltpu.SemaphoreType.DMA((2,))],
        input_output_aliases={2: 0},
        compiler_params=params(),
        cost_estimate=cost(1 << 20),
    )(kept, partner, gap_rows)
    return (out.reshape(1, pipes, SEGF, columns), gap.reshape(pipes, 2, columns))


def solution(mesh):
    in_specs = (
        P("level", "dom", None, "samp"),
        P("dom", None, "samp"),
        P("dom", None, "samp"),
        P("dom"),
        P("dom"),
        P("dom", None),
        P("dom"),
    )
    out_specs = (P("level", "dom", None, "samp"), P("dom", "level", "samp"))
    return jax.shard_map(
        per_device, mesh=mesh, in_specs=in_specs, out_specs=out_specs, check_vma=False
    )
```

```python
import jax
import jax.numpy as jnp
from jax import lax
from jax.experimental import pallas as pl
from jax.experimental.pallas import tpu as pltpu
from jax.sharding import PartitionSpec as P

SEGF = 16
SEGC = 4
GROUPS = SEGF // SEGC
LANES = 128
CHUNKS = 8
MARK = -(1 << 31)

HBM = pl.BlockSpec(memory_space=pltpu.HBM)
VMEM = pl.BlockSpec(memory_space=pltpu.VMEM)
SMEM = pl.BlockSpec(memory_space=pltpu.SMEM)


def params():
    return pltpu.CompilerParams(vmem_limit_bytes=8 << 20)


def cost(nbytes):
    return pl.CostEstimate(flops=0, bytes_accessed=nbytes, transcendentals=0)


def pinned(space, *arrays):
    return [pltpu.with_memory_space_constraint(x, space) for x in arrays]


def down_rows(row):
    return jnp.broadcast_to(row, (LANES, LANES)).T


def spread(ref, row):
    return jnp.broadcast_to(ref[pl.ds(row, 1), :], (8, LANES))


def load_kernel(
    panel, rate, dirs, feed, decay, boost, faces,
    cells, rates, outflow, factor, boosts, flow_back, words, face_rows,
    dir_v, feed_v, decay_v, boost_v, face_s, panel_sem, rate_sem, small_sem,
):
    rows = panel.shape[0] // CHUNKS
    blocks = decay.shape[0]
    pipes = blocks * LANES
    level = lax.axis_index("level")

    def chunk(n):
        part = pl.ds(pl.multiple_of(n * rows, rows), rows)
        return pltpu.make_async_copy(panel.at[part], cells.at[part], panel_sem.at[n])

    small = [
        pltpu.make_async_copy(src, dst, small_sem.at[n])
        for n, (src, dst) in enumerate(
            ((dirs, dir_v), (feed, feed_v), (decay, decay_v), (boost, boost_v), (faces, face_s))
        )
    ]
    rate_copy = pltpu.make_async_copy(rate, rates, rate_sem)
    for copy in small:
        copy.start()

    @pl.when(level == 0)
    def _():
        rate_copy.start()

    for n in range(CHUNKS):
        chunk(n).start(priority=1)
    for copy in small:
        copy.wait()

    scale = jnp.where(level == 0, jnp.float32(-0.25), jnp.float32(-1.0))
    fac = jnp.exp(decay_v[...] * scale)
    for b in range(blocks):
        own = slice(b * LANES, (b + 1) * LANES)
        factor[own, :] = down_rows(fac[b : b + 1])
        boosts[own, :] = down_rows(boost_v[b : b + 1])
    outflow[GROUPS * pipes :, :] = jnp.zeros_like(outflow[GROUPS * pipes :, :])
    back = (dir_v[...] == 1).astype(jnp.int32)
    lane = lax.broadcasted_iota(jnp.int32, (1, LANES), 1)
    for b in range(blocks):
        ahead = feed_v[2 * b : 2 * b + 1, :]
        behind = feed_v[2 * b + 1 : 2 * b + 2, :]
        rev = back[b : b + 1, :]
        src = jnp.where(rev == 1, behind, ahead)
        p = lane + b * LANES
        fine = src + (p << 10) + (rev << 20) + jnp.where(src >= pipes, MARK, 0)
        revs = [back[g * blocks + b : g * blocks + b + 1, :] for g in range(GROUPS)]
        most = jnp.maximum(jnp.maximum(revs[0], revs[1]), jnp.maximum(revs[2], revs[3]))
        least = jnp.minimum(jnp.minimum(revs[0], revs[1]), jnp.minimum(revs[2], revs[3]))
        fed = jnp.maximum(ahead * (1 - least), behind * most) >= pipes
        coarse = ahead + (behind << 10) + (p << 20) + jnp.where(fed, MARK, 0)
        words[b : b + 1, :] = jnp.where(level == 0, fine, coarse)
    backf = back.astype(jnp.float32)

    def back_rows(g):
        for b in range(blocks):
            at = g * blocks + b
            flow_back[at * LANES : (at + 1) * LANES, :] = down_rows(backf[at : at + 1])

    back_rows(0)

    @pl.when(level == 1)
    def _():
        for g in range(1, GROUPS):
            back_rows(g)

    per_chunk = pipes // 8 // CHUNKS

    @pl.when(level == 0)
    def _():
        rate_copy.wait()

        @pl.loop(0, CHUNKS)
        def _(n):
            chunk(n).wait()
            for i in range(per_chunk):
                q = n * per_chunk + i
                base = pl.multiple_of(q * 128, 128)
                own = pl.ds(pl.multiple_of(q * 8, 8), 8)
                rev = flow_back[own, :] != 0.0
                b = factor[own, :] * rates[pl.ds(pl.multiple_of(q * 32, 32), 8, stride=4), :]
                a = factor[own, :] - b
                y = [
                    jnp.where(
                        rev,
                        cells[pl.ds(base + j, 8, stride=16), :],
                        cells[pl.ds(base + 15 - j, 8, stride=16), :],
                    )
                    for j in range(GROUPS)
                ]
                for s in range(GROUPS):
                    outflow[pl.ds(pl.multiple_of(q * 32, 32) + s, 8, stride=4), :] = y[0]
                    y = [a * y[j] + b * y[j + 1] for j in range(len(y) - 1)]

    @pl.when(level == 1)
    def _():
        @pl.loop(0, CHUNKS)
        def _(n):
            chunk(n).wait()
            for i in range(per_chunk):
                q = n * per_chunk + i
                base = pl.multiple_of(q * 128, 128)
                for g in range(GROUPS):
                    rev = flow_back[pl.ds(pl.multiple_of(g * pipes + q * 8, 8), 8), :] != 0.0
                    outflow[pl.ds(pl.multiple_of(q * 32, 32) + g, 8, stride=4), :] = jnp.where(
                        rev,
                        cells[pl.ds(base + 4 * g, 8, stride=16), :],
                        cells[pl.ds(base + 4 * g + 3, 8, stride=16), :],
                    )

    @pl.loop(0, faces.shape[0] // 16)
    def _(m):
        moved = [
            outflow[pl.ds(pl.multiple_of(face_s[m * 16 + u] * 4, 4), 4), :] for u in range(16)
        ]
        for u in range(16):
            face_rows[pl.ds(pl.multiple_of(m * 64, 64) + 4 * u, 4), :] = moved[u]


def eight_words(q, words):
    per = LANES // 8
    return [words[q // per, (q % per) * 8 + u] for u in range(8)]


def gather_eight(fine, q, words, outflow, ahead_in, behind_in):
    start = pl.multiple_of(q * 32, 32)
    entries = eight_words(q, words)
    moved = [[outflow[pl.ds(pl.multiple_of((w & 1023) * 4, 4), 4), :] for w in entries]]
    if not fine:
        moved.append(
            [outflow[pl.ds(pl.multiple_of((w >> 10 & 1023) * 4, 4), 4), :] for w in entries]
        )
    for dest, tiles in zip((ahead_in, behind_in), moved):
        for u in range(8):
            dest[pl.ds(start + 4 * u, 4), :] = tiles[u]


def list_eight(fine, q, words, ghosts, counts):
    count, turned = counts
    second = ghosts.shape[0] // 2
    for w in eight_words(q, words):
        fed = lax.shift_right_logical(w, 31)
        ghosts[count] = w
        count = count + fed
        if fine:
            ghosts[second + turned] = w
            turned = turned + (fed & (w >> 20))
    return count, turned


def fine_block(q, cells, rates, factor, boosts, flow_back, ahead_in, new, shares):
    kept, kept_mid, sent_mid, sent = shares
    own = pl.ds(pl.multiple_of(q * 8, 8), 8)
    base = pl.multiple_of(q * 128, 128)
    quad = pl.multiple_of(q * 32, 32)
    rev = flow_back[own, :] != 0.0
    f = factor[own, :]
    b = f * rates[pl.ds(quad, 8, stride=4), :]
    a = f - b
    bo = boosts[own, :]
    x = [cells[pl.ds(base + k, 8, stride=16), :] for k in range(SEGF)]
    o = [jnp.where(rev, x[SEGF - 1 - k], x[k]) for k in range(SEGF)]
    for s in range(GROUPS):
        inflow = ahead_in[pl.ds(quad + s, 8, stride=4), :] + bo
        o = [a * o[k] + b * (o[k - 1] if k else inflow) for k in range(SEGF)]
    y = [jnp.where(rev, o[SEGF - 1 - k], o[k]) for k in range(SEGF)]
    for k in range(SEGF):
        new[pl.ds(base + k, 8, stride=16), :] = y[k]
    for k, dest in enumerate((kept, kept_mid, sent_mid, sent)):
        dest[own, :] = ((y[4 * k] + y[4 * k + 1]) + (y[4 * k + 2] + y[4 * k + 3])) * 0.25


def coarse_block(
    q, cells, rates, factor, boosts, flow_back, ahead_in, behind_in, new, shares
):
    kept, kept_mid, sent_mid, sent = shares
    pipes = factor.shape[0]
    own = pl.ds(pl.multiple_of(q * 8, 8), 8)
    base = pl.multiple_of(q * 128, 128)
    quad = pl.multiple_of(q * 32, 32)
    f = factor[own, :]
    bo = boosts[own, :]
    for g in range(GROUPS):
        rev = flow_back[pl.ds(pl.multiple_of(g * pipes + q * 8, 8), 8), :] != 0.0
        four = pl.ds(quad + g, 8, stride=4)
        b = f * rates[four, :]
        a = f - b
        inflow = jnp.where(rev, behind_in[four, :], ahead_in[four, :]) + bo
        x = [cells[pl.ds(base + 4 * g + k, 8, stride=16), :] for k in range(SEGC)]
        up = [
            jnp.where(
                rev, x[k + 1] if k + 1 < SEGC else inflow, x[k - 1] if k else inflow
            )
            for k in range(SEGC)
        ]
        y = [a * x[k] + b * up[k] for k in range(SEGC)]
        for k in range(SEGC):
            new[pl.ds(base + 4 * g + k, 8, stride=16), :] = y[k]
            if g == 0:
                (sent, sent_mid, kept_mid, kept)[k][own, :] = y[k]


def step_kernel(
    words, rate, cells, rates_in, outflow, factor, boosts, flow_back,
    new, out, kept, kept_mid, sent_mid, sent, ghosts, rates,
    ahead_in, behind_in, sems, rate_sems,
):
    shares = (kept, kept_mid, sent_mid, sent)
    level = lax.axis_index("level")
    eights = factor.shape[0] // 8
    parts = sems.shape[0]
    rows = new.shape[0] // parts

    def written(n):
        part = pl.ds(pl.multiple_of(n * rows, rows), rows)
        return pltpu.make_async_copy(new.at[part], out.at[part], sems.at[n])

    rate_rows = rates.shape[0] // parts

    def fetched(n):
        part = pl.ds(pl.multiple_of(n * rate_rows, rate_rows), rate_rows)
        return pltpu.make_async_copy(rate.at[part], rates.at[part], rate_sems.at[n])

    def run(fine):
        if not fine:
            for n in range(parts):
                fetched(n).start()
        gather_eight(fine, 0, words, outflow, ahead_in, behind_in)

        def some(q, count):
            if fine:
                fine_block(q, cells, rates, factor, boosts, flow_back, ahead_in, new, shares)
            else:
                coarse_block(
                    q, cells, rates, factor, boosts, flow_back, ahead_in, behind_in,
                    new, shares,
                )
            later = jnp.minimum(q + 1, eights - 1)
            gather_eight(fine, later, words, outflow, ahead_in, behind_in)
            return list_eight(fine, q, words, ghosts, count)

        per = eights // parts

        def part(n, count):
            if not fine:
                fetched(n).wait()
            count = lax.fori_loop(n * per, (n + 1) * per, some, count)
            @pl.when(n < parts - 1)
            def _():
                written(n).start()

            return count

        count, turned = lax.fori_loop(0, parts, part, (jnp.int32(0), jnp.int32(0)))
        ghosts[8 * eights] = count
        ghosts[16 * eights + 8] = turned

    @pl.when(level == 0)
    def _():
        run(True)

    @pl.when(level == 1)
    def _():
        run(False)

    for n in range(parts - 1):
        written(n).wait()


def arrive_kernel(first, near, arrived, outflow_in, outflow):
    odd = lax.axis_index("dom") % 2
    half = arrived.shape[0]
    slot = 1 - odd if near else odd
    start = pl.multiple_of(first + slot * half, 8)
    outflow[pl.ds(start, half), :] = arrived[...]


def over_list(count, ghosts, width, each, first=0):
    whole = count // width

    @pl.loop(0, whole)
    def _(m):
        each([ghosts[first + m * width + u] for u in range(width)])

    @pl.loop(whole * width, count)
    def _(i):
        each([ghosts[first + i]])


def send_kernel(
    first, ghosts, arrived, rates, factor, flow_back,
    outflow_in, sent_in, new_in, kept_in, outflow, sent, new, kept,
):
    pipes = factor.shape[0]
    level = lax.axis_index("level")
    arrive_kernel(first, False, arrived, outflow_in, outflow)

    def fine(entries):
        done = []
        for w in entries:
            src, p = w & 1023, w >> 10 & 1023
            own = pl.ds(p, 1)
            rows = outflow[pl.ds(pl.multiple_of(src * 4, 4), 4), :]
            f, r = factor[own, :], rates[pl.ds(p * 4, 1), :]
            total = rows[0:1]
            for s in range(1, GROUPS):
                total = f * total + rows[s : s + 1]
            done.append((own, sent[own, :] + f * r * total * 0.25))
        for own, row in done:
            sent[own, :] = row

    def coarse(entries):
        coarse_fix(entries, rates, factor, flow_back, outflow, new, kept, sent)

    @pl.when(level == 0)
    def _():
        over_list(ghosts[2 * pipes + 8], ghosts, 4, fine, pipes + 8)

    @pl.when(level == 1)
    def _():
        over_list(ghosts[pipes], ghosts, 4, coarse)


def fine_fix(entries, rates, factor, outflow, new, kept):
    row = lax.broadcasted_iota(jnp.int32, (8, LANES), 0)
    loaded = []
    for w in entries:
        src, p, rev = w & 1023, w >> 10 & 1023, w >> 20 & 1
        near = pl.ds(pl.multiple_of(p * 16 + 8 * rev, 8), 8)
        own = pl.ds(p, 1)
        inflow = [spread(outflow, src * 4 + s) for s in range(GROUPS)]
        loaded.append((
            rev, near, own, spread(factor, p), spread(rates, p * 4), inflow,
            new[near, :], kept[own, :],
        ))
    done = []
    for rev, near, own, f, r, inflow, tile, kept_row in loaded:
        b = f * r
        a = f - b
        edge = row == 7 * rev
        shift = 1 + 6 * rev
        total = b * inflow[0]
        delta = jnp.where(edge, total, 0.0)
        for s in range(1, GROUPS):
            up = jnp.where(edge, inflow[s], pltpu.roll(delta, shift, 0))
            delta = a * delta + b * up
            total = f * total + b * inflow[s]
        ahead = jnp.where(rev == 1, jnp.float32(0.0), jnp.float32(0.25))
        done.append((near, own, tile + delta, kept_row + total[0:1] * ahead))
    for near, own, tile, kept_row in done:
        new[near, :] = tile
        kept[own, :] = kept_row


def coarse_fix(entries, rates, factor, flow_back, outflow, new, kept, sent):
    pipes = factor.shape[0]
    zeros = outflow.shape[0] - 8
    loaded = []
    for w in entries:
        p = w >> 20 & 1023
        rows = []
        for src in (w & 1023, w >> 10 & 1023):
            at = jnp.where(src >= pipes, src * 4, zeros)
            rows.append(outflow[pl.ds(pl.multiple_of(at, 4), 4), :])
        low = pl.ds(p * 16, 4, stride=4)
        high = pl.ds(p * 16 + 3, 4, stride=4)
        loaded.append((
            p, low, high, rows, flow_back[pl.ds(p, 4, stride=pipes), :],
            rates[pl.ds(pl.multiple_of(p * 4, 4), 4), :], jnp.broadcast_to(factor[pl.ds(p, 1), :], (4, LANES)),
            new[low, :], new[high, :],
        ))
    done = []
    for p, low, high, rows, rev, r, f, first_rows, last_rows in loaded:
        turned = rev != 0.0
        delta = f * r * jnp.where(turned, rows[1], rows[0])
        done.append((
            p, low, high,
            first_rows + jnp.where(turned, 0.0, delta), last_rows + jnp.where(turned, delta, 0.0),
        ))
    for p, low, high, first_rows, last_rows in done:
        new[low, :] = first_rows
        new[high, :] = last_rows
        kept[pl.ds(p, 1), :] = last_rows[0:1]
        sent[pl.ds(p, 1), :] = first_rows[0:1]


def fix_kernel(
    ghosts, rates, factor, outflow, kept_mid, partner_mid, new_in, kept_in, out_in,
    new, kept, out, gap_rows, sem, tail_sem,
):
    pipes = factor.shape[0]
    level = lax.axis_index("level")
    shift = jnp.where(level == 0, 10, 20)
    count = ghosts[pipes]

    def write(entries):
        for w in entries:
            p = lax.shift_right_logical(w, shift) & 1023
            part = pl.ds(pl.multiple_of(p * SEGF, SEGF), SEGF)
            pltpu.make_async_copy(new.at[part], out.at[part], sem).start()

    def fine(entries):
        fine_fix(entries, rates, factor, outflow, new, kept)
        write(entries)

    @pl.when(level == 0)
    def _():
        over_list(count, ghosts, 4, fine)

    @pl.when(level == 1)
    def _():
        over_list(count, ghosts, 8, write)

    tail = pl.ds(pipes * SEGF // 8 * 7, pipes * SEGF // 8)
    last = pltpu.make_async_copy(new.at[tail], out.at[tail], tail_sem)
    last.start()
    sign = jnp.where(level == 0, jnp.float32(1.0), jnp.float32(-1.0))

    @pl.loop(0, pipes // 64)
    def _(m):
        for u in range(8):
            own = pl.ds(pl.multiple_of(m * 64 + 8 * u, 8), 8)
            spots = pl.ds(pl.multiple_of(m * 128, 128) + 16 * u + 1 - level, 8, stride=2)
            gap_rows[spots, :] = (kept_mid[own, :] - partner_mid[own, :]) * sign

    def wait(some):
        part = pl.ds(0, SEGF * some)
        pltpu.make_async_copy(new.at[part], out.at[part], sem).wait()

    whole = count // 8

    @pl.loop(0, whole)
    def _(m):
        wait(8)

    @pl.loop(whole * 8, count)
    def _(i):
        wait(1)

    last.wait()


def gap_kernel(kept, partner, rows_in, rows, gap, sems):
    level = lax.axis_index("level")
    sign = jnp.where(level == 0, jnp.float32(1.0), jnp.float32(-1.0))
    parts = sems.shape[0]
    copies = []
    per = kept.shape[0] // 8 // parts
    for n in range(parts):
        for q in range(n * per, (n + 1) * per):
            own = pl.ds(8 * q, 8)
            rows[pl.ds(16 * q + level, 8, stride=2), :] = (kept[own, :] - partner[own, :]) * sign
        part = pl.ds(n * per * 16, per * 16)
        copies.append(pltpu.make_async_copy(rows.at[part], gap.at[part], sems.at[n]))
        copies[-1].start()
    for copy in copies:
        copy.wait()


def per_device(panels, courant, direction, decay, booster, feeder, face_index):
    pipes = panels.shape[1]
    columns = panels.shape[3]
    faces = face_index.shape[0]
    blocks = pipes // LANES
    domains = lax.axis_size("dom")
    f32, i32 = jnp.float32, jnp.int32
    cells_in = panels.reshape(pipes * SEGF, columns)
    rates_in = courant.reshape(pipes * GROUPS, columns)
    dirs = direction.transpose(1, 2, 0).reshape(GROUPS * blocks, LANES)
    feed = feeder.reshape(blocks, LANES, 2).transpose(0, 2, 1).reshape(2 * blocks, LANES)
    ghost_rows = GROUPS * (pipes + 2 * faces) + 8

    cells_in, rates_in, dirs, feed, decay, booster, face_index = pinned(
        pltpu.HBM, cells_in, rates_in, dirs, feed,
        decay.reshape(blocks, LANES), booster.reshape(blocks, LANES), face_index,
    )
    cells, rates, outflow, factor, boosts, flow_back, words, face_rows = pl.pallas_call(
        load_kernel,
        name="load_step",
        in_specs=[HBM] * 7,
        out_specs=[VMEM] * 8,
        out_shape=[
            pltpu.VMEM((pipes * SEGF, columns), f32),
            pltpu.VMEM((pipes * GROUPS, columns), f32),
            pltpu.VMEM((ghost_rows, columns), f32),
            pltpu.VMEM((pipes, columns), f32),
            pltpu.VMEM((pipes, columns), f32),
            pltpu.VMEM((GROUPS * pipes, columns), f32),
            jax.ShapeDtypeStruct((blocks, LANES), i32),
            pltpu.VMEM((faces * GROUPS, columns), f32),
        ],
        scratch_shapes=[
            pltpu.VMEM(dirs.shape, i32),
            pltpu.VMEM(feed.shape, i32),
            pltpu.VMEM((blocks, LANES), f32),
            pltpu.VMEM((blocks, LANES), f32),
            pltpu.SMEM((faces,), i32),
            pltpu.SemaphoreType.DMA((CHUNKS,)),
            pltpu.SemaphoreType.DMA(()),
            pltpu.SemaphoreType.DMA((5,)),
        ],
        compiler_params=params(),
        cost_estimate=cost(5 << 20),
    )(cells_in, rates_in, dirs, feed, decay, booster, face_index)

    near_pairs = [(i, i ^ 1) for i in range(domains) if i ^ 1 < domains]
    far_pairs = [(i, i + 1) for i in range(1, domains - 1, 2)]
    far_pairs = far_pairs + [(j, i) for i, j in far_pairs]
    near_rows = lax.ppermute(face_rows, "dom", near_pairs)
    far_rows = lax.ppermute(face_rows, "dom", far_pairs)

    new, out, kept, kept_mid, sent_mid, sent, ghosts, rates = pl.pallas_call(
        step_kernel,
        name="advance_step",
        in_specs=[SMEM, HBM] + [VMEM] * 6,
        out_specs=[VMEM, HBM] + [VMEM] * 4 + [SMEM, VMEM],
        out_shape=[
            pltpu.VMEM((pipes * SEGF, columns), f32),
            jax.ShapeDtypeStruct((pipes * SEGF, columns), f32),
            *[pltpu.VMEM((pipes, columns), f32)] * 4,
            pltpu.SMEM((2 * (pipes + 8),), i32),
            pltpu.VMEM((pipes * GROUPS, columns), f32),
        ],
        scratch_shapes=[pltpu.VMEM((GROUPS * pipes, columns), f32)] * 2
        + [pltpu.SemaphoreType.DMA((8,))] * 2,
        input_output_aliases={3: 7},
        compiler_params=params(),
        cost_estimate=cost(20 << 20),
    )(words, rates_in, cells, rates, outflow, factor, boosts, flow_back)

    swap = [(0, 1), (1, 0)]
    partner_mid = lax.ppermute(sent_mid, "level", swap)
    first = GROUPS * pipes
    outflow = pl.pallas_call(
        lambda *refs: arrive_kernel(first, True, *refs),
        name="near_arrive",
        in_specs=[VMEM] * 2,
        out_specs=VMEM,
        out_shape=pltpu.VMEM((ghost_rows, columns), f32),
        input_output_aliases={1: 0},
        compiler_params=params(),
        cost_estimate=cost(1 << 19),
    )(near_rows, outflow)

    outflow, sent, new, kept = pl.pallas_call(
        lambda *refs: send_kernel(first, *refs),
        name="ghost_send",
        in_specs=[SMEM] + [VMEM] * 8,
        out_specs=[VMEM] * 4,
        out_shape=[
            pltpu.VMEM((ghost_rows, columns), f32),
            pltpu.VMEM((pipes, columns), f32),
            pltpu.VMEM((pipes * SEGF, columns), f32),
            pltpu.VMEM((pipes, columns), f32),
        ],
        input_output_aliases={5: 0, 6: 1, 7: 2, 8: 3},
        compiler_params=params(),
        cost_estimate=cost(1 << 20),
    )(ghosts, far_rows, rates, factor, flow_back, outflow, sent, new, kept)

    partner = lax.ppermute(sent, "level", swap)

    new, kept, out, gap_rows = pl.pallas_call(
        fix_kernel,
        name="ghost_fix",
        in_specs=[SMEM] + [VMEM] * 7 + [HBM],
        out_specs=[VMEM, VMEM, HBM, VMEM],
        out_shape=[
            pltpu.VMEM((pipes * SEGF, columns), f32),
            pltpu.VMEM((pipes, columns), f32),
            jax.ShapeDtypeStruct((pipes * SEGF, columns), f32),
            pltpu.VMEM((pipes * 2, columns), f32),
        ],
        scratch_shapes=[pltpu.SemaphoreType.DMA(())] * 2,
        input_output_aliases={6: 0, 7: 1, 8: 2},
        compiler_params=params(),
        cost_estimate=cost(4 << 20),
    )(
        ghosts, rates, factor, outflow, kept_mid, partner_mid, new, kept,
        *pinned(pltpu.HBM, out),
    )

    _, gap = pl.pallas_call(
        gap_kernel,
        name="level_gap",
        in_specs=[VMEM] * 3,
        out_specs=[VMEM, HBM],
        out_shape=[
            pltpu.VMEM((pipes * 2, columns), f32),
            jax.ShapeDtypeStruct((pipes * 2, columns), f32),
        ],
        scratch_shapes=[pltpu.SemaphoreType.DMA((2,))],
        input_output_aliases={2: 0},
        compiler_params=params(),
        cost_estimate=cost(1 << 20),
    )(kept, partner, gap_rows)
    return (out.reshape(1, pipes, SEGF, columns), gap.reshape(pipes, 2, columns))


def solution(mesh):
    in_specs = (
        P("level", "dom", None, "samp"),
        P("dom", None, "samp"),
        P("dom", None, "samp"),
        P("dom"),
        P("dom"),
        P("dom", None),
        P("dom"),
    )
    out_specs = (P("level", "dom", None, "samp"), P("dom", "level", "samp"))
    return jax.shard_map(
        per_device, mesh=mesh, in_specs=in_specs, out_specs=out_specs, check_vma=False
    )
```

```python
import jax
import jax.numpy as jnp
from jax import lax
from jax.experimental import pallas as pl
from jax.experimental.pallas import tpu as pltpu
from jax.sharding import PartitionSpec as P

SEGF = 16
SEGC = 4
GROUPS = SEGF // SEGC
LANES = 128
CHUNKS = 8
MARK = -(1 << 31)

HBM = pl.BlockSpec(memory_space=pltpu.HBM)
VMEM = pl.BlockSpec(memory_space=pltpu.VMEM)
SMEM = pl.BlockSpec(memory_space=pltpu.SMEM)


def params():
    return pltpu.CompilerParams(vmem_limit_bytes=8 << 20)


def cost(nbytes):
    return pl.CostEstimate(flops=0, bytes_accessed=nbytes, transcendentals=0)


def pinned(space, *arrays):
    return [pltpu.with_memory_space_constraint(x, space) for x in arrays]


def down_rows(row):
    return jnp.broadcast_to(row, (LANES, LANES)).T


def spread(ref, row):
    return jnp.broadcast_to(ref[pl.ds(row, 1), :], (8, LANES))


def load_kernel(
    panel, rate, dirs, feed, decay, boost, faces,
    cells, rates, outflow, factor, boosts, flow_back, words, face_rows,
    dir_v, feed_v, decay_v, boost_v, face_s, panel_sem, rate_sem, small_sem,
):
    rows = panel.shape[0] // CHUNKS
    blocks = decay.shape[0]
    pipes = blocks * LANES
    level = lax.axis_index("level")

    def chunk(n):
        part = pl.ds(pl.multiple_of(n * rows, rows), rows)
        return pltpu.make_async_copy(panel.at[part], cells.at[part], panel_sem.at[n])

    small = [
        pltpu.make_async_copy(src, dst, small_sem.at[n])
        for n, (src, dst) in enumerate(
            ((dirs, dir_v), (feed, feed_v), (decay, decay_v), (boost, boost_v), (faces, face_s))
        )
    ]
    rate_copy = pltpu.make_async_copy(rate, rates, rate_sem)
    for copy in small:
        copy.start()

    @pl.when(level == 0)
    def _():
        rate_copy.start()

    for n in range(CHUNKS):
        chunk(n).start(priority=1)
    for copy in small:
        copy.wait()

    scale = jnp.where(level == 0, jnp.float32(-0.25), jnp.float32(-1.0))
    fac = jnp.exp(decay_v[...] * scale)
    for b in range(blocks):
        own = slice(b * LANES, (b + 1) * LANES)
        factor[own, :] = down_rows(fac[b : b + 1])
        boosts[own, :] = down_rows(boost_v[b : b + 1])
    outflow[GROUPS * pipes :, :] = jnp.zeros_like(outflow[GROUPS * pipes :, :])
    back = (dir_v[...] == 1).astype(jnp.int32)
    lane = lax.broadcasted_iota(jnp.int32, (1, LANES), 1)
    for b in range(blocks):
        ahead = feed_v[2 * b : 2 * b + 1, :]
        behind = feed_v[2 * b + 1 : 2 * b + 2, :]
        rev = back[b : b + 1, :]
        src = jnp.where(rev == 1, behind, ahead)
        p = lane + b * LANES
        fine = src + (p << 10) + (rev << 20) + jnp.where(src >= pipes, MARK, 0)
        revs = [back[g * blocks + b : g * blocks + b + 1, :] for g in range(GROUPS)]
        most = jnp.maximum(jnp.maximum(revs[0], revs[1]), jnp.maximum(revs[2], revs[3]))
        least = jnp.minimum(jnp.minimum(revs[0], revs[1]), jnp.minimum(revs[2], revs[3]))
        fed = jnp.maximum(ahead * (1 - least), behind * most) >= pipes
        coarse = ahead + (behind << 10) + (p << 20) + jnp.where(fed, MARK, 0)
        words[b : b + 1, :] = jnp.where(level == 0, fine, coarse)
    backf = back.astype(jnp.float32)

    def back_rows(g):
        for b in range(blocks):
            at = g * blocks + b
            flow_back[at * LANES : (at + 1) * LANES, :] = down_rows(backf[at : at + 1])

    back_rows(0)

    @pl.when(level == 1)
    def _():
        for g in range(1, GROUPS):
            back_rows(g)

    per_chunk = pipes // 8 // CHUNKS

    @pl.when(level == 0)
    def _():
        rate_copy.wait()

        @pl.loop(0, CHUNKS)
        def _(n):
            chunk(n).wait()
            for i in range(per_chunk):
                q = n * per_chunk + i
                base = pl.multiple_of(q * 128, 128)
                own = pl.ds(pl.multiple_of(q * 8, 8), 8)
                rev = flow_back[own, :] != 0.0
                b = factor[own, :] * rates[pl.ds(pl.multiple_of(q * 32, 32), 8, stride=4), :]
                a = factor[own, :] - b
                y = [
                    jnp.where(
                        rev,
                        cells[pl.ds(base + j, 8, stride=16), :],
                        cells[pl.ds(base + 15 - j, 8, stride=16), :],
                    )
                    for j in range(GROUPS)
                ]
                for s in range(GROUPS):
                    outflow[pl.ds(pl.multiple_of(q * 32, 32) + s, 8, stride=4), :] = y[0]
                    y = [a * y[j] + b * y[j + 1] for j in range(len(y) - 1)]

    @pl.when(level == 1)
    def _():
        @pl.loop(0, CHUNKS)
        def _(n):
            chunk(n).wait()
            for i in range(per_chunk):
                q = n * per_chunk + i
                base = pl.multiple_of(q * 128, 128)
                for g in range(GROUPS):
                    rev = flow_back[pl.ds(pl.multiple_of(g * pipes + q * 8, 8), 8), :] != 0.0
                    outflow[pl.ds(pl.multiple_of(q * 32, 32) + g, 8, stride=4), :] = jnp.where(
                        rev,
                        cells[pl.ds(base + 4 * g, 8, stride=16), :],
                        cells[pl.ds(base + 4 * g + 3, 8, stride=16), :],
                    )

    @pl.loop(0, faces.shape[0] // 64)
    def _(m):
        moved = [
            outflow[pl.ds(pl.multiple_of(face_s[m * 64 + u] * 4, 4), 4), :] for u in range(64)
        ]
        for u in range(64):
            face_rows[pl.ds(pl.multiple_of(m * 256, 256) + 4 * u, 4), :] = moved[u]


def eight_words(q, words):
    per = LANES // 8
    return [words[q // per, (q % per) * 8 + u] for u in range(8)]


def gather_eight(fine, q, words, outflow, ahead_in, behind_in):
    start = pl.multiple_of(q * 32, 32)
    entries = eight_words(q, words)
    moved = [[outflow[pl.ds(pl.multiple_of((w & 1023) * 4, 4), 4), :] for w in entries]]
    if not fine:
        moved.append(
            [outflow[pl.ds(pl.multiple_of((w >> 10 & 1023) * 4, 4), 4), :] for w in entries]
        )
    for dest, tiles in zip((ahead_in, behind_in), moved):
        for u in range(8):
            dest[pl.ds(start + 4 * u, 4), :] = tiles[u]


def list_eight(fine, q, words, ghosts, counts):
    count, turned = counts
    second = ghosts.shape[0] // 2
    for w in eight_words(q, words):
        fed = lax.shift_right_logical(w, 31)
        ghosts[count] = w
        count = count + fed
        if fine:
            ghosts[second + turned] = w
            turned = turned + (fed & (w >> 20))
    return count, turned


def fine_block(q, cells, rates, factor, boosts, flow_back, ahead_in, new, shares):
    kept, kept_mid, sent_mid, sent = shares
    own = pl.ds(pl.multiple_of(q * 8, 8), 8)
    base = pl.multiple_of(q * 128, 128)
    quad = pl.multiple_of(q * 32, 32)
    rev = flow_back[own, :] != 0.0
    f = factor[own, :]
    b = f * rates[pl.ds(quad, 8, stride=4), :]
    a = f - b
    bo = boosts[own, :]
    x = [cells[pl.ds(base + k, 8, stride=16), :] for k in range(SEGF)]
    o = [jnp.where(rev, x[SEGF - 1 - k], x[k]) for k in range(SEGF)]
    for s in range(GROUPS):
        inflow = ahead_in[pl.ds(quad + s, 8, stride=4), :] + bo
        o = [a * o[k] + b * (o[k - 1] if k else inflow) for k in range(SEGF)]
    y = [jnp.where(rev, o[SEGF - 1 - k], o[k]) for k in range(SEGF)]
    for k in range(SEGF):
        new[pl.ds(base + k, 8, stride=16), :] = y[k]
    for k, dest in enumerate((kept, kept_mid, sent_mid, sent)):
        dest[own, :] = ((y[4 * k] + y[4 * k + 1]) + (y[4 * k + 2] + y[4 * k + 3])) * 0.25


def coarse_block(
    q, cells, rates, factor, boosts, flow_back, ahead_in, behind_in, new, shares
):
    kept, kept_mid, sent_mid, sent = shares
    pipes = factor.shape[0]
    own = pl.ds(pl.multiple_of(q * 8, 8), 8)
    base = pl.multiple_of(q * 128, 128)
    quad = pl.multiple_of(q * 32, 32)
    f = factor[own, :]
    bo = boosts[own, :]
    for g in range(GROUPS):
        rev = flow_back[pl.ds(pl.multiple_of(g * pipes + q * 8, 8), 8), :] != 0.0
        four = pl.ds(quad + g, 8, stride=4)
        b = f * rates[four, :]
        a = f - b
        inflow = jnp.where(rev, behind_in[four, :], ahead_in[four, :]) + bo
        x = [cells[pl.ds(base + 4 * g + k, 8, stride=16), :] for k in range(SEGC)]
        up = [
            jnp.where(
                rev, x[k + 1] if k + 1 < SEGC else inflow, x[k - 1] if k else inflow
            )
            for k in range(SEGC)
        ]
        y = [a * x[k] + b * up[k] for k in range(SEGC)]
        for k in range(SEGC):
            new[pl.ds(base + 4 * g + k, 8, stride=16), :] = y[k]
            if g == 0:
                (sent, sent_mid, kept_mid, kept)[k][own, :] = y[k]


def step_kernel(
    words, rate, cells, rates_in, outflow, factor, boosts, flow_back,
    new, out, kept, kept_mid, sent_mid, sent, ghosts, rates,
    ahead_in, behind_in, sems, rate_sems,
):
    shares = (kept, kept_mid, sent_mid, sent)
    level = lax.axis_index("level")
    eights = factor.shape[0] // 8
    parts = sems.shape[0]
    rows = new.shape[0] // parts

    def written(n):
        part = pl.ds(pl.multiple_of(n * rows, rows), rows)
        return pltpu.make_async_copy(new.at[part], out.at[part], sems.at[n])

    rate_rows = rates.shape[0] // parts

    def fetched(n):
        part = pl.ds(pl.multiple_of(n * rate_rows, rate_rows), rate_rows)
        return pltpu.make_async_copy(rate.at[part], rates.at[part], rate_sems.at[n])

    def run(fine):
        if not fine:
            for n in range(parts):
                fetched(n).start()
        gather_eight(fine, 0, words, outflow, ahead_in, behind_in)

        def some(q, count):
            if fine:
                fine_block(q, cells, rates, factor, boosts, flow_back, ahead_in, new, shares)
            else:
                coarse_block(
                    q, cells, rates, factor, boosts, flow_back, ahead_in, behind_in,
                    new, shares,
                )
            later = jnp.minimum(q + 1, eights - 1)
            gather_eight(fine, later, words, outflow, ahead_in, behind_in)
            return list_eight(fine, q, words, ghosts, count)

        per = eights // parts

        def part(n, count):
            if not fine:
                fetched(n).wait()
            count = lax.fori_loop(n * per, (n + 1) * per, some, count)
            @pl.when(n < parts - 1)
            def _():
                written(n).start()

            return count

        count, turned = lax.fori_loop(0, parts, part, (jnp.int32(0), jnp.int32(0)))
        ghosts[8 * eights] = count
        ghosts[16 * eights + 8] = turned

    @pl.when(level == 0)
    def _():
        run(True)

    @pl.when(level == 1)
    def _():
        run(False)

    for n in range(parts - 1):
        written(n).wait()


def arrive_kernel(first, near, arrived, outflow_in, outflow):
    odd = lax.axis_index("dom") % 2
    half = arrived.shape[0]
    slot = 1 - odd if near else odd
    start = pl.multiple_of(first + slot * half, 8)
    outflow[pl.ds(start, half), :] = arrived[...]


def over_list(count, ghosts, width, each, first=0):
    whole = count // width

    @pl.loop(0, whole)
    def _(m):
        each([ghosts[first + m * width + u] for u in range(width)])

    @pl.loop(whole * width, count)
    def _(i):
        each([ghosts[first + i]])


def send_kernel(
    first, ghosts, arrived, rates, factor, flow_back,
    outflow_in, sent_in, new_in, kept_in, outflow, sent, new, kept,
):
    pipes = factor.shape[0]
    level = lax.axis_index("level")
    arrive_kernel(first, False, arrived, outflow_in, outflow)

    def fine(entries):
        done = []
        for w in entries:
            src, p = w & 1023, w >> 10 & 1023
            own = pl.ds(p, 1)
            rows = outflow[pl.ds(pl.multiple_of(src * 4, 4), 4), :]
            f, r = factor[own, :], rates[pl.ds(p * 4, 1), :]
            total = rows[0:1]
            for s in range(1, GROUPS):
                total = f * total + rows[s : s + 1]
            done.append((own, sent[own, :] + f * r * total * 0.25))
        for own, row in done:
            sent[own, :] = row

    def coarse(entries):
        coarse_fix(entries, rates, factor, flow_back, outflow, new, kept, sent)

    @pl.when(level == 0)
    def _():
        over_list(ghosts[2 * pipes + 8], ghosts, 4, fine, pipes + 8)

    @pl.when(level == 1)
    def _():
        over_list(ghosts[pipes], ghosts, 4, coarse)


def fine_fix(entries, rates, factor, outflow, new, kept):
    row = lax.broadcasted_iota(jnp.int32, (8, LANES), 0)
    loaded = []
    for w in entries:
        src, p, rev = w & 1023, w >> 10 & 1023, w >> 20 & 1
        near = pl.ds(pl.multiple_of(p * 16 + 8 * rev, 8), 8)
        own = pl.ds(p, 1)
        inflow = [spread(outflow, src * 4 + s) for s in range(GROUPS)]
        loaded.append((
            rev, near, own, spread(factor, p), spread(rates, p * 4), inflow,
            new[near, :], kept[own, :],
        ))
    done = []
    for rev, near, own, f, r, inflow, tile, kept_row in loaded:
        b = f * r
        a = f - b
        edge = row == 7 * rev
        shift = 1 + 6 * rev
        total = b * inflow[0]
        delta = jnp.where(edge, total, 0.0)
        for s in range(1, GROUPS):
            up = jnp.where(edge, inflow[s], pltpu.roll(delta, shift, 0))
            delta = a * delta + b * up
            total = f * total + b * inflow[s]
        ahead = jnp.where(rev == 1, jnp.float32(0.0), jnp.float32(0.25))
        done.append((near, own, tile + delta, kept_row + total[0:1] * ahead))
    for near, own, tile, kept_row in done:
        new[near, :] = tile
        kept[own, :] = kept_row


def coarse_fix(entries, rates, factor, flow_back, outflow, new, kept, sent):
    pipes = factor.shape[0]
    zeros = outflow.shape[0] - 8
    loaded = []
    for w in entries:
        p = w >> 20 & 1023
        rows = []
        for src in (w & 1023, w >> 10 & 1023):
            at = jnp.where(src >= pipes, src * 4, zeros)
            rows.append(outflow[pl.ds(pl.multiple_of(at, 4), 4), :])
        low = pl.ds(p * 16, 4, stride=4)
        high = pl.ds(p * 16 + 3, 4, stride=4)
        loaded.append((
            p, low, high, rows, flow_back[pl.ds(p, 4, stride=pipes), :],
            rates[pl.ds(pl.multiple_of(p * 4, 4), 4), :], jnp.broadcast_to(factor[pl.ds(p, 1), :], (4, LANES)),
            new[low, :], new[high, :],
        ))
    done = []
    for p, low, high, rows, rev, r, f, first_rows, last_rows in loaded:
        turned = rev != 0.0
        delta = f * r * jnp.where(turned, rows[1], rows[0])
        done.append((
            p, low, high,
            first_rows + jnp.where(turned, 0.0, delta), last_rows + jnp.where(turned, delta, 0.0),
        ))
    for p, low, high, first_rows, last_rows in done:
        new[low, :] = first_rows
        new[high, :] = last_rows
        kept[pl.ds(p, 1), :] = last_rows[0:1]
        sent[pl.ds(p, 1), :] = first_rows[0:1]


def fix_kernel(
    ghosts, rates, factor, outflow, kept_mid, partner_mid, new_in, kept_in, out_in,
    new, kept, out, gap_rows, sem, tail_sem,
):
    pipes = factor.shape[0]
    level = lax.axis_index("level")
    shift = jnp.where(level == 0, 10, 20)
    count = ghosts[pipes]

    def write(entries):
        for w in entries:
            p = lax.shift_right_logical(w, shift) & 1023
            part = pl.ds(pl.multiple_of(p * SEGF, SEGF), SEGF)
            pltpu.make_async_copy(new.at[part], out.at[part], sem).start()

    def fine(entries):
        fine_fix(entries, rates, factor, outflow, new, kept)
        write(entries)

    @pl.when(level == 0)
    def _():
        over_list(count, ghosts, 4, fine)

    @pl.when(level == 1)
    def _():
        over_list(count, ghosts, 8, write)

    tail = pl.ds(pipes * SEGF // 8 * 7, pipes * SEGF // 8)
    last = pltpu.make_async_copy(new.at[tail], out.at[tail], tail_sem)
    last.start()
    sign = jnp.where(level == 0, jnp.float32(1.0), jnp.float32(-1.0))

    @pl.loop(0, pipes // 64)
    def _(m):
        for u in range(8):
            own = pl.ds(pl.multiple_of(m * 64 + 8 * u, 8), 8)
            spots = pl.ds(pl.multiple_of(m * 128, 128) + 16 * u + 1 - level, 8, stride=2)
            gap_rows[spots, :] = (kept_mid[own, :] - partner_mid[own, :]) * sign

    def wait(some):
        part = pl.ds(0, SEGF * some)
        pltpu.make_async_copy(new.at[part], out.at[part], sem).wait()

    whole = count // 8

    @pl.loop(0, whole)
    def _(m):
        wait(8)

    @pl.loop(whole * 8, count)
    def _(i):
        wait(1)

    last.wait()


def gap_kernel(kept, partner, rows_in, rows, gap, sems):
    level = lax.axis_index("level")
    sign = jnp.where(level == 0, jnp.float32(1.0), jnp.float32(-1.0))
    parts = sems.shape[0]
    copies = []
    per = kept.shape[0] // 8 // parts
    for n in range(parts):
        for q in range(n * per, (n + 1) * per):
            own = pl.ds(8 * q, 8)
            rows[pl.ds(16 * q + level, 8, stride=2), :] = (kept[own, :] - partner[own, :]) * sign
        part = pl.ds(n * per * 16, per * 16)
        copies.append(pltpu.make_async_copy(rows.at[part], gap.at[part], sems.at[n]))
        copies[-1].start()
    for copy in copies:
        copy.wait()


def per_device(panels, courant, direction, decay, booster, feeder, face_index):
    pipes = panels.shape[1]
    columns = panels.shape[3]
    faces = face_index.shape[0]
    blocks = pipes // LANES
    domains = lax.axis_size("dom")
    f32, i32 = jnp.float32, jnp.int32
    cells_in = panels.reshape(pipes * SEGF, columns)
    rates_in = courant.reshape(pipes * GROUPS, columns)
    dirs = direction.transpose(1, 2, 0).reshape(GROUPS * blocks, LANES)
    feed = feeder.reshape(blocks, LANES, 2).transpose(0, 2, 1).reshape(2 * blocks, LANES)
    ghost_rows = GROUPS * (pipes + 2 * faces) + 8

    cells_in, rates_in, dirs, feed, decay, booster, face_index = pinned(
        pltpu.HBM, cells_in, rates_in, dirs, feed,
        decay.reshape(blocks, LANES), booster.reshape(blocks, LANES), face_index,
    )
    cells, rates, outflow, factor, boosts, flow_back, words, face_rows = pl.pallas_call(
        load_kernel,
        name="load_step",
        in_specs=[HBM] * 7,
        out_specs=[VMEM] * 8,
        out_shape=[
            pltpu.VMEM((pipes * SEGF, columns), f32),
            pltpu.VMEM((pipes * GROUPS, columns), f32),
            pltpu.VMEM((ghost_rows, columns), f32),
            pltpu.VMEM((pipes, columns), f32),
            pltpu.VMEM((pipes, columns), f32),
            pltpu.VMEM((GROUPS * pipes, columns), f32),
            jax.ShapeDtypeStruct((blocks, LANES), i32),
            pltpu.VMEM((faces * GROUPS, columns), f32),
        ],
        scratch_shapes=[
            pltpu.VMEM(dirs.shape, i32),
            pltpu.VMEM(feed.shape, i32),
            pltpu.VMEM((blocks, LANES), f32),
            pltpu.VMEM((blocks, LANES), f32),
            pltpu.SMEM((faces,), i32),
            pltpu.SemaphoreType.DMA((CHUNKS,)),
            pltpu.SemaphoreType.DMA(()),
            pltpu.SemaphoreType.DMA((5,)),
        ],
        compiler_params=params(),
        cost_estimate=cost(5 << 20),
    )(cells_in, rates_in, dirs, feed, decay, booster, face_index)

    near_pairs = [(i, i ^ 1) for i in range(domains) if i ^ 1 < domains]
    far_pairs = [(i, i + 1) for i in range(1, domains - 1, 2)]
    far_pairs = far_pairs + [(j, i) for i, j in far_pairs]
    near_rows = lax.ppermute(face_rows, "dom", near_pairs)
    far_rows = lax.ppermute(face_rows, "dom", far_pairs)

    new, out, kept, kept_mid, sent_mid, sent, ghosts, rates = pl.pallas_call(
        step_kernel,
        name="advance_step",
        in_specs=[SMEM, HBM] + [VMEM] * 6,
        out_specs=[VMEM, HBM] + [VMEM] * 4 + [SMEM, VMEM],
        out_shape=[
            pltpu.VMEM((pipes * SEGF, columns), f32),
            jax.ShapeDtypeStruct((pipes * SEGF, columns), f32),
            *[pltpu.VMEM((pipes, columns), f32)] * 4,
            pltpu.SMEM((2 * (pipes + 8),), i32),
            pltpu.VMEM((pipes * GROUPS, columns), f32),
        ],
        scratch_shapes=[pltpu.VMEM((GROUPS * pipes, columns), f32)] * 2
        + [pltpu.SemaphoreType.DMA((8,))] * 2,
        input_output_aliases={3: 7},
        compiler_params=params(),
        cost_estimate=cost(20 << 20),
    )(words, rates_in, cells, rates, outflow, factor, boosts, flow_back)

    swap = [(0, 1), (1, 0)]
    partner_mid = lax.ppermute(sent_mid, "level", swap)
    first = GROUPS * pipes
    outflow = pl.pallas_call(
        lambda *refs: arrive_kernel(first, True, *refs),
        name="near_arrive",
        in_specs=[VMEM] * 2,
        out_specs=VMEM,
        out_shape=pltpu.VMEM((ghost_rows, columns), f32),
        input_output_aliases={1: 0},
        compiler_params=params(),
        cost_estimate=cost(1 << 19),
    )(near_rows, outflow)

    outflow, sent, new, kept = pl.pallas_call(
        lambda *refs: send_kernel(first, *refs),
        name="ghost_send",
        in_specs=[SMEM] + [VMEM] * 8,
        out_specs=[VMEM] * 4,
        out_shape=[
            pltpu.VMEM((ghost_rows, columns), f32),
            pltpu.VMEM((pipes, columns), f32),
            pltpu.VMEM((pipes * SEGF, columns), f32),
            pltpu.VMEM((pipes, columns), f32),
        ],
        input_output_aliases={5: 0, 6: 1, 7: 2, 8: 3},
        compiler_params=params(),
        cost_estimate=cost(1 << 20),
    )(ghosts, far_rows, rates, factor, flow_back, outflow, sent, new, kept)

    partner = lax.ppermute(sent, "level", swap)

    new, kept, out, gap_rows = pl.pallas_call(
        fix_kernel,
        name="ghost_fix",
        in_specs=[SMEM] + [VMEM] * 7 + [HBM],
        out_specs=[VMEM, VMEM, HBM, VMEM],
        out_shape=[
            pltpu.VMEM((pipes * SEGF, columns), f32),
            pltpu.VMEM((pipes, columns), f32),
            jax.ShapeDtypeStruct((pipes * SEGF, columns), f32),
            pltpu.VMEM((pipes * 2, columns), f32),
        ],
        scratch_shapes=[pltpu.SemaphoreType.DMA(())] * 2,
        input_output_aliases={6: 0, 7: 1, 8: 2},
        compiler_params=params(),
        cost_estimate=cost(4 << 20),
    )(
        ghosts, rates, factor, outflow, kept_mid, partner_mid, new, kept,
        *pinned(pltpu.HBM, out),
    )

    _, gap = pl.pallas_call(
        gap_kernel,
        name="level_gap",
        in_specs=[VMEM] * 3,
        out_specs=[VMEM, HBM],
        out_shape=[
            pltpu.VMEM((pipes * 2, columns), f32),
            jax.ShapeDtypeStruct((pipes * 2, columns), f32),
        ],
        scratch_shapes=[pltpu.SemaphoreType.DMA((2,))],
        input_output_aliases={2: 0},
        compiler_params=params(),
        cost_estimate=cost(1 << 20),
    )(kept, partner, gap_rows)
    return (out.reshape(1, pipes, SEGF, columns), gap.reshape(pipes, 2, columns))


def solution(mesh):
    in_specs = (
        P("level", "dom", None, "samp"),
        P("dom", None, "samp"),
        P("dom", None, "samp"),
        P("dom"),
        P("dom"),
        P("dom", None),
        P("dom"),
    )
    out_specs = (P("level", "dom", None, "samp"), P("dom", "level", "samp"))
    return jax.shard_map(
        per_device, mesh=mesh, in_specs=in_specs, out_specs=out_specs, check_vma=False
    )
```

```python
import jax
import jax.numpy as jnp
from jax import lax
from jax.experimental import pallas as pl
from jax.experimental.pallas import tpu as pltpu
from jax.sharding import PartitionSpec as P

SEGF = 16
SEGC = 4
GROUPS = SEGF // SEGC
LANES = 128
CHUNKS = 8
MARK = -(1 << 31)

HBM = pl.BlockSpec(memory_space=pltpu.HBM)
VMEM = pl.BlockSpec(memory_space=pltpu.VMEM)
SMEM = pl.BlockSpec(memory_space=pltpu.SMEM)


def params():
    return pltpu.CompilerParams(vmem_limit_bytes=8 << 20)


def cost(nbytes):
    return pl.CostEstimate(flops=0, bytes_accessed=nbytes, transcendentals=0)


def pinned(space, *arrays):
    return [pltpu.with_memory_space_constraint(x, space) for x in arrays]


def down_rows(row):
    return jnp.broadcast_to(row, (LANES, LANES)).T


def spread(ref, row):
    return jnp.broadcast_to(ref[pl.ds(row, 1), :], (8, LANES))


def load_kernel(
    panel, rate, dirs, feed, decay, boost, faces,
    cells, rates, outflow, factor, boosts, flow_back, words, face_rows,
    dir_v, feed_v, decay_v, boost_v, face_s, panel_sem, rate_sem, small_sem,
):
    rows = panel.shape[0] // CHUNKS
    blocks = decay.shape[0]
    pipes = blocks * LANES
    level = lax.axis_index("level")

    def chunk(n):
        part = pl.ds(pl.multiple_of(n * rows, rows), rows)
        return pltpu.make_async_copy(panel.at[part], cells.at[part], panel_sem.at[n])

    small = [
        pltpu.make_async_copy(src, dst, small_sem.at[n])
        for n, (src, dst) in enumerate(
            ((dirs, dir_v), (feed, feed_v), (decay, decay_v), (boost, boost_v), (faces, face_s))
        )
    ]
    rate_copy = pltpu.make_async_copy(rate, rates, rate_sem)
    for copy in small:
        copy.start()

    @pl.when(level == 0)
    def _():
        rate_copy.start()

    for n in range(CHUNKS):
        chunk(n).start(priority=1)
    for copy in small:
        copy.wait()

    scale = jnp.where(level == 0, jnp.float32(-0.25), jnp.float32(-1.0))
    fac = jnp.exp(decay_v[...] * scale)
    for b in range(blocks):
        own = slice(b * LANES, (b + 1) * LANES)
        factor[own, :] = down_rows(fac[b : b + 1])
        boosts[own, :] = down_rows(boost_v[b : b + 1])
    outflow[GROUPS * pipes :, :] = jnp.zeros_like(outflow[GROUPS * pipes :, :])
    back = (dir_v[...] == 1).astype(jnp.int32)
    lane = lax.broadcasted_iota(jnp.int32, (1, LANES), 1)
    for b in range(blocks):
        ahead = feed_v[2 * b : 2 * b + 1, :]
        behind = feed_v[2 * b + 1 : 2 * b + 2, :]
        rev = back[b : b + 1, :]
        src = jnp.where(rev == 1, behind, ahead)
        p = lane + b * LANES
        fine = src + (p << 10) + (rev << 20) + jnp.where(src >= pipes, MARK, 0)
        revs = [back[g * blocks + b : g * blocks + b + 1, :] for g in range(GROUPS)]
        most = jnp.maximum(jnp.maximum(revs[0], revs[1]), jnp.maximum(revs[2], revs[3]))
        least = jnp.minimum(jnp.minimum(revs[0], revs[1]), jnp.minimum(revs[2], revs[3]))
        fed = jnp.maximum(ahead * (1 - least), behind * most) >= pipes
        coarse = ahead + (behind << 10) + (p << 20) + jnp.where(fed, MARK, 0)
        words[b : b + 1, :] = jnp.where(level == 0, fine, coarse)
    backf = back.astype(jnp.float32)

    def back_rows(g):
        for b in range(blocks):
            at = g * blocks + b
            flow_back[at * LANES : (at + 1) * LANES, :] = down_rows(backf[at : at + 1])

    back_rows(0)

    @pl.when(level == 1)
    def _():
        for g in range(1, GROUPS):
            back_rows(g)

    per_chunk = pipes // 8 // CHUNKS

    @pl.when(level == 0)
    def _():
        rate_copy.wait()

        @pl.loop(0, CHUNKS)
        def _(n):
            chunk(n).wait()
            for i in range(per_chunk):
                q = n * per_chunk + i
                base = pl.multiple_of(q * 128, 128)
                own = pl.ds(pl.multiple_of(q * 8, 8), 8)
                rev = flow_back[own, :] != 0.0
                b = factor[own, :] * rates[pl.ds(pl.multiple_of(q * 32, 32), 8, stride=4), :]
                a = factor[own, :] - b
                y = [
                    jnp.where(
                        rev,
                        cells[pl.ds(base + j, 8, stride=16), :],
                        cells[pl.ds(base + 15 - j, 8, stride=16), :],
                    )
                    for j in range(GROUPS)
                ]
                for s in range(GROUPS):
                    outflow[pl.ds(pl.multiple_of(q * 32, 32) + s, 8, stride=4), :] = y[0]
                    y = [a * y[j] + b * y[j + 1] for j in range(len(y) - 1)]

    @pl.when(level == 1)
    def _():
        @pl.loop(0, CHUNKS)
        def _(n):
            chunk(n).wait()
            for i in range(per_chunk):
                q = n * per_chunk + i
                base = pl.multiple_of(q * 128, 128)
                for g in range(GROUPS):
                    rev = flow_back[pl.ds(pl.multiple_of(g * pipes + q * 8, 8), 8), :] != 0.0
                    outflow[pl.ds(pl.multiple_of(q * 32, 32) + g, 8, stride=4), :] = jnp.where(
                        rev,
                        cells[pl.ds(base + 4 * g, 8, stride=16), :],
                        cells[pl.ds(base + 4 * g + 3, 8, stride=16), :],
                    )

    @pl.loop(0, faces.shape[0] // 16)
    def _(m):
        moved = [
            outflow[pl.ds(pl.multiple_of(face_s[m * 16 + u] * 4, 4), 4), :] for u in range(16)
        ]
        for u in range(16):
            face_rows[pl.ds(pl.multiple_of(m * 64, 64) + 4 * u, 4), :] = moved[u]


def eight_words(q, words):
    per = LANES // 8
    return [words[q // per, (q % per) * 8 + u] for u in range(8)]


def gather_eight(fine, q, words, outflow, ahead_in, behind_in):
    start = pl.multiple_of(q * 32, 32)
    entries = eight_words(q, words)
    moved = [[outflow[pl.ds(pl.multiple_of((w & 1023) * 4, 4), 4), :] for w in entries]]
    if not fine:
        moved.append(
            [outflow[pl.ds(pl.multiple_of((w >> 10 & 1023) * 4, 4), 4), :] for w in entries]
        )
    for dest, tiles in zip((ahead_in, behind_in), moved):
        for u in range(8):
            dest[pl.ds(start + 4 * u, 4), :] = tiles[u]


def list_eight(fine, q, words, ghosts, counts):
    count, turned = counts
    second = ghosts.shape[0] // 2
    for w in eight_words(q, words):
        fed = lax.shift_right_logical(w, 31)
        ghosts[count] = w
        count = count + fed
        if fine:
            ghosts[second + turned] = w
            turned = turned + (fed & (w >> 20))
    return count, turned


def fine_block(q, cells, rates, factor, boosts, flow_back, ahead_in, new, shares):
    kept, kept_mid, sent_mid, sent = shares
    own = pl.ds(pl.multiple_of(q * 8, 8), 8)
    base = pl.multiple_of(q * 128, 128)
    quad = pl.multiple_of(q * 32, 32)
    rev = flow_back[own, :] != 0.0
    f = factor[own, :]
    b = f * rates[pl.ds(quad, 8, stride=4), :]
    a = f - b
    bo = boosts[own, :]
    x = [cells[pl.ds(base + k, 8, stride=16), :] for k in range(SEGF)]
    o = [jnp.where(rev, x[SEGF - 1 - k], x[k]) for k in range(SEGF)]
    for s in range(GROUPS):
        inflow = ahead_in[pl.ds(quad + s, 8, stride=4), :] + bo
        o = [a * o[k] + b * (o[k - 1] if k else inflow) for k in range(SEGF)]
    y = [jnp.where(rev, o[SEGF - 1 - k], o[k]) for k in range(SEGF)]
    for k in range(SEGF):
        new[pl.ds(base + k, 8, stride=16), :] = y[k]
    for k, dest in enumerate((kept, kept_mid, sent_mid, sent)):
        dest[own, :] = ((y[4 * k] + y[4 * k + 1]) + (y[4 * k + 2] + y[4 * k + 3])) * 0.25


def coarse_block(
    q, cells, rates, factor, boosts, flow_back, ahead_in, behind_in, new, shares
):
    kept, kept_mid, sent_mid, sent = shares
    pipes = factor.shape[0]
    own = pl.ds(pl.multiple_of(q * 8, 8), 8)
    base = pl.multiple_of(q * 128, 128)
    quad = pl.multiple_of(q * 32, 32)
    f = factor[own, :]
    bo = boosts[own, :]
    for g in range(GROUPS):
        rev = flow_back[pl.ds(pl.multiple_of(g * pipes + q * 8, 8), 8), :] != 0.0
        four = pl.ds(quad + g, 8, stride=4)
        b = f * rates[four, :]
        a = f - b
        inflow = jnp.where(rev, behind_in[four, :], ahead_in[four, :]) + bo
        x = [cells[pl.ds(base + 4 * g + k, 8, stride=16), :] for k in range(SEGC)]
        up = [
            jnp.where(
                rev, x[k + 1] if k + 1 < SEGC else inflow, x[k - 1] if k else inflow
            )
            for k in range(SEGC)
        ]
        y = [a * x[k] + b * up[k] for k in range(SEGC)]
        for k in range(SEGC):
            new[pl.ds(base + 4 * g + k, 8, stride=16), :] = y[k]
            if g == 0:
                (sent, sent_mid, kept_mid, kept)[k][own, :] = y[k]


def step_kernel(
    words, rate, cells, rates_in, outflow, factor, boosts, flow_back,
    new, out, kept, kept_mid, sent_mid, sent, ghosts, rates,
    ahead_in, behind_in, sems, rate_sems,
):
    shares = (kept, kept_mid, sent_mid, sent)
    level = lax.axis_index("level")
    eights = factor.shape[0] // 8
    parts = sems.shape[0]
    rows = new.shape[0] // parts

    def written(n):
        part = pl.ds(pl.multiple_of(n * rows, rows), rows)
        return pltpu.make_async_copy(new.at[part], out.at[part], sems.at[n])

    rate_rows = rates.shape[0] // parts

    def fetched(n):
        part = pl.ds(pl.multiple_of(n * rate_rows, rate_rows), rate_rows)
        return pltpu.make_async_copy(rate.at[part], rates.at[part], rate_sems.at[n])

    def run(fine):
        if not fine:
            for n in range(parts):
                fetched(n).start()
        gather_eight(fine, 0, words, outflow, ahead_in, behind_in)

        def some(q, count):
            if fine:
                fine_block(q, cells, rates, factor, boosts, flow_back, ahead_in, new, shares)
            else:
                coarse_block(
                    q, cells, rates, factor, boosts, flow_back, ahead_in, behind_in,
                    new, shares,
                )
            later = jnp.minimum(q + 1, eights - 1)
            gather_eight(fine, later, words, outflow, ahead_in, behind_in)
            return list_eight(fine, q, words, ghosts, count)

        per = eights // parts

        def part(n, count):
            if not fine:
                fetched(n).wait()
            count = lax.fori_loop(n * per, (n + 1) * per, some, count)
            @pl.when(n < parts - 1)
            def _():
                written(n).start()

            return count

        count, turned = lax.fori_loop(0, parts, part, (jnp.int32(0), jnp.int32(0)))
        ghosts[8 * eights] = count
        ghosts[16 * eights + 8] = turned

    @pl.when(level == 0)
    def _():
        run(True)

    @pl.when(level == 1)
    def _():
        run(False)

    for n in range(parts - 1):
        written(n).wait()


def arrive_kernel(first, near, arrived, outflow_in, outflow):
    odd = lax.axis_index("dom") % 2
    half = arrived.shape[0]
    slot = 1 - odd if near else odd
    start = pl.multiple_of(first + slot * half, 8)
    outflow[pl.ds(start, half), :] = arrived[...]


def over_list(count, ghosts, width, each, first=0):
    whole = count // width

    @pl.loop(0, whole)
    def _(m):
        each([ghosts[first + m * width + u] for u in range(width)])

    @pl.loop(whole * width, count)
    def _(i):
        each([ghosts[first + i]])


def send_kernel(
    first, ghosts, arrived, rates, factor, flow_back,
    outflow_in, sent_in, new_in, kept_in, outflow, sent, new, kept,
):
    pipes = factor.shape[0]
    level = lax.axis_index("level")
    arrive_kernel(first, False, arrived, outflow_in, outflow)

    def fine(entries):
        done = []
        for w in entries:
            src, p = w & 1023, w >> 10 & 1023
            own = pl.ds(p, 1)
            rows = outflow[pl.ds(pl.multiple_of(src * 4, 4), 4), :]
            f, r = factor[own, :], rates[pl.ds(p * 4, 1), :]
            total = rows[0:1]
            for s in range(1, GROUPS):
                total = f * total + rows[s : s + 1]
            done.append((own, sent[own, :] + f * r * total * 0.25))
        for own, row in done:
            sent[own, :] = row

    def coarse(entries):
        coarse_fix(entries, rates, factor, flow_back, outflow, new, kept, sent)

    @pl.when(level == 0)
    def _():
        over_list(ghosts[2 * pipes + 8], ghosts, 4, fine, pipes + 8)

    @pl.when(level == 1)
    def _():
        over_list(ghosts[pipes], ghosts, 4, coarse)


def fine_fix(entries, rates, factor, outflow, new, kept):
    row = lax.broadcasted_iota(jnp.int32, (8, LANES), 0)
    loaded = []
    for w in entries:
        src, p, rev = w & 1023, w >> 10 & 1023, w >> 20 & 1
        near = pl.ds(pl.multiple_of(p * 16 + 8 * rev, 8), 8)
        own = pl.ds(p, 1)
        inflow = [spread(outflow, src * 4 + s) for s in range(GROUPS)]
        loaded.append((
            rev, near, own, spread(factor, p), spread(rates, p * 4), inflow,
            new[near, :], kept[own, :],
        ))
    done = []
    for rev, near, own, f, r, inflow, tile, kept_row in loaded:
        b = f * r
        a = f - b
        edge = row == 7 * rev
        shift = 1 + 6 * rev
        total = b * inflow[0]
        delta = jnp.where(edge, total, 0.0)
        for s in range(1, GROUPS):
            up = jnp.where(edge, inflow[s], pltpu.roll(delta, shift, 0))
            delta = a * delta + b * up
            total = f * total + b * inflow[s]
        ahead = jnp.where(rev == 1, jnp.float32(0.0), jnp.float32(0.25))
        done.append((near, own, tile + delta, kept_row + total[0:1] * ahead))
    for near, own, tile, kept_row in done:
        new[near, :] = tile
        kept[own, :] = kept_row


def coarse_fix(entries, rates, factor, flow_back, outflow, new, kept, sent):
    pipes = factor.shape[0]
    zeros = outflow.shape[0] - 8
    loaded = []
    for w in entries:
        p = w >> 20 & 1023
        rows = []
        for src in (w & 1023, w >> 10 & 1023):
            at = jnp.where(src >= pipes, src * 4, zeros)
            rows.append(outflow[pl.ds(pl.multiple_of(at, 4), 4), :])
        low = pl.ds(p * 16, 4, stride=4)
        high = pl.ds(p * 16 + 3, 4, stride=4)
        loaded.append((
            p, low, high, rows, flow_back[pl.ds(p, 4, stride=pipes), :],
            rates[pl.ds(pl.multiple_of(p * 4, 4), 4), :], jnp.broadcast_to(factor[pl.ds(p, 1), :], (4, LANES)),
            new[low, :], new[high, :],
        ))
    done = []
    for p, low, high, rows, rev, r, f, first_rows, last_rows in loaded:
        turned = rev != 0.0
        delta = f * r * jnp.where(turned, rows[1], rows[0])
        done.append((
            p, low, high,
            first_rows + jnp.where(turned, 0.0, delta), last_rows + jnp.where(turned, delta, 0.0),
        ))
    for p, low, high, first_rows, last_rows in done:
        new[low, :] = first_rows
        new[high, :] = last_rows
        kept[pl.ds(p, 1), :] = last_rows[0:1]
        sent[pl.ds(p, 1), :] = first_rows[0:1]


def fix_kernel(
    ghosts, rates, factor, outflow, kept_mid, partner_mid, new_in, kept_in, out_in,
    new, kept, out, gap_rows, sem, tail_sem,
):
    pipes = factor.shape[0]
    level = lax.axis_index("level")
    shift = jnp.where(level == 0, 10, 20)
    count = ghosts[pipes]

    def write(entries):
        for w in entries:
            p = lax.shift_right_logical(w, shift) & 1023
            part = pl.ds(pl.multiple_of(p * SEGF, SEGF), SEGF)
            pltpu.make_async_copy(new.at[part], out.at[part], sem).start()

    def fine(entries):
        fine_fix(entries, rates, factor, outflow, new, kept)
        write(entries)

    @pl.when(level == 0)
    def _():
        over_list(count, ghosts, 4, fine)

    @pl.when(level == 1)
    def _():
        over_list(count, ghosts, 8, write)

    tail = pl.ds(pipes * SEGF // 8 * 7, pipes * SEGF // 8)
    last = pltpu.make_async_copy(new.at[tail], out.at[tail], tail_sem)
    last.start()
    sign = jnp.where(level == 0, jnp.float32(1.0), jnp.float32(-1.0))

    @pl.loop(0, pipes // 64)
    def _(m):
        for u in range(8):
            own = pl.ds(pl.multiple_of(m * 64 + 8 * u, 8), 8)
            spots = pl.ds(pl.multiple_of(m * 128, 128) + 16 * u + 1 - level, 8, stride=2)
            gap_rows[spots, :] = (kept_mid[own, :] - partner_mid[own, :]) * sign

    def wait(some):
        part = pl.ds(0, SEGF * some)
        pltpu.make_async_copy(new.at[part], out.at[part], sem).wait()

    whole = count // 8

    @pl.loop(0, whole)
    def _(m):
        wait(8)

    @pl.loop(whole * 8, count)
    def _(i):
        wait(1)

    last.wait()


def gap_kernel(kept, partner, rows_in, rows, gap, sems):
    level = lax.axis_index("level")
    sign = jnp.where(level == 0, jnp.float32(1.0), jnp.float32(-1.0))
    parts = sems.shape[0]
    copies = []
    per = kept.shape[0] // 8 // parts
    for n in range(parts):
        @pl.loop(0, per // 8)
        def _(m):
            for u in range(8):
                at = pl.multiple_of(n * per * 8 + m * 64 + 8 * u, 8)
                own = pl.ds(at, 8)
                spots = pl.ds(pl.multiple_of(2 * at, 16) + level, 8, stride=2)
                rows[spots, :] = (kept[own, :] - partner[own, :]) * sign

        part = pl.ds(n * per * 16, per * 16)
        copies.append(pltpu.make_async_copy(rows.at[part], gap.at[part], sems.at[n]))
        copies[-1].start()
    for copy in copies:
        copy.wait()


def per_device(panels, courant, direction, decay, booster, feeder, face_index):
    pipes = panels.shape[1]
    columns = panels.shape[3]
    faces = face_index.shape[0]
    blocks = pipes // LANES
    domains = lax.axis_size("dom")
    f32, i32 = jnp.float32, jnp.int32
    cells_in = panels.reshape(pipes * SEGF, columns)
    rates_in = courant.reshape(pipes * GROUPS, columns)
    dirs = direction.transpose(1, 2, 0).reshape(GROUPS * blocks, LANES)
    feed = feeder.reshape(blocks, LANES, 2).transpose(0, 2, 1).reshape(2 * blocks, LANES)
    ghost_rows = GROUPS * (pipes + 2 * faces) + 8

    cells_in, rates_in, dirs, feed, decay, booster, face_index = pinned(
        pltpu.HBM, cells_in, rates_in, dirs, feed,
        decay.reshape(blocks, LANES), booster.reshape(blocks, LANES), face_index,
    )
    cells, rates, outflow, factor, boosts, flow_back, words, face_rows = pl.pallas_call(
        load_kernel,
        name="load_step",
        in_specs=[HBM] * 7,
        out_specs=[VMEM] * 8,
        out_shape=[
            pltpu.VMEM((pipes * SEGF, columns), f32),
            pltpu.VMEM((pipes * GROUPS, columns), f32),
            pltpu.VMEM((ghost_rows, columns), f32),
            pltpu.VMEM((pipes, columns), f32),
            pltpu.VMEM((pipes, columns), f32),
            pltpu.VMEM((GROUPS * pipes, columns), f32),
            jax.ShapeDtypeStruct((blocks, LANES), i32),
            pltpu.VMEM((faces * GROUPS, columns), f32),
        ],
        scratch_shapes=[
            pltpu.VMEM(dirs.shape, i32),
            pltpu.VMEM(feed.shape, i32),
            pltpu.VMEM((blocks, LANES), f32),
            pltpu.VMEM((blocks, LANES), f32),
            pltpu.SMEM((faces,), i32),
            pltpu.SemaphoreType.DMA((CHUNKS,)),
            pltpu.SemaphoreType.DMA(()),
            pltpu.SemaphoreType.DMA((5,)),
        ],
        compiler_params=params(),
        cost_estimate=cost(5 << 20),
    )(cells_in, rates_in, dirs, feed, decay, booster, face_index)

    near_pairs = [(i, i ^ 1) for i in range(domains) if i ^ 1 < domains]
    far_pairs = [(i, i + 1) for i in range(1, domains - 1, 2)]
    far_pairs = far_pairs + [(j, i) for i, j in far_pairs]
    near_rows = lax.ppermute(face_rows, "dom", near_pairs)
    far_rows = lax.ppermute(face_rows, "dom", far_pairs)

    new, out, kept, kept_mid, sent_mid, sent, ghosts, rates = pl.pallas_call(
        step_kernel,
        name="advance_step",
        in_specs=[SMEM, HBM] + [VMEM] * 6,
        out_specs=[VMEM, HBM] + [VMEM] * 4 + [SMEM, VMEM],
        out_shape=[
            pltpu.VMEM((pipes * SEGF, columns), f32),
            jax.ShapeDtypeStruct((pipes * SEGF, columns), f32),
            *[pltpu.VMEM((pipes, columns), f32)] * 4,
            pltpu.SMEM((2 * (pipes + 8),), i32),
            pltpu.VMEM((pipes * GROUPS, columns), f32),
        ],
        scratch_shapes=[pltpu.VMEM((GROUPS * pipes, columns), f32)] * 2
        + [pltpu.SemaphoreType.DMA((8,))] * 2,
        input_output_aliases={3: 7},
        compiler_params=params(),
        cost_estimate=cost(20 << 20),
    )(words, rates_in, cells, rates, outflow, factor, boosts, flow_back)

    swap = [(0, 1), (1, 0)]
    partner_mid = lax.ppermute(sent_mid, "level", swap)
    first = GROUPS * pipes
    outflow = pl.pallas_call(
        lambda *refs: arrive_kernel(first, True, *refs),
        name="near_arrive",
        in_specs=[VMEM] * 2,
        out_specs=VMEM,
        out_shape=pltpu.VMEM((ghost_rows, columns), f32),
        input_output_aliases={1: 0},
        compiler_params=params(),
        cost_estimate=cost(1 << 19),
    )(near_rows, outflow)

    outflow, sent, new, kept = pl.pallas_call(
        lambda *refs: send_kernel(first, *refs),
        name="ghost_send",
        in_specs=[SMEM] + [VMEM] * 8,
        out_specs=[VMEM] * 4,
        out_shape=[
            pltpu.VMEM((ghost_rows, columns), f32),
            pltpu.VMEM((pipes, columns), f32),
            pltpu.VMEM((pipes * SEGF, columns), f32),
            pltpu.VMEM((pipes, columns), f32),
        ],
        input_output_aliases={5: 0, 6: 1, 7: 2, 8: 3},
        compiler_params=params(),
        cost_estimate=cost(1 << 20),
    )(ghosts, far_rows, rates, factor, flow_back, outflow, sent, new, kept)

    partner = lax.ppermute(sent, "level", swap)

    new, kept, out, gap_rows = pl.pallas_call(
        fix_kernel,
        name="ghost_fix",
        in_specs=[SMEM] + [VMEM] * 7 + [HBM],
        out_specs=[VMEM, VMEM, HBM, VMEM],
        out_shape=[
            pltpu.VMEM((pipes * SEGF, columns), f32),
            pltpu.VMEM((pipes, columns), f32),
            jax.ShapeDtypeStruct((pipes * SEGF, columns), f32),
            pltpu.VMEM((pipes * 2, columns), f32),
        ],
        scratch_shapes=[pltpu.SemaphoreType.DMA(())] * 2,
        input_output_aliases={6: 0, 7: 1, 8: 2},
        compiler_params=params(),
        cost_estimate=cost(4 << 20),
    )(
        ghosts, rates, factor, outflow, kept_mid, partner_mid, new, kept,
        *pinned(pltpu.HBM, out),
    )

    _, gap = pl.pallas_call(
        gap_kernel,
        name="level_gap",
        in_specs=[VMEM] * 3,
        out_specs=[VMEM, HBM],
        out_shape=[
            pltpu.VMEM((pipes * 2, columns), f32),
            jax.ShapeDtypeStruct((pipes * 2, columns), f32),
        ],
        scratch_shapes=[pltpu.SemaphoreType.DMA((2,))],
        input_output_aliases={2: 0},
        compiler_params=params(),
        cost_estimate=cost(1 << 20),
    )(kept, partner, gap_rows)
    return (out.reshape(1, pipes, SEGF, columns), gap.reshape(pipes, 2, columns))


def solution(mesh):
    in_specs = (
        P("level", "dom", None, "samp"),
        P("dom", None, "samp"),
        P("dom", None, "samp"),
        P("dom"),
        P("dom"),
        P("dom", None),
        P("dom"),
    )
    out_specs = (P("level", "dom", None, "samp"), P("dom", "level", "samp"))
    return jax.shard_map(
        per_device, mesh=mesh, in_specs=in_specs, out_specs=out_specs, check_vma=False
    )
```
